256 devices in a mesh: flow: 8 (over z_lo, y), trans: 32 (over z_hi, x, core).
Axes of the slice: x: 4, y: 4, z: 8 (z_hi: 4, z_lo: 2; z = z_hi * 2 + z_lo), core: 2. Of those that a mesh axis runs over, the one named last changes fastest.
Arguments:
- main_pos: float32 [16, 2048, 3, 128], P('flow', 'trans')
- main_vel: float32 [16, 2048, 3, 128], P('flow', 'trans'), may hold values from -6 to 6
- main_force: float32 [16, 2048, 3, 128], P('flow', 'trans'), may hold values from -240 to 240
- main_seed: int32 [16, 2048, 128], P('flow', 'trans'), may hold values from 0 to 4095
- main_count: int32 [16, 2048], P('flow', 'trans'), may hold values from 1 to 128, as said below
- prec_pos: float32 [8, 1024, 3, 128], P('flow', 'trans')
- prec_vel: float32 [8, 1024, 3, 128], P('flow', 'trans'), may hold values from -6 to 6
- prec_force: float32 [8, 1024, 3, 128], P('flow', 'trans'), may hold values from -240 to 240
- prec_seed: int32 [8, 1024, 128], P('flow', 'trans'), may hold values from 0 to 4095
- cross_row: int32 [512], P('trans'), may hold values from 0 to 4095, as said below
- cross_dest: int32 [512], P('trans'), may hold values from 0 to 31, as said below
- cross_cell: int32 [512], P('trans'), may hold values from 0 to 63
- outlet_bin: int32 [2048, 128], P('trans'), may hold values from 0 to 63
- outlet_coef: float32 [64], replicated, may hold values from 2 to 20
Outputs:
- main_pos_out: float32 [16, 2048, 3, 128], P('flow', 'trans')
- main_vel_out: float32 [16, 2048, 3, 128], P('flow', 'trans')
- main_force_out: float32 [16, 2048, 3, 128], P('flow', 'trans')
- prec_pos_out: float32 [8, 1024, 3, 128], P('flow', 'trans')
- prec_vel_out: float32 [8, 1024, 3, 128], P('flow', 'trans')
- prec_force_out: float32 [8, 1024, 3, 128], P('flow', 'trans')
The draws below stay inside these ranges and needn't reach their ends.
Inputs may be any that keep to these rules, and one draw needn't show every extreme that they name: `main_count`: cells of main flow column 0 hold at most 64 beads, one of them exactly that many; some cell holds 128. `cross_row`: the 16 rows of one trans index name distinct slots. `cross_dest`: among the 16 rows of one trans index no destination appears more than 2 times; one destination appears exactly 2 times among the rows of every trans index.
All inputs are finite; a program needn't handle non-finite values.
Results may differ from the reference program's by a relative error of at most 0.0003.
Values sent between devices are 32-bit elements; how exact they have to be, the bound alone decides.
A program may use at most 192 MiB of HBM per device.

```python
import math
import jax
import jax.numpy as jnp
from jax import lax

CT = 64
DMOST = 2
BINS = 64
CROSS = 16
NFC = 16
NTC = 2048
NPF = 8
NPT = 1024
N_TRANS = 32


def cell_positions(key, leading):
    plane_xy = jax.random.uniform(jax.random.fold_in(key, 1), leading + (2, 128), jnp.float32)
    height = jax.random.uniform(jax.random.fold_in(key, 2), leading + (1, 128), jnp.float32, 0.0, 16.0)
    return jnp.concatenate([plane_xy, height], axis=2)


def draw_main_pos(key, part):
    return cell_positions(key, (NFC, NTC))


def draw_prec_pos(key, part):
    return cell_positions(key, (NPF, NPT))


def draw_main_count(key, part):
    across = jnp.arange(NTC, dtype=jnp.int32)
    baseline = 40 + 80 * across // NTC
    jitter = jax.random.randint(jax.random.fold_in(key, 1), (NFC, NTC), -8, 9)
    counts = jnp.clip(baseline[None, :] + jitter, 1, 128)
    inlet_cap = 128 - N_TRANS * DMOST
    inlet_pick = jax.random.randint(jax.random.fold_in(key, 2), (), 0, NTC)
    inlet_row = jnp.where(across == inlet_pick, inlet_cap, jnp.minimum(counts[0], inlet_cap))
    full_pick = jax.random.randint(jax.random.fold_in(key, 3), (), 0, NTC)
    outlet = jnp.where(across == full_pick, 128, counts[NFC - 1])
    counts = counts.at[NFC - 1].set(outlet)
    counts = counts.at[0].set(inlet_row)
    return counts.astype(jnp.int32)


def draw_cross_row(key, part):

    def per_source(source_index):
        return jax.random.permutation(jax.random.fold_in(key, source_index), CT // 2 * 128)[:CROSS]
    return jax.vmap(per_source)(jnp.arange(N_TRANS, dtype=jnp.int32)).reshape(-1).astype(jnp.int32)


def draw_cross_dest(key, part):
    pool_size = N_TRANS * DMOST
    dest_pool = jnp.repeat(jnp.arange(N_TRANS, dtype=jnp.int32), DMOST)
    hot_dest = jax.random.randint(jax.random.fold_in(key, 7), (), 0, N_TRANS)

    def per_source(source_index):
        sub_key = jax.random.fold_in(key, source_index + 100)
        rank_order = jax.random.permutation(jax.random.fold_in(sub_key, 1), pool_size)
        priority = jnp.where(dest_pool == hot_dest, jnp.arange(pool_size, dtype=jnp.int32) - pool_size, rank_order)
        chosen = dest_pool[jnp.argsort(priority, stable=True)[:CROSS]]
        return chosen[jax.random.permutation(jax.random.fold_in(sub_key, 2), CROSS)]
    return jax.vmap(per_source)(jnp.arange(N_TRANS, dtype=jnp.int32)).reshape(-1).astype(jnp.int32)


def draw_outlet_bin(key, part):
    regions = 8
    level = jax.random.randint(jax.random.fold_in(key, 1), (regions, BINS), 0, 7)
    weight = jnp.left_shift(jnp.ones_like(level), level)
    bounds = jnp.cumsum(weight, axis=1).astype(jnp.int32)
    region = jnp.arange(NTC, dtype=jnp.int32) * regions // NTC
    cell_bounds = bounds[region]
    ticket = jax.random.randint(jax.random.fold_in(key, 2), (NTC, 128), 0, cell_bounds[:, BINS - 1:BINS])

    def add_bin(index, acc):
        limit = lax.dynamic_slice_in_dim(cell_bounds, index, 1, 1)
        return acc + (limit <= ticket).astype(jnp.int32)
    bins = lax.fori_loop(0, BINS, add_bin, jnp.zeros((NTC, 128), jnp.int32))
    every_bin = jax.random.permutation(jax.random.fold_in(key, 3), BINS).astype(jnp.int32)
    bins = bins.at[0, 0:BINS].set(every_bin)
    return bins.astype(jnp.int32)


def touch_ends(array, rng, low, high):
    dims = array.shape
    spot = [jax.random.randint(jax.random.fold_in(rng, axis), (), 0, dims[axis]) for axis in range(len(dims))]
    array = array.at[tuple(spot)].set(low)
    longest = dims.index(max(dims))
    spot[longest] = (spot[longest] + 1) % dims[longest]
    return array.at[tuple(spot)].set(high)


def shard_levels(stream_key, extent, pieces, low, high):
    factor_of, own = 1.0, jax.random.fold_in(stream_key, 6)
    for dim, blocks in pieces:
        heights = jnp.exp(jax.random.uniform(jax.random.fold_in(own, dim), (blocks,), jnp.float32, low / len(pieces), high / len(pieces)))
        factor_of = factor_of * jnp.repeat(heights, extent[dim] // blocks).reshape([-1 if axis == dim else 1 for axis in range(len(extent))])
    return factor_of


def scatter_about(own_key, dims, scale, bound, pieces=(), held_as=jnp.bfloat16):
    result = scale * jax.random.normal(own_key, dims, jnp.float32)
    if pieces:
        result = result * shard_levels(own_key, dims, pieces, -0.22, 0.18)
    return jnp.clip(result, -bound, bound).astype(held_as)


def setup_inputs(seed: int = 0) -> dict:
    arg_keys = jax.random.split(jax.random.key(seed), 15)
    return {
        "main_pos": draw_main_pos(jax.random.fold_in(arg_keys[14], 71), 0),
        "main_vel": scatter_about(arg_keys[1], (NFC, NTC, 3, 128), 1.0, 6.0, ((0, 8), (1, 32)), jnp.float32),
        "main_force": scatter_about(arg_keys[2], (NFC, NTC, 3, 128), 40.0, 240.0, ((0, 8), (1, 32)), jnp.float32),
        "main_seed": touch_ends(jax.random.randint(arg_keys[3], (NFC, NTC, 128), 0, 4096), jax.random.fold_in(arg_keys[3], 1), 0, 4095).astype(jnp.int32),
        "main_count": draw_main_count(jax.random.fold_in(arg_keys[14], 71), 0),
        "prec_pos": draw_prec_pos(jax.random.fold_in(arg_keys[14], 71), 0),
        "prec_vel": scatter_about(arg_keys[6], (NPF, NPT, 3, 128), 1.0, 6.0, ((0, 8), (1, 32)), jnp.float32),
        "prec_force": scatter_about(arg_keys[7], (NPF, NPT, 3, 128), 40.0, 240.0, ((0, 8), (1, 32)), jnp.float32),
        "prec_seed": touch_ends(jax.random.randint(arg_keys[8], (NPF, NPT, 128), 0, 4096), jax.random.fold_in(arg_keys[8], 1), 0, 4095).astype(jnp.int32),
        "cross_row": draw_cross_row(jax.random.fold_in(arg_keys[14], 71), 0),
        "cross_dest": draw_cross_dest(jax.random.fold_in(arg_keys[14], 71), 0),
        "cross_cell": touch_ends(jax.random.randint(arg_keys[11], (N_TRANS * CROSS,), 0, CT), jax.random.fold_in(arg_keys[11], 1), 0, CT - 1).astype(jnp.int32),
        "outlet_bin": draw_outlet_bin(jax.random.fold_in(arg_keys[14], 71), 0),
        "outlet_coef": jnp.clip(jnp.exp(jax.random.uniform(arg_keys[13], (BINS,), jnp.float32, math.log(2.0), math.log(20.0))), 2.0, 20.0),
    }


time_step = 0.01
repulsion = 25.0
friction = 4.5
noise_amp = 30.0
box_height = 16.0
seed_modulus = 4093
unit_spread = 3.4641016151377544

def tile_forces(center, padded):
    count_cells = center.shape[0]
    tile_slots = center.shape[2]
    pos_i = center[:, 0:3, :, None]
    vel_i = center[:, 3:6, :, None]
    code_i = center[:, 6, :, None]
    seed_i = (code_i - 1.0).astype(jnp.int32)
    summed = jnp.zeros((count_cells, 3, tile_slots), jnp.float32)
    for step_flow in (-1, 0, 1):
        for step_trans in (-1, 0, 1):
            others = lax.slice_in_dim(padded[1 + step_flow], 1 + step_trans, 1 + step_trans + count_cells, axis=0)
            pos_j = others[:, 0:3, None, :]
            vel_j = others[:, 3:6, None, :]
            code_j = others[:, 6, None, :]
            seed_j = (code_j - 1.0).astype(jnp.int32)
            delta_x = pos_i[:, 0] - (pos_j[:, 0] + float(step_flow))
            delta_y = pos_i[:, 1] - (pos_j[:, 1] + float(step_trans))
            delta_z = pos_i[:, 2] - pos_j[:, 2]
            delta_z = delta_z - box_height * jnp.floor(delta_z / box_height + 0.5)
            pair_mask = (code_i > 0.5) & (code_j > 0.5)
            if step_flow == 0 and step_trans == 0:
                pair_mask = pair_mask & jnp.logical_not(jnp.eye(tile_slots, dtype=bool))
            dist_sq = jnp.where(pair_mask, delta_x * delta_x + delta_y * delta_y + delta_z * delta_z, 1.0)
            inverse = lax.rsqrt(dist_sq)
            weight = jnp.where(pair_mask, jnp.maximum(1.0 - dist_sq * inverse, 0.0), 0.0)
            along = ((vel_i[:, 0] - vel_j[:, 0]) * delta_x + (vel_i[:, 1] - vel_j[:, 1]) * delta_y + (vel_i[:, 2] - vel_j[:, 2]) * delta_z) * inverse
            hashed = (seed_i * seed_j + seed_i + seed_j) % seed_modulus
            noise_term = (hashed.astype(jnp.float32) / seed_modulus - 0.5) * unit_spread
            scalar = (repulsion * weight - friction * weight * weight * along + noise_amp * weight * noise_term) * inverse
            summed = summed + jnp.stack([lax.optimization_barrier(jnp.sum(scalar * delta_x, axis=2)), lax.optimization_barrier(jnp.sum(scalar * delta_y, axis=2)), lax.optimization_barrier(jnp.sum(scalar * delta_z, axis=2))], axis=1)
    return summed

def drift_state(position, velocity, force):
    half_vel = velocity + 0.5 * time_step * force
    return (position + time_step * half_vel, half_vel)

def all_forces(bead_state, padded, block_width):
    flow_rows = bead_state.shape[0]
    trans_blocks = bead_state.shape[1] // block_width
    tile_slots = bead_state.shape[3]
    zero_index = jnp.zeros((), jnp.int32)

    def one_block(block_index):
        flow_at = (block_index // trans_blocks).astype(jnp.int32)
        trans_at = (block_index % trans_blocks * block_width).astype(jnp.int32)
        center = lax.dynamic_slice(bead_state, (flow_at, trans_at, zero_index, zero_index), (1, block_width, 7, tile_slots))[0]
        window = lax.dynamic_slice(padded, (flow_at, trans_at, zero_index, zero_index), (3, block_width + 2, 7, tile_slots))
        return tile_forces(center, window)
    forces = lax.map(one_block, jnp.arange(flow_rows * trans_blocks, dtype=jnp.int32))
    return forces.reshape(flow_rows, trans_blocks * block_width, 3, tile_slots)

def reference(main_pos, main_vel, main_force, main_seed, main_count, prec_pos, prec_vel, prec_force, prec_seed, cross_row, cross_dest, cross_cell, outlet_bin, outlet_coef):
    tile_slots = main_pos.shape[3]
    half_cells = CT // 2
    sources = jnp.arange(N_TRANS * CROSS, dtype=jnp.int32) // CROSS
    src_cell = sources * half_cells + cross_row // tile_slots
    src_slot = cross_row % tile_slots
    moved_pos = prec_pos[0, src_cell, :, src_slot]
    moved_vel = prec_vel[0, src_cell, :, src_slot]
    moved_force = prec_force[0, src_cell, :, src_slot]
    moved_seed = prec_seed[0, src_cell, src_slot]
    dest_cell = cross_dest * CT + cross_cell
    cell_hot = (dest_cell[:, None] == jnp.arange(NTC, dtype=jnp.int32)[None, :]).astype(jnp.int32)
    earlier = lax.optimization_barrier(jnp.sum((jnp.cumsum(cell_hot, axis=0) - cell_hot) * cell_hot, axis=1))
    arrivals = lax.optimization_barrier(jnp.sum(cell_hot, axis=0))
    target_slot = main_count[0, dest_cell] + earlier
    main_pos = main_pos.at[0, dest_cell, :, target_slot].set(moved_pos)
    main_vel = main_vel.at[0, dest_cell, :, target_slot].set(moved_vel)
    main_force = main_force.at[0, dest_cell, :, target_slot].set(moved_force)
    main_seed = main_seed.at[0, dest_cell, target_slot].set(moved_seed)
    new_count = main_count.at[0].add(arrivals)
    occupied = jnp.arange(tile_slots, dtype=jnp.int32)[None, None, :] < new_count[:, :, None]
    main_moved, main_half = drift_state(main_pos, main_vel, main_force)
    prec_moved, prec_half = drift_state(prec_pos, prec_vel, prec_force)
    main_code = jnp.where(occupied, main_seed + 1, 0).astype(jnp.float32)[:, :, None, :]
    prec_code = (prec_seed + 1).astype(jnp.float32)[:, :, None, :]
    main_state = jnp.concatenate([main_moved, main_half, main_code], axis=2)
    prec_state = jnp.concatenate([prec_moved, prec_half, prec_code], axis=2)
    main_padded = jnp.pad(main_state, ((1, 1), (1, 1), (0, 0), (0, 0)))
    prec_padded = jnp.pad(prec_state, ((1, 1), (1, 1), (0, 0), (0, 0)), mode='wrap')
    main_forces = all_forces(main_state, main_padded, CT)
    prec_forces = all_forces(prec_state, prec_padded, half_cells)
    last_column = occupied[NFC - 1].astype(jnp.float32)
    profile = jax.ops.segment_sum(last_column.reshape(-1), outlet_bin.reshape(-1), BINS)
    density = profile * BINS / (NTC * tile_slots)
    outlet_push = outlet_coef * density
    main_forces = main_forces.at[NFC - 1, :, 0, :].add(-outlet_push[outlet_bin] * last_column)
    main_vel_out = main_half + 0.5 * time_step * main_forces
    prec_vel_out = prec_half + 0.5 * time_step * prec_forces
    slot_mask = occupied[:, :, None, :]
    return (jnp.where(slot_mask, main_moved, 0.0), jnp.where(slot_mask, main_vel_out, 0.0), jnp.where(slot_mask, main_forces, 0.0), prec_moved, prec_vel_out, prec_forces)
```

```python
import jax
import jax.numpy as jnp
from jax import lax
from jax.experimental import pallas as pl
from jax.experimental.pallas import tpu as pltpu
from jax.sharding import PartitionSpec as P

BINS = 64
LANES = 128
SHARE = 4
CLASSES = LANES // SHARE

time_step = 0.01
repulsion = 25.0
friction = 4.5
noise_amp = 30.0
box_height = 16.0
seed_modulus = 4093
unit_spread = 3.4641016151377544

reach = 1.0005
nowhere = 1000.0
table_rate = 8.0
hash_shift = 2047.0 / 4093.0
noise_slope = noise_amp * unit_spread
noise_base = repulsion - noise_slope * 0.5 / 4093.0

VMEM = pltpu.VMEM
SMEM = pltpu.SMEM


def take(rows, lanes):
    return jnp.take_along_axis(rows, lanes, axis=1, mode="promise_in_bounds")


def lane_iota(rows):
    return lax.broadcasted_iota(jnp.int32, (rows, LANES), 1)


def centred(seed):
    code = seed + 1
    code = jnp.where(code > 2046, code - seed_modulus, code)
    return jnp.where(code > 2046, code - seed_modulus, code)


def start_kernel(row_ref, dest_ref, cell_ref, count_ref, pos_ref, vel_ref, force_ref, seed_ref,
                 bin_ref, out_ref, profile_ref):
    rows = row_ref.shape[0]
    lane3 = lane_iota(3)
    lane1 = lane_iota(1)
    parts = [jnp.zeros((3, LANES), jnp.float32) for _ in range(3)]
    tail = [jnp.zeros((1, LANES), jnp.float32) for _ in range(3)]
    for q in range(rows):
        cell = row_ref[q] // LANES
        slot = row_ref[q] % LANES
        hit = lane3 == slot
        for a, ref in enumerate((pos_ref, vel_ref, force_ref)):
            value = jnp.sum(jnp.where(hit, ref[0, cell], 0.0), axis=1, keepdims=True)
            parts[a] = jnp.where(lane3 == q, value, parts[a])
        seed = jnp.where(lane1 == slot, seed_ref[0, pl.ds(cell, 1), :].astype(jnp.float32), 0.0)
        seed = jnp.sum(seed, axis=1, keepdims=True)
        here = lane1 == q
        tail[0] = jnp.where(here, seed, tail[0])
        tail[1] = jnp.where(here, dest_ref[q].astype(jnp.float32), tail[1])
        tail[2] = jnp.where(here, cell_ref[q].astype(jnp.float32), tail[2])
    for a in range(3):
        out_ref[3 * a : 3 * a + 3, :] = parts[a][:, 0:rows]
        out_ref[9 + a : 10 + a, :] = tail[a][:, 0:rows]
    last = count_ref.shape[0] // 2
    bins = jnp.where(lane_iota(last) < count_ref[last:, :], bin_ref[...], BINS)
    lane = lane_iota(1)
    profile = jnp.zeros((1, LANES), jnp.float32)
    for b in range(BINS):
        hits = jnp.sum((bins == b).astype(jnp.float32), axis=0, keepdims=True)
        profile = jnp.where(lane == b, jnp.sum(hits, axis=1, keepdims=True), profile)
    profile_ref[...] = profile


def sorted_by(key, rows):
    lane = lane_iota(rows)
    load = lane
    size = 2
    while size <= LANES:
        dist = size // 2
        while dist >= 1:
            partner = lane ^ dist
            low = ((lane & size) == 0) == ((lane & dist) == 0)
            sign = jnp.where(low, 1.0, -1.0)
            other_key = take(key, partner)
            other_load = take(load, partner)
            swap = (other_key - key) * sign < 0.0
            key = jnp.where(swap, other_key, key)
            load = jnp.where(swap, other_load, load)
            dist //= 2
        size *= 2
    return key, load


def first_at_least(sorted_rows, bound, rows):
    at = jnp.zeros((rows, LANES), jnp.int32)
    step = LANES // 2
    while step >= 1:
        below = take(sorted_rows, at + (step - 1)) < bound
        at = jnp.where(below, at + step, at)
        step //= 2
    return jnp.where(take(sorted_rows, at) < bound, at + 1, at)


def prep_kernel(dest_ref, cell_ref, pay_ref, me_ref, count0_ref, count_ref,
                mpos_ref, mvel_ref, mforce_ref, mseed_ref,
                ppos_ref, pvel_ref, pforce_ref, pseed_ref,
                msort_ref, psort_ref, mraw_ref, praw_ref, mrank_ref, prank_ref,
                raw_ref, filled_ref):
    flow_rows, cells = mseed_ref.shape[0], mseed_ref.shape[1]
    sources = pay_ref.shape[0] // 256
    per = dest_ref.shape[0] // sources
    for f in range(flow_rows):
        for c in range(3):
            raw_ref[c, f * cells : (f + 1) * cells, :] = mpos_ref[f, :, c, :]
            raw_ref[3 + c, f * cells : (f + 1) * cells, :] = mvel_ref[f, :, c, :]
            raw_ref[6 + c, f * cells : (f + 1) * cells, :] = mforce_ref[f, :, c, :]
        seed = mseed_ref[f]
        occupied = lane_iota(cells) < count_ref[f * cells : (f + 1) * cells, :]
        raw_ref[9, f * cells : (f + 1) * cells, :] = jnp.where(occupied, seed, -1).astype(jnp.float32)

    me = me_ref[0]

    def fill(cell, carry):
        filled_ref[cell] = count0_ref[cell]
        return carry

    lax.fori_loop(0, cells, fill, 0)
    lane1 = lane_iota(1)

    def look(block, carry):
        start = block * 8
        found = dest_ref[start] == me
        for u in range(1, 8):
            found = found | (dest_ref[start + u] == me)

        @pl.when(found)
        def _():
            def one(u, inner):
                q = start + u

                @pl.when(dest_ref[q] == me)
                def _():
                    cell = cell_ref[q]
                    slot = filled_ref[cell]
                    filled_ref[cell] = slot + 1
                    origin = (q // per) * 256 + q % per
                    for c in range(10):
                        row = raw_ref[c, pl.ds(cell, 1), :]
                        raw_ref[c, pl.ds(cell, 1), :] = jnp.where(
                            lane1 == slot, pay_ref[origin + c * per], row
                        )

                return inner

            lax.fori_loop(0, 8, one, 0)

        return carry

    lax.fori_loop(0, dest_ref.shape[0] // 8, look, 0)

    def finish(state, seed, rows, sort_ref, rank_ref, raw_out, f, at):
        occupied = seed >= 0
        half = [state[3 + c] + 0.5 * time_step * state[6 + c] for c in range(3)]
        moved = [state[c] + time_step * half[c] for c in range(3)]
        for c in range(3):
            raw_out[c, at : at + rows, :] = moved[c]
            raw_out[3 + c, at : at + rows, :] = half[c]
        raw_out[6, at : at + rows, :] = seed.astype(jnp.float32)
        height = moved[2] - box_height * jnp.floor(moved[2] * (1.0 / box_height))
        key, order = sorted_by(jnp.where(occupied, height, nowhere), rows)
        _, rank = sorted_by(order.astype(jnp.float32), rows)
        rank_ref[at : at + rows, :] = rank
        hashed = centred(seed).astype(jnp.float32) / seed_modulus
        fields = [moved[0], moved[1], None] + [friction * v for v in half] + [hashed]
        for c, field in enumerate(fields):
            if field is None:
                sort_ref[c, f, :, :] = key
            else:
                sort_ref[c, f, :, :] = take(jnp.where(occupied, field, 0.0), order)
        edges = lane_iota(rows).astype(jnp.float32) * (1.0 / table_rate)
        sort_ref[7, f, :, :] = first_at_least(key, edges, rows).astype(jnp.float32)

    for f in range(flow_rows):
        at = f * cells
        state = [raw_ref[c, at : at + cells, :] for c in range(9)]
        finish(state, raw_ref[9, at : at + cells, :].astype(jnp.int32), cells,
               msort_ref, mrank_ref, mraw_ref, f, at)
    state = [ref[0, :, c, :] for ref in (ppos_ref, pvel_ref, pforce_ref) for c in range(3)]
    finish(state, pseed_ref[0], pseed_ref.shape[1], psort_ref, prank_ref, praw_ref, 0, 0)


def assemble(j_ref, sort_ref, below, above, left_ref, right_ref, shift, open_ends):
    fields, flow_rows, cells, _ = sort_ref.shape

    def keep(c, value, here):
        if open_ends is None or c != 2:
            return value
        return jnp.where(here, value, nowhere)

    for c in range(fields):
        for f in range(flow_rows):
            j_ref[c, 1 + f, 8 : 8 + cells, :] = sort_ref[c, f]
        ends = open_ends or (True,) * 4
        j_ref[c, 0, 8 : 8 + cells, :] = keep(c, below(c), ends[0])
        j_ref[c, 1 + flow_rows, 8 : 8 + cells, :] = keep(c, above(c), ends[1])
        for f in range(flow_rows + 2):
            inside_left, inside_right = ends[2], ends[3]
            if open_ends is not None and f == 0:
                inside_left, inside_right = ends[2] & ends[0], ends[3] & ends[0]
            if open_ends is not None and f == flow_rows + 1:
                inside_left, inside_right = ends[2] & ends[1], ends[3] & ends[1]
            j_ref[c, f, 7:8, :] = keep(c, left_ref[c, shift + f : shift + f + 1, :], inside_left)
            j_ref[c, f, 8 + cells : 9 + cells, :] = keep(
                c, right_ref[c, shift + f : shift + f + 1, :], inside_right
            )


def search(j_ref, f, cells, i_ref, base_ref, count_ref, held_ref, reach_ref, combo0):
    at = f * cells
    low = i_ref[2 * SHARE, at : at + cells, :]
    high = jnp.full((cells, LANES), -nowhere, jnp.float32)
    for v in range(SHARE):
        height = i_ref[2 * SHARE + v, at : at + cells, :]
        high = jnp.maximum(high, jnp.where(height < 500.0, height, -nowhere))
    used = low < 500.0
    low = jnp.where(used, low - reach, 0.0)
    high = jnp.where(used, high + reach, 0.0)
    below = low < 0.0
    above = high >= box_height
    low = jnp.where(below, low + box_height, low)
    high = jnp.where(above, high - box_height, high)
    low_bin = jnp.clip((low * table_rate).astype(jnp.int32), 0, LANES - 1)
    high_bin = jnp.floor(high * table_rate).astype(jnp.int32) + 1
    high_in = jnp.clip(high_bin, 0, LANES - 1)
    quarter = lane_iota(cells) // CLASSES
    most = jnp.zeros((cells, LANES), jnp.int32)
    for nb in range(9):
        df, dt = nb // 3, nb % 3
        heights = j_ref[2, f + df, 7 + dt : 7 + dt + cells, :]
        table = j_ref[7, f + df, 7 + dt : 7 + dt + cells, :]
        held = held_ref[f + df, 7 + dt : 7 + dt + cells, :]
        first = take(table, low_bin).astype(jnp.int32)
        step = (first < LANES - 1) & (take(heights, jnp.minimum(first + 1, LANES - 1)) < low)
        first = jnp.where(step, first + 2, first)
        step = (first < LANES) & (take(heights, jnp.minimum(first, LANES - 1)) < low)
        first = jnp.where(step, first + 1, first)
        last = jnp.where(high_bin >= LANES, held, take(table, high_in).astype(jnp.int32))
        step = (last >= 2) & (take(heights, jnp.maximum(last - 2, 0)) > high)
        last = jnp.where(step, last - 2, last)
        step = (last >= 1) & (take(heights, jnp.maximum(last - 1, 0)) > high)
        last = jnp.where(step, last - 1, last)
        first = jnp.where(below, first - held, first)
        last = jnp.where(above, last + held, last)
        count = jnp.where(used, last - first, 0)
        most = jnp.maximum(most, count)
        base_ref[combo0 + nb, at : at + cells, :] = first + quarter
        count_ref[combo0 + nb, at : at + cells, :] = count - quarter
    reach_ref[at : at + cells, :] = most


def pair_sums(j_ref, f, r0, i_ref, i0, base_ref, count_ref, held_ref, steps):
    beads = [[i_ref[c * SHARE + v, pl.ds(i0, 8), :] for c in range(7)] for v in range(SHARE)]

    def body(t, sums):
        sums = list(sums)
        k = t * SHARE
        for nb in range(9):
            df, dt = nb // 3, nb % 3
            rows = pl.ds(r0 + (7 + dt), 8)
            held = held_ref[f + df, rows, :]
            at = base_ref[nb, pl.ds(i0, 8), :] + k
            under, over = at < 0, at >= held
            lanes = (at + jnp.where(under, held, jnp.where(over, -held, 0))) & (LANES - 1)
            turn = jnp.where(under, -box_height, jnp.where(over, box_height, 0.0))
            turn = jnp.where(count_ref[nb, pl.ds(i0, 8), :] > k, turn, 10.0 * nowhere)
            other = [take(j_ref[c, f + df, rows, :], lanes) for c in range(7)]
            if df != 1:
                other[0] = other[0] + (df - 1.0)
            if dt != 1:
                other[1] = other[1] + (dt - 1.0)
            other[2] = other[2] + turn
            for v in range(SHARE):
                own = beads[v]
                dx, dy, dz = own[0] - other[0], own[1] - other[1], own[2] - other[2]
                dist_sq = jnp.maximum(dx * dx + dy * dy + dz * dz, 1e-30)
                weight = jnp.maximum(lax.rsqrt(dist_sq) - 1.0, 0.0)
                along = ((own[3] - other[3]) * dx + (own[4] - other[4]) * dy
                         + (own[5] - other[5]) * dz)
                ratio = own[6] * other[6] - hash_shift
                noise = ratio - jnp.round(ratio)
                scalar = weight * ((noise_slope * noise + noise_base) - weight * along)
                sums[v] = sums[v] + scalar * dx
                sums[SHARE + v] = sums[SHARE + v] + scalar * dy
                sums[2 * SHARE + v] = sums[2 * SHARE + v] + scalar * dz
        return tuple(sums)

    zero = jnp.zeros((8, LANES), jnp.float32)
    return lax.fori_loop(0, steps, body, (zero,) * (3 * SHARE))


def unsorted_sums(sums, rank):
    lanes = rank // SHARE
    which = rank % SHARE
    out = []
    for c in range(3):
        total = None
        for v in range(SHARE):
            part = sums[c * SHARE + v]
            part = part + pltpu.roll(part, LANES // 2, 1)
            part = part + pltpu.roll(part, LANES // 4, 1)
            part = take(part, lanes)
            total = part if total is None else jnp.where(which == v, part, total)
        out.append(total)
    return out


def arrange(i_ref, sort_ref, f, cells, at):
    lane = lane_iota(cells) % CLASSES
    for v in range(SHARE):
        lanes = lane * SHARE + v
        for c in range(7):
            field = take(sort_ref[c, f], lanes)
            if c == 6:
                field = jnp.round(field * seed_modulus)
            i_ref[c * SHARE + v, at : at + cells, :] = field


def force_kernel(end_ref, msort_ref, psort_ref, mraw_ref, praw_ref, mrank_ref, prank_ref,
                 below_ref, above_ref, left_ref, right_ref, bin_ref, push_ref,
                 mpos_out, mvel_out, mforce_out, ppos_out, pvel_out, pforce_out,
                 mj_ref, pj_ref, mi_ref, pi_ref, mbase_ref, mcount_ref, pbase_ref, pcount_ref,
                 mheld_ref, pheld_ref, mreach_ref, preach_ref, steps_ref):
    flow_rows, cells = msort_ref.shape[1], msort_ref.shape[2]
    prec_cells = psort_ref.shape[2]
    ends = tuple(end_ref[e] > 0 for e in range(4))
    assemble(mj_ref, msort_ref, lambda c: below_ref[c, 0:cells, :], lambda c: above_ref[c, 0:cells, :],
             left_ref, right_ref, 0, ends)
    assemble(pj_ref, psort_ref, lambda c: below_ref[c, cells : cells + prec_cells, :],
             lambda c: above_ref[c, cells : cells + prec_cells, :], left_ref, right_ref,
             flow_rows + 2, None)
    for j_ref, held_ref, n in ((mj_ref, mheld_ref, cells), (pj_ref, pheld_ref, prec_cells)):
        for f in range(held_ref.shape[0]):
            real = (j_ref[2, f, 0 : n + 16, :] < 500.0).astype(jnp.float32)
            held = jnp.sum(real, axis=1, keepdims=True).astype(jnp.int32)
            held_ref[f] = jnp.broadcast_to(held, (n + 16, LANES))
    for f in range(flow_rows):
        arrange(mi_ref, msort_ref, f, cells, f * cells)
    arrange(pi_ref, psort_ref, 0, prec_cells, 0)
    for f in range(flow_rows):
        search(mj_ref, f, cells, mi_ref, mbase_ref, mcount_ref, mheld_ref, mreach_ref, 0)
    search(pj_ref, 0, prec_cells, pi_ref, pbase_ref, pcount_ref, pheld_ref, preach_ref, 0)
    groups = flow_rows * cells // 8
    prec_groups = prec_cells // 8
    for g in range(groups):
        steps_ref[g] = (jnp.max(mreach_ref[8 * g : 8 * g + 8, :]) + (SHARE - 1)) // SHARE
    for g in range(prec_groups):
        steps_ref[groups + g] = (jnp.max(preach_ref[8 * g : 8 * g + 8, :]) + (SHARE - 1)) // SHARE

    def main_group(g, carry):
        f = g // (cells // 8)
        r0 = pl.multiple_of((g % (cells // 8)) * 8, 8)
        i0 = pl.multiple_of(g * 8, 8)
        sums = pair_sums(mj_ref, f, r0, mi_ref, i0, mbase_ref, mcount_ref, mheld_ref, steps_ref[g])
        force = unsorted_sums(sums, mrank_ref[pl.ds(i0, 8), :])
        occupied = mraw_ref[6, pl.ds(i0, 8), :] >= 0.0
        push = take(jnp.broadcast_to(push_ref[...], (8, LANES)), bin_ref[pl.ds(r0, 8), :])
        force[0] = force[0] + push * (f == flow_rows - 1).astype(jnp.float32)
        for c in range(3):
            half = mraw_ref[3 + c, pl.ds(i0, 8), :]
            mforce_out[f, pl.ds(r0, 8), c, :] = jnp.where(occupied, force[c], 0.0)
            mvel_out[f, pl.ds(r0, 8), c, :] = jnp.where(
                occupied, half + 0.5 * time_step * force[c], 0.0
            )
            mpos_out[f, pl.ds(r0, 8), c, :] = jnp.where(
                occupied, mraw_ref[c, pl.ds(i0, 8), :], 0.0
            )
        return carry

    def prec_group(g, carry):
        r0 = pl.multiple_of(g * 8, 8)
        sums = pair_sums(pj_ref, 0, r0, pi_ref, r0, pbase_ref, pcount_ref, pheld_ref,
                         steps_ref[groups + g])
        force = unsorted_sums(sums, prank_ref[pl.ds(r0, 8), :])
        for c in range(3):
            half = praw_ref[3 + c, pl.ds(r0, 8), :]
            pforce_out[0, pl.ds(r0, 8), c, :] = force[c]
            pvel_out[0, pl.ds(r0, 8), c, :] = half + 0.5 * time_step * force[c]
            ppos_out[0, pl.ds(r0, 8), c, :] = praw_ref[c, pl.ds(r0, 8), :]
        return carry

    lax.fori_loop(0, prec_groups, prec_group, 0)
    lax.fori_loop(0, groups, main_group, 0)


def whole(space, n):
    return [pl.BlockSpec(memory_space=space)] * n


def shape(dims, dtype=jnp.float32):
    return jax.ShapeDtypeStruct(dims, dtype)


def shards(
    main_pos,
    main_vel,
    main_force,
    main_seed,
    main_count,
    prec_pos,
    prec_vel,
    prec_force,
    prec_seed,
    cross_row,
    cross_dest,
    cross_cell,
    outlet_bin,
    outlet_coef,
):
    flow_rows, cells = main_seed.shape[0], main_seed.shape[1]
    prec_cells = prec_seed.shape[1]
    flow_index = lax.axis_index("flow")
    trans_index = lax.axis_index("trans")
    flow_devices = lax.axis_size("flow")
    trans_devices = lax.axis_size("trans")
    rows = cross_row.shape[0]
    count_column = main_count.reshape(flow_rows * cells, 1)
    big = pltpu.CompilerParams(vmem_limit_bytes=48 << 20)

    payload, profile = pl.pallas_call(
        start_kernel,
        out_shape=(shape((16, rows)), shape((1, LANES))),
        in_specs=whole(SMEM, 3) + whole(VMEM, 6),
        out_specs=tuple(whole(VMEM, 2)),
        compiler_params=big,
        name="start",
    )(cross_row, cross_dest, cross_cell, count_column, prec_pos, prec_vel, prec_force, prec_seed,
      outlet_bin)
    gathered = lax.all_gather(payload, "trans", axis=0)
    total_profile = lax.psum(profile[0, 0:BINS], "trans")
    density = total_profile * BINS / (cells * trans_devices * LANES)
    push = -outlet_coef * density
    push = jnp.where(flow_index == flow_devices - 1, push, 0.0)
    push = jnp.concatenate([push, jnp.zeros((LANES - BINS,), jnp.float32)])[None]
    dests = gathered[:, 10, :].reshape(-1).astype(jnp.int32)
    places = gathered[:, 11, :].reshape(-1).astype(jnp.int32)
    me = jnp.where(flow_index == 0, trans_index, -1).astype(jnp.int32)[None]

    total = flow_rows * cells
    msort, psort, mraw, praw, mrank, prank = pl.pallas_call(
        prep_kernel,
        out_shape=(
            shape((8, flow_rows, cells, LANES)),
            shape((8, 1, prec_cells, LANES)),
            shape((7, total, LANES)),
            shape((7, prec_cells, LANES)),
            shape((total, LANES), jnp.int32),
            shape((prec_cells, LANES), jnp.int32),
        ),
        in_specs=whole(SMEM, 5) + whole(VMEM, 9),
        out_specs=tuple(whole(VMEM, 6)),
        scratch_shapes=[VMEM((10, total, LANES), jnp.float32), SMEM((cells,), jnp.int32)],
        compiler_params=big,
        name="prep",
    )(dests, places, gathered.reshape(-1), me, main_count[0], count_column,
      main_pos, main_vel, main_force, main_seed, prec_pos, prec_vel, prec_force, prec_seed)

    def ring(value, axis, step):
        count = lax.axis_size(axis)
        return lax.ppermute(value, axis, [(i, (i + step) % count) for i in range(count)])

    top = jnp.concatenate([msort[:, flow_rows - 1], psort[:, 0]], axis=1)
    bottom = jnp.concatenate([msort[:, 0], psort[:, 0]], axis=1)
    below = ring(top, "flow", 1)
    above = ring(bottom, "flow", -1)

    def column(at_main, at_prec):
        return jnp.stack(
            [below[:, at_main]]
            + [msort[:, f, at_main] for f in range(flow_rows)]
            + [above[:, at_main], below[:, cells + at_prec], psort[:, 0, at_prec],
               above[:, cells + at_prec]],
            axis=1,
        )

    left = ring(column(cells - 1, prec_cells - 1), "trans", 1)
    right = ring(column(0, 0), "trans", -1)
    ends = jnp.stack([
        flow_index > 0,
        flow_index < flow_devices - 1,
        trans_index > 0,
        trans_index < trans_devices - 1,
    ]).astype(jnp.int32)

    out_main = shape((flow_rows, cells, 3, LANES))
    out_prec = shape((1, prec_cells, 3, LANES))
    return pl.pallas_call(
        force_kernel,
        out_shape=(out_main, out_main, out_main, out_prec, out_prec, out_prec),
        in_specs=whole(SMEM, 1) + whole(VMEM, 12),
        out_specs=tuple(whole(VMEM, 6)),
        scratch_shapes=[
            VMEM((8, flow_rows + 2, cells + 16, LANES), jnp.float32),
            VMEM((8, 3, prec_cells + 16, LANES), jnp.float32),
            VMEM((7 * SHARE, total, LANES), jnp.float32),
            VMEM((7 * SHARE, prec_cells, LANES), jnp.float32),
            VMEM((9, total, LANES), jnp.int32),
            VMEM((9, total, LANES), jnp.int32),
            VMEM((9, prec_cells, LANES), jnp.int32),
            VMEM((9, prec_cells, LANES), jnp.int32),
            VMEM((flow_rows + 2, cells + 16, LANES), jnp.int32),
            VMEM((3, prec_cells + 16, LANES), jnp.int32),
            VMEM((total, LANES), jnp.int32),
            VMEM((prec_cells, LANES), jnp.int32),
            SMEM((total // 8 + prec_cells // 8,), jnp.int32),
        ],
        compiler_params=big,
        name="force",
    )(ends, msort, psort, mraw, praw, mrank, prank, below, above, left, right, outlet_bin, push)


def solution(mesh):
    return jax.shard_map(
        shards,
        mesh=mesh,
        in_specs=(
            P("flow", "trans", None, None),
            P("flow", "trans", None, None),
            P("flow", "trans", None, None),
            P("flow", "trans", None),
            P("flow", "trans"),
            P("flow", "trans", None, None),
            P("flow", "trans", None, None),
            P("flow", "trans", None, None),
            P("flow", "trans", None),
            P("trans"),
            P("trans"),
            P("trans"),
            P("trans", None),
            P(),
        ),
        out_specs=(
            P("flow", "trans", None, None),
            P("flow", "trans", None, None),
            P("flow", "trans", None, None),
            P("flow", "trans", None, None),
            P("flow", "trans", None, None),
            P("flow", "trans", None, None),
        ),
        check_vma=False,
    )
```

```python
import jax
import jax.numpy as jnp
from jax import lax
from jax.experimental import pallas as pl
from jax.experimental.pallas import tpu as pltpu
from jax.sharding import PartitionSpec as P

BINS = 64
LANES = 128
SHARE = 4
CLASSES = LANES // SHARE

time_step = 0.01
repulsion = 25.0
friction = 4.5
noise_amp = 30.0
box_height = 16.0
seed_modulus = 4093
unit_spread = 3.4641016151377544

reach = 1.0005
nowhere = 1000.0
table_rate = 8.0
hash_shift = 2047.0 / 4093.0
noise_slope = noise_amp * unit_spread
noise_base = repulsion - noise_slope * 0.5 / 4093.0

VMEM = pltpu.VMEM
SMEM = pltpu.SMEM


def take(rows, lanes):
    return jnp.take_along_axis(rows, lanes, axis=1, mode="promise_in_bounds")


def lane_iota(rows):
    return lax.broadcasted_iota(jnp.int32, (rows, LANES), 1)


def centred(seed):
    code = seed + 1
    code = jnp.where(code > 2046, code - seed_modulus, code)
    return jnp.where(code > 2046, code - seed_modulus, code)


def start_kernel(row_ref, dest_ref, cell_ref, count_ref, pos_ref, vel_ref, force_ref, seed_ref,
                 bin_ref, out_ref):
    rows = row_ref.shape[0]
    lane = lane_iota(1)
    lines = [jnp.zeros((1, LANES), jnp.float32) for _ in range(2)]

    def put(field, q, value):
        at = field * rows + q
        lines[at // LANES] = jnp.where(lane == at % LANES, value, lines[at // LANES])

    for q in range(rows):
        cell = row_ref[q] // LANES
        slot = row_ref[q] % LANES
        hit = lane == slot
        for a, ref in enumerate((pos_ref, vel_ref, force_ref)):
            for c in range(3):
                value = jnp.where(hit, ref[0, c, pl.ds(cell, 1), :], 0.0)
                put(3 * a + c, q, jnp.sum(value, axis=1, keepdims=True))
        seed = jnp.where(hit, seed_ref[0, pl.ds(cell, 1), :].astype(jnp.float32), 0.0)
        put(9, q, jnp.sum(seed, axis=1, keepdims=True))
        put(10, q, dest_ref[q].astype(jnp.float32))
        put(11, q, cell_ref[q].astype(jnp.float32))
    last = count_ref.shape[0] // 2
    bins = jnp.where(lane_iota(last) < count_ref[last:, :], bin_ref[...], BINS)
    profile = jnp.zeros((1, LANES), jnp.float32)
    for b in range(BINS):
        hits = jnp.sum((bins == b).astype(jnp.float32), axis=0, keepdims=True)
        profile = jnp.where(lane == b, jnp.sum(hits, axis=1, keepdims=True), profile)
    out_ref[...] = jnp.zeros(out_ref.shape, jnp.float32)
    out_ref[0:1, :] = lines[0]
    out_ref[1:2, :] = lines[1]
    out_ref[2:3, :] = profile


def exchange_kernel(own_ref, out_ref, send_sem, recv_sem):
    me = lax.axis_index("trans")
    count = out_ref.shape[0]
    barrier = pltpu.get_barrier_semaphore()

    def greet(s, carry):
        pl.semaphore_signal(barrier, inc=1, device_id={"trans": lax.rem(me + s, count)},
                            device_id_type=pl.DeviceIdType.MESH)
        return carry

    lax.fori_loop(1, count, greet, 0)
    pl.semaphore_wait(barrier, count - 1)

    def copy(s, slot):
        return pltpu.make_async_remote_copy(
            src_ref=own_ref, dst_ref=out_ref.at[slot], send_sem=send_sem.at[s],
            recv_sem=recv_sem.at[slot], device_id={"trans": lax.rem(me + s, count)},
            device_id_type=pl.DeviceIdType.MESH)

    def send(s, carry):
        copy(s, me).start()
        return carry

    def finish(s, carry):
        copy(s, lax.rem(me + count - s, count)).wait_recv()
        copy(s, me).wait_send()
        return carry

    lax.fori_loop(1, count, send, 0)
    out_ref[me] = own_ref[...]
    lax.fori_loop(1, count, finish, 0)


def halo_kernel(msort_ref, psort_ref, left_ref, right_ref, below_ref, above_ref, side_ref,
                send_sem, recv_sem):
    flow, trans = lax.axis_index("flow"), lax.axis_index("trans")
    flows, transes = lax.axis_size("flow"), lax.axis_size("trans")
    flow_rows, cells = msort_ref.shape[1], msort_ref.shape[2]
    prec_cells = psort_ref.shape[2]

    def at(df, dt):
        return (lax.rem(flow + flows + df, flows), lax.rem(trans + transes + dt, transes))

    mesh_id = pl.DeviceIdType.MESH
    barrier = pltpu.get_barrier_semaphore()
    around = [(df, dt) for df in (-1, 0, 1) for dt in (-1, 0, 1) if (df, dt) != (0, 0)]
    for df, dt in around:
        pl.semaphore_signal(barrier, inc=1, device_id=at(df, dt), device_id_type=mesh_id)
    pl.semaphore_wait(barrier, len(around))
    main_part, prec_part = pl.ds(0, cells), pl.ds(cells, prec_cells)
    plan = [
        (msort_ref.at[:, flow_rows - 1], below_ref.at[:, main_part], (1, 0)),
        (msort_ref.at[:, 0], above_ref.at[:, main_part], (-1, 0)),
        (psort_ref.at[:, 0], below_ref.at[:, prec_part], (1, 0)),
        (psort_ref.at[:, 0], above_ref.at[:, prec_part], (-1, 0)),
        (right_ref, side_ref.at[0], (0, 1)),
        (right_ref, side_ref.at[1], (1, 1)),
        (right_ref, side_ref.at[2], (-1, 1)),
        (left_ref, side_ref.at[3], (0, -1)),
        (left_ref, side_ref.at[4], (1, -1)),
        (left_ref, side_ref.at[5], (-1, -1)),
    ]
    copies = [
        pltpu.make_async_remote_copy(src_ref=src, dst_ref=dst, send_sem=send_sem.at[n],
                                     recv_sem=recv_sem.at[n], device_id=at(*step),
                                     device_id_type=mesh_id)
        for n, (src, dst, step) in enumerate(plan)
    ]
    for copy in copies:
        copy.start()
    for copy in copies:
        copy.wait()


def sorted_by(key, rows):
    lane = lane_iota(rows)
    load = lane
    size = 2
    while size <= LANES:
        dist = size // 2
        while dist >= 1:
            partner = lane ^ dist
            low = ((lane & size) == 0) == ((lane & dist) == 0)
            sign = jnp.where(low, 1.0, -1.0)
            other_key = take(key, partner)
            other_load = take(load, partner)
            swap = (other_key - key) * sign < 0.0
            key = jnp.where(swap, other_key, key)
            load = jnp.where(swap, other_load, load)
            dist //= 2
        size *= 2
    return key, load


def first_at_least(sorted_rows, bound, rows):
    at = jnp.zeros((rows, LANES), jnp.int32)
    step = LANES // 2
    while step >= 1:
        below = take(sorted_rows, at + (step - 1)) < bound
        at = jnp.where(below, at + step, at)
        step //= 2
    return jnp.where(take(sorted_rows, at) < bound, at + 1, at)


def prep_kernel(pay_ref, me_ref, count0_ref, share_ref, count_ref, coef_ref, got_ref,
                mpos_ref, mvel_ref, mforce_ref, mseed_ref,
                ppos_ref, pvel_ref, pforce_ref, pseed_ref,
                msort_ref, psort_ref, mraw_ref, praw_ref, mrank_ref, prank_ref,
                left_ref, right_ref, push_ref, raw_ref, filled_ref):
    flow_rows, cells = mseed_ref.shape[0], mseed_ref.shape[1]
    sources = got_ref.shape[0]
    stride = pay_ref.shape[0] // sources
    per = 16
    profile = jnp.sum(got_ref[:, 2:3, :], axis=0)
    push_ref[...] = -coef_ref[...] * (profile * share_ref[0])
    for f in range(flow_rows):
        for c in range(3):
            raw_ref[c, f * cells : (f + 1) * cells, :] = mpos_ref[f, c]
            raw_ref[3 + c, f * cells : (f + 1) * cells, :] = mvel_ref[f, c]
            raw_ref[6 + c, f * cells : (f + 1) * cells, :] = mforce_ref[f, c]
        seed = mseed_ref[f]
        occupied = lane_iota(cells) < count_ref[f * cells : (f + 1) * cells, :]
        raw_ref[9, f * cells : (f + 1) * cells, :] = jnp.where(occupied, seed, -1).astype(jnp.float32)

    me = me_ref[0]

    def fill(cell, carry):
        filled_ref[cell] = count0_ref[cell]
        return carry

    lax.fori_loop(0, cells, fill, 0)
    lane1 = lane_iota(1)

    def look(source, carry):
        start = source * stride
        found = pay_ref[start + 10 * per] == me
        for u in range(1, per):
            found = found | (pay_ref[start + 10 * per + u] == me)

        @pl.when(found)
        def _():
            def one(u, inner):
                origin = start + u

                @pl.when(pay_ref[origin + 10 * per] == me)
                def _():
                    cell = pay_ref[origin + 11 * per].astype(jnp.int32)
                    slot = filled_ref[cell]
                    filled_ref[cell] = slot + 1
                    for c in range(10):
                        row = raw_ref[c, pl.ds(cell, 1), :]
                        raw_ref[c, pl.ds(cell, 1), :] = jnp.where(
                            lane1 == slot, pay_ref[origin + c * per], row
                        )

                return inner

            lax.fori_loop(0, per, one, 0)

        return carry

    @pl.when(me >= 0.0)
    def _():
        lax.fori_loop(0, sources, look, 0)

    def finish(state, seed, rows, sort_ref, rank_ref, raw_out, f, at):
        occupied = seed >= 0
        half = [state[3 + c] + 0.5 * time_step * state[6 + c] for c in range(3)]
        moved = [state[c] + time_step * half[c] for c in range(3)]
        for c in range(3):
            raw_out[c, at : at + rows, :] = moved[c]
            raw_out[3 + c, at : at + rows, :] = half[c]
        raw_out[6, at : at + rows, :] = seed.astype(jnp.float32)
        height = moved[2] - box_height * jnp.floor(moved[2] * (1.0 / box_height))
        key, order = sorted_by(jnp.where(occupied, height, nowhere), rows)
        _, rank = sorted_by(order.astype(jnp.float32), rows)
        rank_ref[at : at + rows, :] = rank
        hashed = centred(seed).astype(jnp.float32) / seed_modulus
        fields = [moved[0], moved[1], None] + [friction * v for v in half] + [hashed]
        for c, field in enumerate(fields):
            if field is None:
                sort_ref[c, f, :, :] = key
            else:
                sort_ref[c, f, :, :] = take(jnp.where(occupied, field, 0.0), order)
        edges = lane_iota(rows).astype(jnp.float32) * (1.0 / table_rate)
        sort_ref[7, f, :, :] = first_at_least(key, edges, rows).astype(jnp.float32)

    for f in range(flow_rows):
        at = f * cells
        state = [raw_ref[c, at : at + cells, :] for c in range(9)]
        finish(state, raw_ref[9, at : at + cells, :].astype(jnp.int32), cells,
               msort_ref, mrank_ref, mraw_ref, f, at)
    state = [ref[0, c] for ref in (ppos_ref, pvel_ref, pforce_ref) for c in range(3)]
    prec_cells = pseed_ref.shape[1]
    finish(state, pseed_ref[0], prec_cells, psort_ref, prank_ref, praw_ref, 0, 0)
    left_ref[...] = jnp.zeros(left_ref.shape, jnp.float32)
    right_ref[...] = jnp.zeros(right_ref.shape, jnp.float32)
    for c in range(msort_ref.shape[0]):
        for f in range(flow_rows):
            left_ref[c, f : f + 1, :] = msort_ref[c, f, 0:1, :]
            right_ref[c, f : f + 1, :] = msort_ref[c, f, cells - 1 : cells, :]
        left_ref[c, flow_rows : flow_rows + 1, :] = psort_ref[c, 0, 0:1, :]
        right_ref[c, flow_rows : flow_rows + 1, :] = psort_ref[c, 0, prec_cells - 1 : prec_cells, :]


def assemble(j_ref, sort_ref, below, above, side_ref, shift, open_ends):
    fields, flow_rows, cells, _ = sort_ref.shape

    def keep(c, value, here):
        if open_ends is None or c != 2:
            return value
        return jnp.where(here, value, nowhere)

    for c in range(fields):
        for f in range(flow_rows):
            j_ref[c, 1 + f, 8 : 8 + cells, :] = sort_ref[c, f]
        ends = open_ends or (True,) * 4
        j_ref[c, 0, 8 : 8 + cells, :] = keep(c, below(c), ends[0])
        j_ref[c, 1 + flow_rows, 8 : 8 + cells, :] = keep(c, above(c), ends[1])
        for f in range(flow_rows + 2):
            inside_left, inside_right = ends[2], ends[3]
            if open_ends is not None and f == 0:
                inside_left, inside_right = ends[2] & ends[0], ends[3] & ends[0]
            if open_ends is not None and f == flow_rows + 1:
                inside_left, inside_right = ends[2] & ends[1], ends[3] & ends[1]
            part = 1 if f == 0 else 2 if f == flow_rows + 1 else 0
            row = shift + (flow_rows - 1 if f == 0 else 0 if f == flow_rows + 1 else f - 1)
            j_ref[c, f, 7:8, :] = keep(c, side_ref[part, c, row : row + 1, :], inside_left)
            j_ref[c, f, 8 + cells : 9 + cells, :] = keep(
                c, side_ref[3 + part, c, row : row + 1, :], inside_right
            )


def search(j_ref, f, cells, i_ref, base_ref, count_ref, held_ref, reach_ref, combo0):
    at = f * cells
    low = i_ref[2 * SHARE, at : at + cells, :]
    high = jnp.full((cells, LANES), -nowhere, jnp.float32)
    for v in range(SHARE):
        height = i_ref[2 * SHARE + v, at : at + cells, :]
        high = jnp.maximum(high, jnp.where(height < 500.0, height, -nowhere))
    used = low < 500.0
    low = jnp.where(used, low - reach, 0.0)
    high = jnp.where(used, high + reach, 0.0)
    below = low < 0.0
    above = high >= box_height
    low = jnp.where(below, low + box_height, low)
    high = jnp.where(above, high - box_height, high)
    low_bin = jnp.clip((low * table_rate).astype(jnp.int32), 0, LANES - 1)
    high_bin = jnp.floor(high * table_rate).astype(jnp.int32) + 1
    high_in = jnp.clip(high_bin, 0, LANES - 1)
    quarter = lane_iota(cells) // CLASSES
    most = jnp.zeros((cells, LANES), jnp.int32)
    for nb in range(9):
        df, dt = nb // 3, nb % 3
        heights = j_ref[2, f + df, 7 + dt : 7 + dt + cells, :]
        table = j_ref[7, f + df, 7 + dt : 7 + dt + cells, :]
        held = held_ref[f + df, 7 + dt : 7 + dt + cells, :]
        first = take(table, low_bin).astype(jnp.int32)
        step = (first < LANES - 1) & (take(heights, jnp.minimum(first + 1, LANES - 1)) < low)
        first = jnp.where(step, first + 2, first)
        step = (first < LANES) & (take(heights, jnp.minimum(first, LANES - 1)) < low)
        first = jnp.where(step, first + 1, first)
        last = jnp.where(high_bin >= LANES, held, take(table, high_in).astype(jnp.int32))
        step = (last >= 2) & (take(heights, jnp.maximum(last - 2, 0)) > high)
        last = jnp.where(step, last - 2, last)
        step = (last >= 1) & (take(heights, jnp.maximum(last - 1, 0)) > high)
        last = jnp.where(step, last - 1, last)
        first = jnp.where(below, first - held, first)
        last = jnp.where(above, last + held, last)
        count = jnp.where(used, last - first, 0)
        most = jnp.maximum(most, count)
        base_ref[combo0 + nb, at : at + cells, :] = first + quarter
        count_ref[combo0 + nb, at : at + cells, :] = count - quarter
    reach_ref[at : at + cells, :] = most


def pair_sums(j_ref, f, r0, i_ref, i0, base_ref, count_ref, held_ref, steps):
    beads = [[i_ref[c * SHARE + v, pl.ds(i0, 8), :] for c in range(7)] for v in range(SHARE)]

    def body(t, sums):
        sums = list(sums)
        k = t * SHARE
        for nb in range(9):
            df, dt = nb // 3, nb % 3
            rows = pl.ds(r0 + (7 + dt), 8)
            held = held_ref[f + df, rows, :]
            at = base_ref[nb, pl.ds(i0, 8), :] + k
            under, over = at < 0, at >= held
            lanes = (at + jnp.where(under, held, jnp.where(over, -held, 0))) & (LANES - 1)
            turn = jnp.where(under, -box_height, jnp.where(over, box_height, 0.0))
            turn = jnp.where(count_ref[nb, pl.ds(i0, 8), :] > k, turn, 10.0 * nowhere)
            other = [take(j_ref[c, f + df, rows, :], lanes) for c in range(7)]
            if df != 1:
                other[0] = other[0] + (df - 1.0)
            if dt != 1:
                other[1] = other[1] + (dt - 1.0)
            other[2] = other[2] + turn
            for v in range(SHARE):
                own = beads[v]
                dx, dy, dz = own[0] - other[0], own[1] - other[1], own[2] - other[2]
                dist_sq = jnp.maximum(dx * dx + dy * dy + dz * dz, 1e-30)
                weight = jnp.maximum(lax.rsqrt(dist_sq) - 1.0, 0.0)
                along = ((own[3] - other[3]) * dx + (own[4] - other[4]) * dy
                         + (own[5] - other[5]) * dz)
                ratio = own[6] * other[6] - hash_shift
                noise = ratio - jnp.round(ratio)
                scalar = weight * ((noise_slope * noise + noise_base) - weight * along)
                sums[v] = sums[v] + scalar * dx
                sums[SHARE + v] = sums[SHARE + v] + scalar * dy
                sums[2 * SHARE + v] = sums[2 * SHARE + v] + scalar * dz
        return tuple(sums)

    zero = jnp.zeros((8, LANES), jnp.float32)
    return lax.fori_loop(0, steps, body, (zero,) * (3 * SHARE))


def unsorted_sums(sums, rank):
    lanes = rank // SHARE
    which = rank % SHARE
    out = []
    for c in range(3):
        total = None
        for v in range(SHARE):
            part = sums[c * SHARE + v]
            part = part + pltpu.roll(part, LANES // 2, 1)
            part = part + pltpu.roll(part, LANES // 4, 1)
            part = take(part, lanes)
            total = part if total is None else jnp.where(which == v, part, total)
        out.append(total)
    return out


def arrange(i_ref, sort_ref, f, cells, at):
    lane = lane_iota(cells) % CLASSES
    for v in range(SHARE):
        lanes = lane * SHARE + v
        for c in range(7):
            field = take(sort_ref[c, f], lanes)
            if c == 6:
                field = jnp.round(field * seed_modulus)
            i_ref[c * SHARE + v, at : at + cells, :] = field


def force_kernel(end_ref, msort_ref, psort_ref, mraw_ref, praw_ref, mrank_ref, prank_ref,
                 below_ref, above_ref, side_ref, bin_ref, push_ref,
                 mpos_out, mvel_out, mforce_out, ppos_out, pvel_out, pforce_out,
                 mj_ref, pj_ref, mi_ref, pi_ref, mbase_ref, mcount_ref, pbase_ref, pcount_ref,
                 mheld_ref, pheld_ref, mreach_ref, preach_ref, steps_ref):
    flow_rows, cells = msort_ref.shape[1], msort_ref.shape[2]
    prec_cells = psort_ref.shape[2]
    ends = tuple(end_ref[e] > 0 for e in range(4))
    assemble(mj_ref, msort_ref, lambda c: below_ref[c, 0:cells, :], lambda c: above_ref[c, 0:cells, :],
             side_ref, 0, ends)
    assemble(pj_ref, psort_ref, lambda c: below_ref[c, cells : cells + prec_cells, :],
             lambda c: above_ref[c, cells : cells + prec_cells, :], side_ref,
             flow_rows, None)
    for j_ref, held_ref, n in ((mj_ref, mheld_ref, cells), (pj_ref, pheld_ref, prec_cells)):
        for f in range(held_ref.shape[0]):
            real = (j_ref[2, f, 0 : n + 16, :] < 500.0).astype(jnp.float32)
            held = jnp.sum(real, axis=1, keepdims=True).astype(jnp.int32)
            held_ref[f] = jnp.broadcast_to(held, (n + 16, LANES))
    for f in range(flow_rows):
        arrange(mi_ref, msort_ref, f, cells, f * cells)
    arrange(pi_ref, psort_ref, 0, prec_cells, 0)
    for f in range(flow_rows):
        search(mj_ref, f, cells, mi_ref, mbase_ref, mcount_ref, mheld_ref, mreach_ref, 0)
    search(pj_ref, 0, prec_cells, pi_ref, pbase_ref, pcount_ref, pheld_ref, preach_ref, 0)
    groups = flow_rows * cells // 8
    prec_groups = prec_cells // 8
    for g in range(groups):
        steps_ref[g] = (jnp.max(mreach_ref[8 * g : 8 * g + 8, :]) + (SHARE - 1)) // SHARE
    for g in range(prec_groups):
        steps_ref[groups + g] = (jnp.max(preach_ref[8 * g : 8 * g + 8, :]) + (SHARE - 1)) // SHARE

    def main_group(g, carry):
        f = g // (cells // 8)
        r0 = pl.multiple_of((g % (cells // 8)) * 8, 8)
        i0 = pl.multiple_of(g * 8, 8)
        sums = pair_sums(mj_ref, f, r0, mi_ref, i0, mbase_ref, mcount_ref, mheld_ref, steps_ref[g])
        force = unsorted_sums(sums, mrank_ref[pl.ds(i0, 8), :])
        occupied = mraw_ref[6, pl.ds(i0, 8), :] >= 0.0
        push = take(jnp.broadcast_to(push_ref[...], (8, LANES)), bin_ref[pl.ds(r0, 8), :])
        force[0] = force[0] + push * (f == flow_rows - 1).astype(jnp.float32)
        for c in range(3):
            half = mraw_ref[3 + c, pl.ds(i0, 8), :]
            mforce_out[f, c, pl.ds(r0, 8), :] = jnp.where(occupied, force[c], 0.0)
            mvel_out[f, c, pl.ds(r0, 8), :] = jnp.where(
                occupied, half + 0.5 * time_step * force[c], 0.0
            )
            mpos_out[f, c, pl.ds(r0, 8), :] = jnp.where(
                occupied, mraw_ref[c, pl.ds(i0, 8), :], 0.0
            )
        return carry

    def prec_group(g, carry):
        r0 = pl.multiple_of(g * 8, 8)
        sums = pair_sums(pj_ref, 0, r0, pi_ref, r0, pbase_ref, pcount_ref, pheld_ref,
                         steps_ref[groups + g])
        force = unsorted_sums(sums, prank_ref[pl.ds(r0, 8), :])
        for c in range(3):
            half = praw_ref[3 + c, pl.ds(r0, 8), :]
            pforce_out[0, c, pl.ds(r0, 8), :] = force[c]
            pvel_out[0, c, pl.ds(r0, 8), :] = half + 0.5 * time_step * force[c]
            ppos_out[0, c, pl.ds(r0, 8), :] = praw_ref[c, pl.ds(r0, 8), :]
        return carry

    lax.fori_loop(0, prec_groups, prec_group, 0)
    lax.fori_loop(0, groups, main_group, 0)


def whole(space, n):
    return [pl.BlockSpec(memory_space=space)] * n


def shape(dims, dtype=jnp.float32):
    return jax.ShapeDtypeStruct(dims, dtype)


def shards(
    main_pos,
    main_vel,
    main_force,
    main_seed,
    main_count,
    prec_pos,
    prec_vel,
    prec_force,
    prec_seed,
    cross_row,
    cross_dest,
    cross_cell,
    outlet_bin,
    outlet_coef,
):
    flow_rows, cells = main_seed.shape[0], main_seed.shape[1]
    prec_cells = prec_seed.shape[1]
    flow_index = lax.axis_index("flow")
    trans_index = lax.axis_index("trans")
    flow_devices = lax.axis_size("flow")
    trans_devices = lax.axis_size("trans")
    total = flow_rows * cells
    count_column = main_count.reshape(total, 1)
    big = pltpu.CompilerParams(vmem_limit_bytes=48 << 20)

    def planes(value):
        return jnp.transpose(value, (0, 2, 1, 3))

    main_state = [planes(v) for v in (main_pos, main_vel, main_force)]
    prec_state = [planes(v) for v in (prec_pos, prec_vel, prec_force)]

    def linked(n):
        return pltpu.CompilerParams(vmem_limit_bytes=48 << 20, collective_id=n,
                                    has_side_effects=True)

    own = pl.pallas_call(
        start_kernel,
        out_shape=shape((8, LANES)),
        in_specs=whole(SMEM, 3) + whole(VMEM, 6),
        out_specs=pl.BlockSpec(memory_space=VMEM),
        compiler_params=big,
        name="start",
    )(cross_row, cross_dest, cross_cell, count_column, *prec_state, prec_seed, outlet_bin)
    got = pl.pallas_call(
        exchange_kernel,
        out_shape=shape((trans_devices, 8, LANES)),
        in_specs=whole(VMEM, 1),
        out_specs=pl.BlockSpec(memory_space=VMEM),
        scratch_shapes=[pltpu.SemaphoreType.DMA((trans_devices,))] * 2,
        compiler_params=linked(0),
        name="exchange",
    )(own)
    share = BINS / (cells * trans_devices * LANES)
    share = jnp.where(flow_index == flow_devices - 1, jnp.float32(share), 0.0)[None]
    coef = jnp.concatenate([outlet_coef, jnp.zeros((LANES - BINS,), jnp.float32)])[None]
    me = jnp.where(flow_index == 0, trans_index, -1).astype(jnp.float32)[None]

    msort, psort, mraw, praw, mrank, prank, left, right, push = pl.pallas_call(
        prep_kernel,
        out_shape=(
            shape((8, flow_rows, cells, LANES)),
            shape((8, 1, prec_cells, LANES)),
            shape((7, total, LANES)),
            shape((7, prec_cells, LANES)),
            shape((total, LANES), jnp.int32),
            shape((prec_cells, LANES), jnp.int32),
            shape((8, 8, LANES)),
            shape((8, 8, LANES)),
            shape((1, LANES)),
        ),
        in_specs=whole(SMEM, 4) + whole(VMEM, 11),
        out_specs=tuple(whole(VMEM, 9)),
        scratch_shapes=[VMEM((10, total, LANES), jnp.float32), SMEM((cells,), jnp.int32)],
        compiler_params=big,
        name="prep",
    )(got[:, 0:2].reshape(-1), me, main_count[0], share, count_column, coef, got,
      *main_state, main_seed, *prec_state, prec_seed)

    span = cells + prec_cells
    below, above, side = pl.pallas_call(
        halo_kernel,
        out_shape=(shape((8, span, LANES)), shape((8, span, LANES)), shape((6, 8, 8, LANES))),
        in_specs=whole(VMEM, 4),
        out_specs=tuple(whole(VMEM, 3)),
        scratch_shapes=[pltpu.SemaphoreType.DMA((10,))] * 2,
        compiler_params=linked(1),
        name="halo",
    )(msort, psort, left, right)
    ends = jnp.stack([
        flow_index > 0,
        flow_index < flow_devices - 1,
        trans_index > 0,
        trans_index < trans_devices - 1,
    ]).astype(jnp.int32)

    out_main = shape((flow_rows, 3, cells, LANES))
    out_prec = shape((1, 3, prec_cells, LANES))
    outs = pl.pallas_call(
        force_kernel,
        out_shape=(out_main, out_main, out_main, out_prec, out_prec, out_prec),
        in_specs=whole(SMEM, 1) + whole(VMEM, 11),
        out_specs=tuple(whole(VMEM, 6)),
        scratch_shapes=[
            VMEM((8, flow_rows + 2, cells + 16, LANES), jnp.float32),
            VMEM((8, 3, prec_cells + 16, LANES), jnp.float32),
            VMEM((7 * SHARE, total, LANES), jnp.float32),
            VMEM((7 * SHARE, prec_cells, LANES), jnp.float32),
            VMEM((9, total, LANES), jnp.int32),
            VMEM((9, total, LANES), jnp.int32),
            VMEM((9, prec_cells, LANES), jnp.int32),
            VMEM((9, prec_cells, LANES), jnp.int32),
            VMEM((flow_rows + 2, cells + 16, LANES), jnp.int32),
            VMEM((3, prec_cells + 16, LANES), jnp.int32),
            VMEM((total, LANES), jnp.int32),
            VMEM((prec_cells, LANES), jnp.int32),
            SMEM((total // 8 + prec_cells // 8,), jnp.int32),
        ],
        compiler_params=big,
        name="force",
    )(ends, msort, psort, mraw, praw, mrank, prank, below, above, side, outlet_bin, push)
    return tuple(planes(v) for v in outs)


def solution(mesh):
    return jax.shard_map(
        shards,
        mesh=mesh,
        in_specs=(
            P("flow", "trans", None, None),
            P("flow", "trans", None, None),
            P("flow", "trans", None, None),
            P("flow", "trans", None),
            P("flow", "trans"),
            P("flow", "trans", None, None),
            P("flow", "trans", None, None),
            P("flow", "trans", None, None),
            P("flow", "trans", None),
            P("trans"),
            P("trans"),
            P("trans"),
            P("trans", None),
            P(),
        ),
        out_specs=(
            P("flow", "trans", None, None),
            P("flow", "trans", None, None),
            P("flow", "trans", None, None),
            P("flow", "trans", None, None),
            P("flow", "trans", None, None),
            P("flow", "trans", None, None),
        ),
        check_vma=False,
    )
```

```python
import jax
import jax.numpy as jnp
from jax import lax
from jax.experimental import pallas as pl
from jax.experimental.pallas import tpu as pltpu
from jax.sharding import PartitionSpec as P

BINS = 64
LANES = 128
SHARE = 4
CLASSES = LANES // SHARE

time_step = 0.01
repulsion = 25.0
friction = 4.5
noise_amp = 30.0
box_height = 16.0
seed_modulus = 4093
unit_spread = 3.4641016151377544

reach = 1.0005
nowhere = 1000.0
table_rate = 8.0
hash_shift = 2047.0 / 4093.0
noise_slope = noise_amp * unit_spread
drag = friction / noise_slope
noise_lift = repulsion / noise_slope - 0.5 / 4093.0 - hash_shift

VMEM = pltpu.VMEM
SMEM = pltpu.SMEM


def take(rows, lanes):
    return jnp.take_along_axis(rows, lanes, axis=1, mode="promise_in_bounds")


def lane_iota(rows):
    return lax.broadcasted_iota(jnp.int32, (rows, LANES), 1)


def centred(seed):
    code = seed + 1
    code = jnp.where(code > 2046, code - seed_modulus, code)
    return jnp.where(code > 2046, code - seed_modulus, code)


def first_tile(row_ref, dest_ref, cell_ref, count_ref, arrays, seed_ref, bin_ref, out_ref):
    rows = row_ref.shape[0]
    lane = lane_iota(1)
    lines = [jnp.zeros((1, LANES), jnp.float32) for _ in range(2)]

    def put(field, q, value):
        at = field * rows + q
        lines[at // LANES] = jnp.where(lane == at % LANES, value, lines[at // LANES])

    for q in range(rows):
        cell = row_ref[q] // LANES
        slot = row_ref[q] % LANES
        hit = lane == slot
        for a, ref in enumerate(arrays):
            for c in range(3):
                value = jnp.where(hit, ref[0, c, pl.ds(cell, 1), :], 0.0)
                put(3 * a + c, q, jnp.sum(value, axis=1, keepdims=True))
        seed = jnp.where(hit, seed_ref[0, pl.ds(cell, 1), :].astype(jnp.float32), 0.0)
        put(9, q, jnp.sum(seed, axis=1, keepdims=True))
        put(10, q, dest_ref[q].astype(jnp.float32))
        put(11, q, cell_ref[q].astype(jnp.float32))
    cells = bin_ref.shape[0]
    last = count_ref.shape[0] - cells
    bins = jnp.where(lane_iota(cells) < count_ref[last:, :], bin_ref[...], BINS)
    profile = jnp.zeros((1, LANES), jnp.float32)
    for b in range(BINS):
        hits = jnp.sum((bins == b).astype(jnp.float32), axis=0, keepdims=True)
        profile = jnp.where(lane == b, jnp.sum(hits, axis=1, keepdims=True), profile)
    out_ref[...] = jnp.zeros(out_ref.shape, jnp.float32)
    out_ref[0:1, :] = lines[0]
    out_ref[1:2, :] = lines[1]
    out_ref[2:3, :] = profile


def link_kernel(own_ref, msort_ref, psort_ref, left_ref, right_ref,
                got_ref, below_ref, above_ref, side_ref,
                tile_send, tile_recv, send_sem, recv_sem):
    flow, trans = lax.axis_index("flow"), lax.axis_index("trans")
    flows, count = lax.axis_size("flow"), got_ref.shape[0]
    flow_rows, cells = msort_ref.shape[1], msort_ref.shape[2]
    prec_cells = psort_ref.shape[2]

    def at(df, dt):
        return (lax.rem(flow + flows + df, flows), lax.rem(trans + count + dt, count))

    mesh_id = pl.DeviceIdType.MESH
    barrier = pltpu.get_barrier_semaphore()
    across = [(df, dt) for df in (-1, 1) for dt in (-1, 0, 1)]
    for df, dt in across:
        pl.semaphore_signal(barrier, inc=1, device_id=at(df, dt), device_id_type=mesh_id)

    def greet(s, carry):
        pl.semaphore_signal(barrier, inc=1, device_id=at(0, s), device_id_type=mesh_id)
        return carry

    lax.fori_loop(1, count, greet, 0)
    pl.semaphore_wait(barrier, len(across) + count - 1)
    main_part, prec_part = pl.ds(0, cells), pl.ds(cells, prec_cells)
    plan = [
        (msort_ref.at[:, flow_rows - 1], below_ref.at[:, main_part], (1, 0)),
        (msort_ref.at[:, 0], above_ref.at[:, main_part], (-1, 0)),
        (psort_ref.at[:, 0], below_ref.at[:, prec_part], (1, 0)),
        (psort_ref.at[:, 0], above_ref.at[:, prec_part], (-1, 0)),
        (right_ref, side_ref.at[0], (0, 1)),
        (right_ref, side_ref.at[1], (1, 1)),
        (right_ref, side_ref.at[2], (-1, 1)),
        (left_ref, side_ref.at[3], (0, -1)),
        (left_ref, side_ref.at[4], (1, -1)),
        (left_ref, side_ref.at[5], (-1, -1)),
    ]
    copies = [
        pltpu.make_async_remote_copy(src_ref=src, dst_ref=dst, send_sem=send_sem.at[n],
                                     recv_sem=recv_sem.at[n], device_id=at(*step),
                                     device_id_type=mesh_id)
        for n, (src, dst, step) in enumerate(plan)
    ]
    for copy in copies:
        copy.start()

    def tile(s, slot):
        return pltpu.make_async_remote_copy(
            src_ref=own_ref, dst_ref=got_ref.at[slot], send_sem=tile_send.at[s],
            recv_sem=tile_recv.at[slot], device_id=at(0, s), device_id_type=mesh_id)

    def send(s, carry):
        tile(s, trans).start()
        return carry

    def finish(s, carry):
        tile(s, lax.rem(trans + count - s, count)).wait_recv()
        tile(s, trans).wait_send()
        return carry

    lax.fori_loop(1, count, send, 0)
    got_ref[trans] = own_ref[...]
    lax.fori_loop(1, count, finish, 0)
    for copy in copies:
        copy.wait()


def sorted_lanes(key):
    rows = key.shape[0]
    lane = lane_iota(rows)
    held = key * LANES + lane
    size = 2
    while size <= LANES:
        dist = size // 2
        while dist >= 1:
            low = ((lane & size) == 0) == ((lane & dist) == 0)
            other = take(held, lane ^ dist)
            held = jnp.where(low, jnp.minimum(held, other), jnp.maximum(held, other))
            dist //= 2
        size *= 2
    return held & (LANES - 1)


def height_order(height):
    level = jnp.minimum(height, 16.25) * float(1 << 19)
    return sorted_lanes(level.astype(jnp.int32))


def first_at_least(sorted_rows, bound, rows):
    at = jnp.zeros((rows, LANES), jnp.int32)
    step = LANES // 2
    while step >= 1:
        below = take(sorted_rows, at + (step - 1)) < bound
        at = jnp.where(below, at + step, at)
        step //= 2
    return jnp.where(take(sorted_rows, at) < bound, at + 1, at)


def prep_kernel(row_ref, dest_ref, cell_ref, count_ref,
                bin_ref, ppos_ref, pvel_ref, pforce_ref, pseed_ref,
                mpos_ref, mvel_ref, mforce_ref, mseed_ref,
                own_ref, msort_ref, psort_ref, mraw_ref, praw_ref, mrank_ref, prank_ref,
                left_ref, right_ref,
                bin_in, ppos_in, pvel_in, pforce_in, pseed_in,
                mpos_in, mvel_in, mforce_in, mseed_in, sem_ref):
    outside = (ppos_ref, pvel_ref, pforce_ref, pseed_ref, bin_ref, mpos_ref, mvel_ref, mforce_ref,
               mseed_ref)
    inside = (ppos_in, pvel_in, pforce_in, pseed_in, bin_in, mpos_in, mvel_in, mforce_in, mseed_in)
    loads = [pltpu.make_async_copy(a, b, sem_ref.at[n])
             for n, (a, b) in enumerate(zip(outside, inside))]
    for load in loads:
        load.start()
    for load in loads[:5]:
        load.wait()
    first_tile(row_ref, dest_ref, cell_ref, count_ref, (ppos_in, pvel_in, pforce_in), pseed_in,
               bin_in, own_ref)
    flow_rows, cells = mseed_in.shape[0], mseed_in.shape[1]
    prec_cells = pseed_in.shape[1]

    def finish(arrays, f, seed, rows, sort_ref, rank_ref, raw_out, at):
        occupied = seed >= 0
        pos, vel, force = [[ref[f, c] for c in range(3)] for ref in arrays]
        half = [vel[c] + 0.5 * time_step * force[c] for c in range(3)]
        moved = [pos[c] + time_step * half[c] for c in range(3)]
        for c in range(3):
            raw_out[c, at : at + rows, :] = moved[c]
            raw_out[3 + c, at : at + rows, :] = half[c]
        raw_out[6, at : at + rows, :] = seed.astype(jnp.float32)
        height = moved[2] - box_height * jnp.floor(moved[2] * (1.0 / box_height))
        height = jnp.where(occupied, height, nowhere)
        order = height_order(height)
        rank_ref[at : at + rows, :] = sorted_lanes(order)
        hashed = centred(seed).astype(jnp.float32) / seed_modulus
        fields = [moved[0], moved[1], None] + [drag * v for v in half] + [hashed]
        for c, field in enumerate(fields):
            if field is None:
                height = take(height, order)
                sort_ref[c, f, :, :] = height
            else:
                sort_ref[c, f, :, :] = take(jnp.where(occupied, field, 0.0), order)
        sort_ref[7, f, :, :] = starts_of(height)

    finish((ppos_in, pvel_in, pforce_in), 0, pseed_in[0], prec_cells, psort_ref, prank_ref,
           praw_ref, 0)
    for load in loads[5:]:
        load.wait()
    for f in range(flow_rows):
        at = f * cells
        occupied = lane_iota(cells) < count_ref[at : at + cells, :]
        finish((mpos_in, mvel_in, mforce_in), f, jnp.where(occupied, mseed_in[f], -1), cells,
               msort_ref, mrank_ref, mraw_ref, at)
    left_ref[...] = jnp.zeros(left_ref.shape, jnp.float32)
    right_ref[...] = jnp.zeros(right_ref.shape, jnp.float32)
    for c in range(msort_ref.shape[0]):
        for f in range(flow_rows):
            left_ref[c, f : f + 1, :] = msort_ref[c, f, 0:1, :]
            right_ref[c, f : f + 1, :] = msort_ref[c, f, cells - 1 : cells, :]
        left_ref[c, flow_rows : flow_rows + 1, :] = psort_ref[c, 0, 0:1, :]
        right_ref[c, flow_rows : flow_rows + 1, :] = psort_ref[c, 0, prec_cells - 1 : prec_cells, :]


def starts_of(height):
    edges = lane_iota(height.shape[0]).astype(jnp.float32) * (1.0 / table_rate)
    return first_at_least(height, edges, height.shape[0]).astype(jnp.float32)


def arrivals(me, pay_ref, count0_ref, count_ref, j_ref, raw_ref, rank_ref, filled_ref):
    cells = count0_ref.shape[0]
    per = 16
    stride = 2 * LANES
    sources = pay_ref.shape[0] // stride
    lane = lane_iota(1)
    for row in (7, 8 + cells):
        real = (j_ref[2, 1, row : row + 1, :] < 500.0).astype(jnp.float32)
        filled_ref[row] = jnp.sum(real).astype(jnp.int32)

    def fill(cell, carry):
        filled_ref[8 + cell] = count0_ref[cell]
        return carry

    lax.fori_loop(0, cells, fill, 0)

    def near(origin):
        return jnp.abs(pay_ref[origin + 10 * per] - me) < 1.5

    def look(source, carry):
        start = source * stride
        found = near(start)
        for u in range(1, per):
            found = found | near(start + u)

        @pl.when(found)
        def _():
            def one(u, inner):
                origin = start + u
                off = pay_ref[origin + 10 * per] - me
                cell = pay_ref[origin + 11 * per].astype(jnp.int32)
                own = off == 0.0
                before = (off == -1.0) & (cell == cells - 1)
                after = (off == 1.0) & (cell == 0)

                @pl.when(own | before | after)
                def _():
                    row = jnp.where(own, 8 + cell, jnp.where(before, 7, 8 + cells))
                    slot = filled_ref[row]
                    filled_ref[row] = slot + 1
                    hit = lane == slot
                    state = [jnp.full((1, LANES), pay_ref[origin + c * per], jnp.float32)
                             for c in range(10)]
                    half = [state[3 + c] + 0.5 * time_step * state[6 + c] for c in range(3)]
                    moved = [state[c] + time_step * half[c] for c in range(3)]
                    height = moved[2] - box_height * jnp.floor(moved[2] * (1.0 / box_height))
                    hashed = centred(state[9].astype(jnp.int32)).astype(jnp.float32) / seed_modulus
                    fields = [moved[0], moved[1], height] + [drag * v for v in half] + [hashed]
                    for c in range(7):
                        old = j_ref[c, 1, pl.ds(row, 1), :]
                        j_ref[c, 1, pl.ds(row, 1), :] = jnp.where(hit, fields[c], old)

                    @pl.when(own)
                    def _():
                        for c, value in enumerate(moved + half + [state[9]]):
                            old = raw_ref[c, pl.ds(cell, 1), :]
                            raw_ref[c, pl.ds(cell, 1), :] = jnp.where(hit, value, old)

                return inner

            lax.fori_loop(0, per, one, 0)

        return carry

    lax.fori_loop(0, sources, look, 0)
    order = height_order(j_ref[2, 1])
    for c in range(7):
        j_ref[c, 1] = take(j_ref[c, 1], order)
    j_ref[7, 1] = starts_of(j_ref[2, 1])
    back = sorted_lanes(order[8 : 8 + cells, :])
    lanes = lane_iota(cells)
    listed = jnp.where(lanes < count_ref[0:cells, :], rank_ref[0:cells, :], lanes)
    rank_ref[0:cells, :] = take(back, listed)


def assemble(j_ref, sort_ref, below, above, side_ref, shift, open_ends):
    fields, flow_rows, cells, _ = sort_ref.shape

    def keep(c, value, here):
        if open_ends is None or c != 2:
            return value
        return jnp.where(here, value, nowhere)

    for c in range(fields):
        for f in range(flow_rows):
            j_ref[c, 1 + f, 8 : 8 + cells, :] = sort_ref[c, f]
        ends = open_ends or (True,) * 4
        j_ref[c, 0, 8 : 8 + cells, :] = keep(c, below(c), ends[0])
        j_ref[c, 1 + flow_rows, 8 : 8 + cells, :] = keep(c, above(c), ends[1])
        for f in range(flow_rows + 2):
            inside_left, inside_right = ends[2], ends[3]
            if open_ends is not None and f == 0:
                inside_left, inside_right = ends[2] & ends[0], ends[3] & ends[0]
            if open_ends is not None and f == flow_rows + 1:
                inside_left, inside_right = ends[2] & ends[1], ends[3] & ends[1]
            part = 1 if f == 0 else 2 if f == flow_rows + 1 else 0
            row = shift + (flow_rows - 1 if f == 0 else 0 if f == flow_rows + 1 else f - 1)
            j_ref[c, f, 7:8, :] = keep(c, side_ref[part, c, row : row + 1, :], inside_left)
            j_ref[c, f, 8 + cells : 9 + cells, :] = keep(
                c, side_ref[3 + part, c, row : row + 1, :], inside_right
            )


def search(j_ref, f, cells, i_ref, base_ref, count_ref, held_ref, reach_ref, combo0):
    at = f * cells
    low = i_ref[2 * SHARE, at : at + cells, :]
    high = jnp.full((cells, LANES), -nowhere, jnp.float32)
    for v in range(SHARE):
        height = i_ref[2 * SHARE + v, at : at + cells, :]
        high = jnp.maximum(high, jnp.where(height < 500.0, height, -nowhere))
    used = low < 500.0
    low = jnp.where(used, low - reach, 0.0)
    high = jnp.where(used, high + reach, 0.0)
    below = low < 0.0
    above = high >= box_height
    low = jnp.where(below, low + box_height, low)
    high = jnp.where(above, high - box_height, high)
    low_bin = jnp.clip((low * table_rate).astype(jnp.int32), 0, LANES - 1)
    high_bin = jnp.floor(high * table_rate).astype(jnp.int32) + 1
    high_in = jnp.clip(high_bin, 0, LANES - 1)
    quarter = lane_iota(cells) // CLASSES
    most = jnp.zeros((cells, LANES), jnp.int32)
    for nb in range(9):
        df, dt = nb // 3, nb % 3
        heights = j_ref[2, f + df, 7 + dt : 7 + dt + cells, :]
        table = j_ref[7, f + df, 7 + dt : 7 + dt + cells, :]
        held = held_ref[f + df, 7 + dt : 7 + dt + cells, :]
        first = take(table, low_bin).astype(jnp.int32)
        step = (first < LANES - 1) & (take(heights, jnp.minimum(first + 1, LANES - 1)) < low)
        first = jnp.where(step, first + 2, first)
        step = (first < LANES) & (take(heights, jnp.minimum(first, LANES - 1)) < low)
        first = jnp.where(step, first + 1, first)
        last = jnp.where(high_bin >= LANES, held, take(table, high_in).astype(jnp.int32))
        step = (last >= 2) & (take(heights, jnp.maximum(last - 2, 0)) > high)
        last = jnp.where(step, last - 2, last)
        step = (last >= 1) & (take(heights, jnp.maximum(last - 1, 0)) > high)
        last = jnp.where(step, last - 1, last)
        first = jnp.where(below, first - held, first)
        last = jnp.where(above, last + held, last)
        count = jnp.where(used, last - first, 0)
        most = jnp.maximum(most, count)
        base_ref[combo0 + nb, at : at + cells, :] = first + quarter
        count_ref[combo0 + nb, at : at + cells, :] = count - quarter
    reach_ref[at : at + cells, :] = most


def pair_sums(j_ref, f, r0, i_ref, i0, base_ref, count_ref, held_ref, steps):
    beads = [[i_ref[c * SHARE + v, pl.ds(i0, 8), :] for c in range(7)] for v in range(SHARE)]

    def body(t, sums):
        sums = list(sums)
        k = t * SHARE
        for nb in range(9):
            df, dt = nb // 3, nb % 3
            rows = pl.ds(r0 + (7 + dt), 8)
            held = held_ref[f + df, rows, :]
            at = base_ref[nb, pl.ds(i0, 8), :] + k
            under, over = at < 0, at >= held
            lanes = (at + jnp.where(under, held, jnp.where(over, -held, 0))) & (LANES - 1)
            turn = jnp.where(under, -box_height, jnp.where(over, box_height, 0.0))
            turn = jnp.where(count_ref[nb, pl.ds(i0, 8), :] > k, turn, 10.0 * nowhere)
            other = [take(j_ref[c, f + df, rows, :], lanes) for c in range(7)]
            if df != 1:
                other[0] = other[0] + (df - 1.0)
            if dt != 1:
                other[1] = other[1] + (dt - 1.0)
            other[2] = other[2] + turn
            for v in range(SHARE):
                own = beads[v]
                dx, dy, dz = own[0] - other[0], own[1] - other[1], own[2] - other[2]
                dist_sq = dx * dx + dy * dy + dz * dz
                if nb == 4:
                    dist_sq = jnp.maximum(dist_sq, 1e-30)
                weight = jnp.maximum(lax.rsqrt(dist_sq) - 1.0, 0.0)
                along = ((own[3] - other[3]) * dx + (own[4] - other[4]) * dy
                         + (own[5] - other[5]) * dz)
                ratio = own[6] * other[6]
                noise = (ratio + noise_lift) - jnp.round(ratio - hash_shift)
                scalar = weight * (noise - weight * along)
                sums[v] = sums[v] + scalar * dx
                sums[SHARE + v] = sums[SHARE + v] + scalar * dy
                sums[2 * SHARE + v] = sums[2 * SHARE + v] + scalar * dz
        return tuple(sums)

    zero = jnp.zeros((8, LANES), jnp.float32)
    return lax.fori_loop(0, steps, body, (zero,) * (3 * SHARE))


def unsorted_sums(sums, rank):
    lanes = rank // SHARE
    which = rank % SHARE
    out = []
    for c in range(3):
        total = None
        for v in range(SHARE):
            part = sums[c * SHARE + v]
            part = part + pltpu.roll(part, LANES // 2, 1)
            part = part + pltpu.roll(part, LANES // 4, 1)
            part = take(part, lanes)
            total = part if total is None else jnp.where(which == v, part, total)
        out.append(noise_slope * total)
    return out


def arrange(i_ref, j_ref, f, cells, at):
    lane = lane_iota(cells) % CLASSES
    for v in range(SHARE):
        lanes = lane * SHARE + v
        for c in range(7):
            field = take(j_ref[c, 1 + f, 8 : 8 + cells, :], lanes)
            if c == 6:
                field = jnp.round(field * seed_modulus)
            i_ref[c * SHARE + v, at : at + cells, :] = field


def force_kernel(end_ref, pay_ref, me_ref, count0_ref, share_ref, count_ref, coef_ref, got_ref,
                 msort_ref, psort_ref, mraw_in, praw_ref, mrank_in, prank_ref,
                 below_ref, above_ref, side_ref, bin_ref,
                 mpos_out, mvel_out, mforce_out, ppos_out, pvel_out, pforce_out,
                 mj_ref, pj_ref, mi_ref, pi_ref, mbase_ref, mcount_ref, pbase_ref, pcount_ref,
                 mheld_ref, pheld_ref, mreach_ref, preach_ref, steps_ref,
                 mraw_ref, mrank_ref, filled_ref):
    flow_rows, cells = msort_ref.shape[1], msort_ref.shape[2]
    prec_cells = psort_ref.shape[2]
    ends = tuple(end_ref[e] > 0 for e in range(4))
    assemble(mj_ref, msort_ref, lambda c: below_ref[c, 0:cells, :], lambda c: above_ref[c, 0:cells, :],
             side_ref, 0, ends)
    assemble(pj_ref, psort_ref, lambda c: below_ref[c, cells : cells + prec_cells, :],
             lambda c: above_ref[c, cells : cells + prec_cells, :], side_ref,
             flow_rows, None)
    mraw_ref[...] = mraw_in[...]
    mrank_ref[...] = mrank_in[...]

    @pl.when(me_ref[0] >= 0.0)
    def _():
        arrivals(me_ref[0], pay_ref, count0_ref, count_ref, mj_ref, mraw_ref, mrank_ref, filled_ref)

    push_row = -coef_ref[...] * (jnp.sum(got_ref[:, 2:3, :], axis=0) * share_ref[0])
    push_row = jnp.broadcast_to(push_row, (8, LANES))
    for j_ref, held_ref, n in ((mj_ref, mheld_ref, cells), (pj_ref, pheld_ref, prec_cells)):
        for f in range(held_ref.shape[0]):
            real = (j_ref[2, f, 0 : n + 16, :] < 500.0).astype(jnp.float32)
            held = jnp.sum(real, axis=1, keepdims=True).astype(jnp.int32)
            held_ref[f] = jnp.broadcast_to(held, (n + 16, LANES))
    for f in range(flow_rows):
        arrange(mi_ref, mj_ref, f, cells, f * cells)
    arrange(pi_ref, pj_ref, 0, prec_cells, 0)
    for f in range(flow_rows):
        search(mj_ref, f, cells, mi_ref, mbase_ref, mcount_ref, mheld_ref, mreach_ref, 0)
    search(pj_ref, 0, prec_cells, pi_ref, pbase_ref, pcount_ref, pheld_ref, preach_ref, 0)
    groups = flow_rows * cells // 8
    prec_groups = prec_cells // 8
    for g in range(groups):
        steps_ref[g] = (jnp.max(mreach_ref[8 * g : 8 * g + 8, :]) + (SHARE - 1)) // SHARE
    for g in range(prec_groups):
        steps_ref[groups + g] = (jnp.max(preach_ref[8 * g : 8 * g + 8, :]) + (SHARE - 1)) // SHARE

    def main_group(g, carry):
        f = g // (cells // 8)
        r0 = pl.multiple_of((g % (cells // 8)) * 8, 8)
        i0 = pl.multiple_of(g * 8, 8)
        sums = pair_sums(mj_ref, f, r0, mi_ref, i0, mbase_ref, mcount_ref, mheld_ref, steps_ref[g])
        force = unsorted_sums(sums, mrank_ref[pl.ds(i0, 8), :])
        occupied = mraw_ref[6, pl.ds(i0, 8), :] >= 0.0
        push = take(push_row, bin_ref[pl.ds(r0, 8), :])
        force[0] = force[0] + push * (f == flow_rows - 1).astype(jnp.float32)
        for c in range(3):
            half = mraw_ref[3 + c, pl.ds(i0, 8), :]
            mforce_out[f, c, pl.ds(r0, 8), :] = jnp.where(occupied, force[c], 0.0)
            mvel_out[f, c, pl.ds(r0, 8), :] = jnp.where(
                occupied, half + 0.5 * time_step * force[c], 0.0
            )
            mpos_out[f, c, pl.ds(r0, 8), :] = jnp.where(
                occupied, mraw_ref[c, pl.ds(i0, 8), :], 0.0
            )
        return carry

    def prec_group(g, carry):
        r0 = pl.multiple_of(g * 8, 8)
        sums = pair_sums(pj_ref, 0, r0, pi_ref, r0, pbase_ref, pcount_ref, pheld_ref,
                         steps_ref[groups + g])
        force = unsorted_sums(sums, prank_ref[pl.ds(r0, 8), :])
        for c in range(3):
            half = praw_ref[3 + c, pl.ds(r0, 8), :]
            pforce_out[0, c, pl.ds(r0, 8), :] = force[c]
            pvel_out[0, c, pl.ds(r0, 8), :] = half + 0.5 * time_step * force[c]
            ppos_out[0, c, pl.ds(r0, 8), :] = praw_ref[c, pl.ds(r0, 8), :]
        return carry

    lax.fori_loop(0, prec_groups, prec_group, 0)
    lax.fori_loop(0, groups, main_group, 0)


def whole(space, n):
    return [pl.BlockSpec(memory_space=space)] * n


def shape(dims, dtype=jnp.float32):
    return jax.ShapeDtypeStruct(dims, dtype)


def scratches(flow_rows, cells, prec_cells):
    total = flow_rows * cells
    return [
        VMEM((8, flow_rows + 2, cells + 16, LANES), jnp.float32),
        VMEM((8, 3, prec_cells + 16, LANES), jnp.float32),
        VMEM((7 * SHARE, total, LANES), jnp.float32),
        VMEM((7 * SHARE, prec_cells, LANES), jnp.float32),
        VMEM((9, total, LANES), jnp.int32),
        VMEM((9, total, LANES), jnp.int32),
        VMEM((9, prec_cells, LANES), jnp.int32),
        VMEM((9, prec_cells, LANES), jnp.int32),
        VMEM((flow_rows + 2, cells + 16, LANES), jnp.int32),
        VMEM((3, prec_cells + 16, LANES), jnp.int32),
        VMEM((total, LANES), jnp.int32),
        VMEM((prec_cells, LANES), jnp.int32),
        SMEM((total // 8 + prec_cells // 8,), jnp.int32),
        VMEM((7, total, LANES), jnp.float32),
        VMEM((total, LANES), jnp.int32),
        SMEM((cells + 16,), jnp.int32),
    ]


def shards(
    main_pos,
    main_vel,
    main_force,
    main_seed,
    main_count,
    prec_pos,
    prec_vel,
    prec_force,
    prec_seed,
    cross_row,
    cross_dest,
    cross_cell,
    outlet_bin,
    outlet_coef,
):
    flow_rows, cells = main_seed.shape[0], main_seed.shape[1]
    prec_cells = prec_seed.shape[1]
    flow_index = lax.axis_index("flow")
    trans_index = lax.axis_index("trans")
    flow_devices = lax.axis_size("flow")
    trans_devices = lax.axis_size("trans")
    total = flow_rows * cells
    count_column = main_count.reshape(total, 1)
    big = pltpu.CompilerParams(vmem_limit_bytes=48 << 20)

    def planes(value):
        return jnp.transpose(value, (0, 2, 1, 3))

    main_state = [planes(v) for v in (main_pos, main_vel, main_force)]
    prec_state = [planes(v) for v in (prec_pos, prec_vel, prec_force)]

    share = BINS / (cells * trans_devices * LANES)
    share = jnp.where(flow_index == flow_devices - 1, jnp.float32(share), 0.0)[None]
    coef = jnp.concatenate([outlet_coef, jnp.zeros((LANES - BINS,), jnp.float32)])[None]
    me = jnp.where(flow_index == 0, trans_index, -9).astype(jnp.float32)[None]

    inputs = [outlet_bin, *prec_state, prec_seed, *main_state, main_seed]
    own, msort, psort, mraw, praw, mrank, prank, left, right = pl.pallas_call(
        prep_kernel,
        out_shape=(
            shape((8, LANES)),
            shape((8, flow_rows, cells, LANES)),
            shape((8, 1, prec_cells, LANES)),
            shape((7, total, LANES)),
            shape((7, prec_cells, LANES)),
            shape((total, LANES), jnp.int32),
            shape((prec_cells, LANES), jnp.int32),
            shape((8, 8, LANES)),
            shape((8, 8, LANES)),
        ),
        in_specs=whole(SMEM, 3) + whole(VMEM, 1) + whole(pl.ANY, 9),
        out_specs=tuple(whole(VMEM, 9)),
        scratch_shapes=[VMEM(v.shape, v.dtype) for v in inputs] + [pltpu.SemaphoreType.DMA((9,))],
        compiler_params=big,
        name="prep",
    )(cross_row, cross_dest, cross_cell, count_column, *inputs)

    span = cells + prec_cells
    got, below, above, side = pl.pallas_call(
        link_kernel,
        out_shape=(shape((trans_devices, 8, LANES)), shape((8, span, LANES)),
                   shape((8, span, LANES)), shape((6, 8, 8, LANES))),
        in_specs=whole(VMEM, 5),
        out_specs=tuple(whole(VMEM, 4)),
        scratch_shapes=[pltpu.SemaphoreType.DMA((trans_devices,))] * 2
        + [pltpu.SemaphoreType.DMA((10,))] * 2,
        compiler_params=pltpu.CompilerParams(vmem_limit_bytes=48 << 20, collective_id=0,
                                             has_side_effects=True),
        name="link",
    )(own, msort, psort, left, right)
    ends = jnp.stack([
        flow_index > 0,
        flow_index < flow_devices - 1,
        trans_index > 0,
        trans_index < trans_devices - 1,
    ]).astype(jnp.int32)

    out_main = shape((flow_rows, 3, cells, LANES))
    out_prec = shape((1, 3, prec_cells, LANES))
    outs = pl.pallas_call(
        force_kernel,
        out_shape=(out_main, out_main, out_main, out_prec, out_prec, out_prec),
        in_specs=whole(SMEM, 5) + whole(VMEM, 13),
        out_specs=tuple(whole(VMEM, 6)),
        scratch_shapes=scratches(flow_rows, cells, prec_cells),
        compiler_params=big,
        name="force",
    )(ends, got[:, 0:2].reshape(-1), me, main_count[0], share, count_column, coef, got,
      msort, psort, mraw, praw, mrank, prank, below, above, side, outlet_bin)
    return tuple(planes(v) for v in outs)


def solution(mesh):
    return jax.shard_map(
        shards,
        mesh=mesh,
        in_specs=(
            P("flow", "trans", None, None),
            P("flow", "trans", None, None),
            P("flow", "trans", None, None),
            P("flow", "trans", None),
            P("flow", "trans"),
            P("flow", "trans", None, None),
            P("flow", "trans", None, None),
            P("flow", "trans", None, None),
            P("flow", "trans", None),
            P("trans"),
            P("trans"),
            P("trans"),
            P("trans", None),
            P(),
        ),
        out_specs=(
            P("flow", "trans", None, None),
            P("flow", "trans", None, None),
            P("flow", "trans", None, None),
            P("flow", "trans", None, None),
            P("flow", "trans", None, None),
            P("flow", "trans", None, None),
        ),
        check_vma=False,
    )
```

```python
import jax
import jax.numpy as jnp
from jax import lax
from jax.experimental import pallas as pl
from jax.experimental.pallas import tpu as pltpu
from jax.sharding import PartitionSpec as P

BINS = 64
LANES = 128
SHARE = 4
CLASSES = LANES // SHARE

time_step = 0.01
repulsion = 25.0
friction = 4.5
noise_amp = 30.0
box_height = 16.0
seed_modulus = 4093
unit_spread = 3.4641016151377544

reach = 1.0005
nowhere = 1000.0
table_rate = 8.0
hash_shift = 2047.0 / 4093.0
noise_slope = noise_amp * unit_spread
drag = friction / noise_slope
noise_lift = repulsion / noise_slope - 0.5 / 4093.0 - hash_shift

VMEM = pltpu.VMEM
SMEM = pltpu.SMEM


def take(rows, lanes):
    return jnp.take_along_axis(rows, lanes, axis=1, mode="promise_in_bounds")


def lane_iota(rows):
    return lax.broadcasted_iota(jnp.int32, (rows, LANES), 1)


def column_of(row):
    n = row.shape[1]
    here = (lax.broadcasted_iota(jnp.int32, (n, n), 0) == lax.broadcasted_iota(jnp.int32, (n, n), 1))
    wide = jnp.where(here, jnp.broadcast_to(row.astype(jnp.float32), (n, n)), 0.0)
    return jnp.sum(wide, axis=1, keepdims=True).astype(jnp.int32)


def centred(seed):
    code = seed + 1
    code = jnp.where(code > 2046, code - seed_modulus, code)
    return jnp.where(code > 2046, code - seed_modulus, code)


def first_tile(row_ref, dest_ref, cell_ref, last_count, arrays, seed_ref, bin_ref, out_ref):
    rows = row_ref.shape[0]
    lane = lane_iota(1)
    lines = [jnp.zeros((1, LANES), jnp.float32) for _ in range(2)]

    def put(field, q, value):
        at = field * rows + q
        lines[at // LANES] = jnp.where(lane == at % LANES, value, lines[at // LANES])

    for q in range(rows):
        cell = row_ref[q] // LANES
        slot = row_ref[q] % LANES
        hit = lane == slot
        for a, ref in enumerate(arrays):
            for c in range(3):
                value = jnp.where(hit, ref[0, c, pl.ds(cell, 1), :], 0.0)
                put(3 * a + c, q, jnp.sum(value, axis=1, keepdims=True))
        seed = jnp.where(hit, seed_ref[0, pl.ds(cell, 1), :].astype(jnp.float32), 0.0)
        put(9, q, jnp.sum(seed, axis=1, keepdims=True))
        place = dest_ref[q] * bin_ref.shape[0] + cell_ref[q]
        put(10, q, place.astype(jnp.float32))
    cells = bin_ref.shape[0]
    bins = jnp.where(lane_iota(cells) < last_count, bin_ref[...], BINS)
    profile = jnp.zeros((1, LANES), jnp.float32)
    for b in range(BINS):
        hits = jnp.sum((bins == b).astype(jnp.float32), axis=0, keepdims=True)
        profile = jnp.where(lane == b, jnp.sum(hits, axis=1, keepdims=True), profile)
    out_ref[...] = jnp.zeros(out_ref.shape, jnp.float32)
    out_ref[0:1, :] = lines[0]
    out_ref[1:2, :] = lines[1]
    out_ref[2:3, :] = profile


def link_kernel(own_ref, msort_ref, psort_ref, left_ref, right_ref,
                got_ref, below_ref, above_ref, side_ref,
                tile_send, tile_recv, send_sem, recv_sem):
    flow, trans = lax.axis_index("flow"), lax.axis_index("trans")
    flows, count = lax.axis_size("flow"), got_ref.shape[0]
    flow_rows, cells = msort_ref.shape[1], msort_ref.shape[2]
    prec_cells = psort_ref.shape[2]

    def at(df, dt):
        return (lax.rem(flow + flows + df, flows), lax.rem(trans + count + dt, count))

    mesh_id = pl.DeviceIdType.MESH
    barrier = pltpu.get_barrier_semaphore()
    across = [(df, dt) for df in (-1, 1) for dt in (-1, 0, 1)]
    for df, dt in across:
        pl.semaphore_signal(barrier, inc=1, device_id=at(df, dt), device_id_type=mesh_id)

    def greet(s, carry):
        pl.semaphore_signal(barrier, inc=1, device_id=at(0, s), device_id_type=mesh_id)
        return carry

    meets = (flow == 0) | (flow == flows - 1)

    @pl.when(meets)
    def _():
        lax.fori_loop(1, count, greet, 0)

    @pl.when(jnp.logical_not(meets))
    def _():
        greet(1, 0)
        greet(count - 1, 0)

    pl.semaphore_wait(barrier, len(across) + jnp.where(meets, count - 1, 2))
    main_part, prec_part = pl.ds(0, cells), pl.ds(cells, prec_cells)
    plan = [
        (msort_ref.at[:, flow_rows - 1], below_ref.at[:, main_part], (1, 0)),
        (msort_ref.at[:, 0], above_ref.at[:, main_part], (-1, 0)),
        (psort_ref.at[:, 0], below_ref.at[:, prec_part], (1, 0)),
        (psort_ref.at[:, 0], above_ref.at[:, prec_part], (-1, 0)),
        (right_ref, side_ref.at[0], (0, 1)),
        (right_ref, side_ref.at[1], (1, 1)),
        (right_ref, side_ref.at[2], (-1, 1)),
        (left_ref, side_ref.at[3], (0, -1)),
        (left_ref, side_ref.at[4], (1, -1)),
        (left_ref, side_ref.at[5], (-1, -1)),
    ]
    copies = [
        pltpu.make_async_remote_copy(src_ref=src, dst_ref=dst, send_sem=send_sem.at[n],
                                     recv_sem=recv_sem.at[n], device_id=at(*step),
                                     device_id_type=mesh_id)
        for n, (src, dst, step) in enumerate(plan)
    ]
    for copy in copies:
        copy.start()

    def tile(s, slot):
        return pltpu.make_async_remote_copy(
            src_ref=own_ref, dst_ref=got_ref.at[slot], send_sem=tile_send.at[s],
            recv_sem=tile_recv.at[slot], device_id=at(0, s), device_id_type=mesh_id)

    def send(s, carry):
        tile(s, trans).start()
        return carry

    def finish(s, carry):
        tile(s, lax.rem(trans + count - s, count)).wait_recv()
        tile(s, trans).wait_send()
        return carry

    @pl.when(meets)
    def _():
        lax.fori_loop(1, count, send, 0)
        got_ref[trans] = own_ref[...]
        lax.fori_loop(1, count, finish, 0)

    @pl.when(jnp.logical_not(meets))
    def _():
        got_ref[...] = jnp.zeros(got_ref.shape, jnp.float32)

    for copy in copies:
        copy.wait()


def sorted_lanes(key):
    rows = key.shape[0]
    lane = lane_iota(rows)
    held = key * LANES + lane
    size = 2
    while size <= LANES:
        dist = size // 2
        while dist >= 1:
            low = ((lane & size) == 0) == ((lane & dist) == 0)
            other = take(held, lane ^ dist)
            held = jnp.where(low, jnp.minimum(held, other), jnp.maximum(held, other))
            dist //= 2
        size *= 2
    return held & (LANES - 1)


def height_order(height):
    level = jnp.minimum(height, 16.25) * float(1 << 19)
    return sorted_lanes(level.astype(jnp.int32))


def first_at_least(sorted_rows, bound, rows):
    at = jnp.zeros((rows, LANES), jnp.int32)
    step = LANES // 2
    while step >= 1:
        below = take(sorted_rows, at + (step - 1)) < bound
        at = jnp.where(below, at + step, at)
        step //= 2
    return jnp.where(take(sorted_rows, at) < bound, at + 1, at)


def prep_kernel(row_ref, dest_ref, cell_ref, count_ref,
                bin_ref, ppos_ref, pvel_ref, pforce_ref, pseed_ref,
                mpos_ref, mvel_ref, mforce_ref, mseed_ref,
                own_ref, msort_ref, psort_ref, mraw_ref, praw_ref, mrank_ref, prank_ref,
                left_ref, right_ref,
                bin_in, ppos_in, pvel_in, pforce_in, pseed_in,
                mpos_in, mvel_in, mforce_in, mseed_in, sem_ref):
    outside = (ppos_ref, pvel_ref, pforce_ref, pseed_ref, bin_ref, mpos_ref, mvel_ref, mforce_ref,
               mseed_ref)
    inside = (ppos_in, pvel_in, pforce_in, pseed_in, bin_in, mpos_in, mvel_in, mforce_in, mseed_in)
    loads = [pltpu.make_async_copy(a, b, sem_ref.at[n])
             for n, (a, b) in enumerate(zip(outside, inside))]
    for load in loads:
        load.start()
    for load in loads[:5]:
        load.wait()
    flow_rows, cells = mseed_in.shape[0], mseed_in.shape[1]
    counts = [column_of(count_ref[f : f + 1, :]) for f in range(flow_rows)]
    first_tile(row_ref, dest_ref, cell_ref, counts[-1], (ppos_in, pvel_in, pforce_in), pseed_in,
               bin_in, own_ref)
    flow_rows, cells = mseed_in.shape[0], mseed_in.shape[1]
    prec_cells = pseed_in.shape[1]

    def finish(arrays, f, seed, rows, sort_ref, rank_ref, raw_out, at):
        occupied = seed >= 0
        pos, vel, force = [[ref[f, c] for c in range(3)] for ref in arrays]
        half = [vel[c] + 0.5 * time_step * force[c] for c in range(3)]
        moved = [pos[c] + time_step * half[c] for c in range(3)]
        for c in range(3):
            raw_out[c, at : at + rows, :] = moved[c]
            raw_out[3 + c, at : at + rows, :] = half[c]
        raw_out[6, at : at + rows, :] = seed.astype(jnp.float32)
        height = moved[2] - box_height * jnp.floor(moved[2] * (1.0 / box_height))
        height = jnp.where(occupied, height, nowhere)
        order = height_order(height)
        rank_ref[at : at + rows, :] = sorted_lanes(order)
        hashed = centred(seed).astype(jnp.float32) / seed_modulus
        fields = [moved[0], moved[1], None] + [drag * v for v in half] + [hashed]
        for c, field in enumerate(fields):
            if field is None:
                height = take(height, order)
                sort_ref[c, f, :, :] = height
            else:
                sort_ref[c, f, :, :] = take(jnp.where(occupied, field, 0.0), order)
        sort_ref[7, f, :, :] = starts_of(height)

    finish((ppos_in, pvel_in, pforce_in), 0, pseed_in[0], prec_cells, psort_ref, prank_ref,
           praw_ref, 0)
    for load in loads[5:]:
        load.wait()
    for f in range(flow_rows):
        at = f * cells
        occupied = lane_iota(cells) < counts[f]
        finish((mpos_in, mvel_in, mforce_in), f, jnp.where(occupied, mseed_in[f], -1), cells,
               msort_ref, mrank_ref, mraw_ref, at)
    left_ref[...] = jnp.zeros(left_ref.shape, jnp.float32)
    right_ref[...] = jnp.zeros(right_ref.shape, jnp.float32)
    for c in range(msort_ref.shape[0]):
        for f in range(flow_rows):
            left_ref[c, f : f + 1, :] = msort_ref[c, f, 0:1, :]
            right_ref[c, f : f + 1, :] = msort_ref[c, f, cells - 1 : cells, :]
        left_ref[c, flow_rows : flow_rows + 1, :] = psort_ref[c, 0, 0:1, :]
        right_ref[c, flow_rows : flow_rows + 1, :] = psort_ref[c, 0, prec_cells - 1 : prec_cells, :]


def starts_of(height):
    edges = lane_iota(height.shape[0]).astype(jnp.float32) * (1.0 / table_rate)
    return first_at_least(height, edges, height.shape[0]).astype(jnp.float32)


def arrivals(first, place_ref, pay_ref, count0_ref, count_ref, j_ref, raw_ref, rank_ref, filled_ref):
    cells = count0_ref.shape[1]
    per = 16
    stride = 2 * LANES
    sources = pay_ref.shape[0] // stride
    lane = lane_iota(1)
    for row in (7, 8 + cells):
        real = (j_ref[2, 1, row : row + 1, :] < 500.0).astype(jnp.float32)
        filled_ref[row] = jnp.sum(real).astype(jnp.int32)

    def fill(cell, carry):
        filled_ref[8 + cell] = count0_ref[0, cell]
        return carry

    lax.fori_loop(0, cells, fill, 0)

    def place(source, u):
        return place_ref[source * per + u] - first

    def near(row):
        return (row >= 7) & (row <= 8 + cells)

    def look(source, carry):
        start = source * stride
        found = near(place(source, 0))
        for u in range(1, per):
            found = found | near(place(source, u))

        @pl.when(found)
        def _():
            for u in range(per):
                origin = start + u
                row = place(source, u)

                @pl.when(near(row))
                def _(row=row, origin=origin):
                    cell = row - 8
                    own = (cell >= 0) & (cell < cells)
                    slot = filled_ref[row]
                    filled_ref[row] = slot + 1
                    hit = lane == slot
                    state = [jnp.full((1, LANES), pay_ref[origin + c * per], jnp.float32)
                             for c in range(10)]
                    half = [state[3 + c] + 0.5 * time_step * state[6 + c] for c in range(3)]
                    moved = [state[c] + time_step * half[c] for c in range(3)]
                    height = moved[2] - box_height * jnp.floor(moved[2] * (1.0 / box_height))
                    hashed = centred(state[9].astype(jnp.int32)).astype(jnp.float32) / seed_modulus
                    fields = [moved[0], moved[1], height] + [drag * v for v in half] + [hashed]
                    for c in range(7):
                        old = j_ref[c, 1, pl.ds(row, 1), :]
                        j_ref[c, 1, pl.ds(row, 1), :] = jnp.where(hit, fields[c], old)

                    @pl.when(own)
                    def _(cell=cell, hit=hit, values=moved + half + [state[9]]):
                        for c, value in enumerate(values):
                            old = raw_ref[c, pl.ds(cell, 1), :]
                            raw_ref[c, pl.ds(cell, 1), :] = jnp.where(hit, value, old)

        return carry

    lax.fori_loop(0, sources, look, 0)
    order = height_order(j_ref[2, 1])
    for c in range(7):
        j_ref[c, 1] = take(j_ref[c, 1], order)
    j_ref[7, 1] = starts_of(j_ref[2, 1])
    back = sorted_lanes(order[8 : 8 + cells, :])
    lanes = lane_iota(cells)
    listed = jnp.where(lanes < column_of(count_ref[0:1, :]), rank_ref[0:cells, :], lanes)
    rank_ref[0:cells, :] = take(back, listed)


def assemble(j_ref, sort_ref, below, above, side_ref, shift, open_ends):
    fields, flow_rows, cells, _ = sort_ref.shape

    def keep(c, value, here):
        if open_ends is None or c != 2:
            return value
        return jnp.where(here, value, nowhere)

    for c in range(fields):
        for f in range(flow_rows):
            j_ref[c, 1 + f, 8 : 8 + cells, :] = sort_ref[c, f]
        ends = open_ends or (True,) * 4
        j_ref[c, 0, 8 : 8 + cells, :] = keep(c, below(c), ends[0])
        j_ref[c, 1 + flow_rows, 8 : 8 + cells, :] = keep(c, above(c), ends[1])
        for f in range(flow_rows + 2):
            inside_left, inside_right = ends[2], ends[3]
            if open_ends is not None and f == 0:
                inside_left, inside_right = ends[2] & ends[0], ends[3] & ends[0]
            if open_ends is not None and f == flow_rows + 1:
                inside_left, inside_right = ends[2] & ends[1], ends[3] & ends[1]
            part = 1 if f == 0 else 2 if f == flow_rows + 1 else 0
            row = shift + (flow_rows - 1 if f == 0 else 0 if f == flow_rows + 1 else f - 1)
            j_ref[c, f, 7:8, :] = keep(c, side_ref[part, c, row : row + 1, :], inside_left)
            j_ref[c, f, 8 + cells : 9 + cells, :] = keep(
                c, side_ref[3 + part, c, row : row + 1, :], inside_right
            )


def search(j_ref, f, cells, i_ref, base_ref, count_ref, held_ref, reach_ref, combo0):
    at = f * cells
    low = i_ref[2 * SHARE, at : at + cells, :]
    high = jnp.full((cells, LANES), -nowhere, jnp.float32)
    for v in range(SHARE):
        height = i_ref[2 * SHARE + v, at : at + cells, :]
        high = jnp.maximum(high, jnp.where(height < 500.0, height, -nowhere))
    used = low < 500.0
    low = jnp.where(used, low - reach, 0.0)
    high = jnp.where(used, high + reach, 0.0)
    below = low < 0.0
    above = high >= box_height
    low = jnp.where(below, low + box_height, low)
    high = jnp.where(above, high - box_height, high)
    low_bin = jnp.clip((low * table_rate).astype(jnp.int32), 0, LANES - 1)
    high_bin = jnp.floor(high * table_rate).astype(jnp.int32) + 1
    high_in = jnp.clip(high_bin, 0, LANES - 1)
    quarter = lane_iota(cells) // CLASSES
    most = jnp.zeros((cells, LANES), jnp.int32)
    for nb in range(9):
        df, dt = nb // 3, nb % 3
        heights = j_ref[2, f + df, 7 + dt : 7 + dt + cells, :]
        table = j_ref[7, f + df, 7 + dt : 7 + dt + cells, :]
        held = held_ref[f + df, 7 + dt : 7 + dt + cells, :]
        first = take(table, low_bin).astype(jnp.int32)
        step = (first < LANES - 1) & (take(heights, jnp.minimum(first + 1, LANES - 1)) < low)
        first = jnp.where(step, first + 2, first)
        step = (first < LANES) & (take(heights, jnp.minimum(first, LANES - 1)) < low)
        first = jnp.where(step, first + 1, first)
        last = jnp.where(high_bin >= LANES, held, take(table, high_in).astype(jnp.int32))
        step = (last >= 2) & (take(heights, jnp.maximum(last - 2, 0)) > high)
        last = jnp.where(step, last - 2, last)
        step = (last >= 1) & (take(heights, jnp.maximum(last - 1, 0)) > high)
        last = jnp.where(step, last - 1, last)
        first = jnp.where(below, first - held, first)
        last = jnp.where(above, last + held, last)
        count = jnp.where(used, last - first, 0)
        most = jnp.maximum(most, count)
        base_ref[combo0 + nb, at : at + cells, :] = first + quarter
        count_ref[combo0 + nb, at : at + cells, :] = count - quarter
    reach_ref[at : at + cells, :] = most


def pair_sums(j_ref, f, r0, i_ref, i0, base_ref, count_ref, held_ref, steps):
    beads = [[i_ref[c * SHARE + v, pl.ds(i0, 8), :] for c in range(7)] for v in range(SHARE)]

    def body(t, sums):
        sums = list(sums)
        k = t * SHARE
        for nb in range(9):
            df, dt = nb // 3, nb % 3
            rows = pl.ds(r0 + (7 + dt), 8)
            held = held_ref[f + df, rows, :]
            at = base_ref[nb, pl.ds(i0, 8), :] + k
            under, over = at < 0, at >= held
            lanes = (at + jnp.where(under, held, jnp.where(over, -held, 0))) & (LANES - 1)
            turn = jnp.where(under, -box_height, jnp.where(over, box_height, 0.0))
            turn = jnp.where(count_ref[nb, pl.ds(i0, 8), :] > k, turn, 10.0 * nowhere)
            other = [take(j_ref[c, f + df, rows, :], lanes) for c in range(7)]
            if df != 1:
                other[0] = other[0] + (df - 1.0)
            if dt != 1:
                other[1] = other[1] + (dt - 1.0)
            other[2] = other[2] + turn
            for v in range(SHARE):
                own = beads[v]
                dx, dy, dz = own[0] - other[0], own[1] - other[1], own[2] - other[2]
                dist_sq = dx * dx + dy * dy + dz * dz
                if nb == 4:
                    dist_sq = jnp.maximum(dist_sq, 1e-30)
                weight = jnp.maximum(lax.rsqrt(dist_sq) - 1.0, 0.0)
                along = ((own[3] - other[3]) * dx + (own[4] - other[4]) * dy
                         + (own[5] - other[5]) * dz)
                ratio = own[6] * other[6]
                noise = (ratio + noise_lift) - jnp.round(ratio - hash_shift)
                scalar = weight * (noise - weight * along)
                sums[v] = sums[v] + scalar * dx
                sums[SHARE + v] = sums[SHARE + v] + scalar * dy
                sums[2 * SHARE + v] = sums[2 * SHARE + v] + scalar * dz
        return tuple(sums)

    zero = jnp.zeros((8, LANES), jnp.float32)
    return lax.fori_loop(0, steps, body, (zero,) * (3 * SHARE))


def unsorted_sums(sums, rank):
    lanes = rank // SHARE
    which = rank % SHARE
    out = []
    for c in range(3):
        total = None
        for v in range(SHARE):
            part = sums[c * SHARE + v]
            part = part + pltpu.roll(part, LANES // 2, 1)
            part = part + pltpu.roll(part, LANES // 4, 1)
            part = take(part, lanes)
            total = part if total is None else jnp.where(which == v, part, total)
        out.append(noise_slope * total)
    return out


def arrange(i_ref, j_ref, f, cells, at):
    lane = lane_iota(cells) % CLASSES
    for v in range(SHARE):
        lanes = lane * SHARE + v
        for c in range(7):
            field = take(j_ref[c, 1 + f, 8 : 8 + cells, :], lanes)
            if c == 6:
                field = jnp.round(field * seed_modulus)
            i_ref[c * SHARE + v, at : at + cells, :] = field


def force_kernel(end_ref, place_ref, pay_ref, count0_ref, share_ref, count_ref, coef_ref, got_ref,
                 msort_ref, psort_ref, mraw_in, praw_ref, mrank_in, prank_ref,
                 below_ref, above_ref, side_ref, bin_ref,
                 mpos_out, mvel_out, mforce_out, ppos_out, pvel_out, pforce_out,
                 mj_ref, pj_ref, mi_ref, pi_ref, mbase_ref, mcount_ref, pbase_ref, pcount_ref,
                 mheld_ref, pheld_ref, mreach_ref, preach_ref, steps_ref,
                 mraw_ref, mrank_ref, filled_ref, push_ref):
    flow_rows, cells = msort_ref.shape[1], msort_ref.shape[2]
    prec_cells = psort_ref.shape[2]
    ends = tuple(end_ref[e] > 0 for e in range(4))
    assemble(mj_ref, msort_ref, lambda c: below_ref[c, 0:cells, :], lambda c: above_ref[c, 0:cells, :],
             side_ref, 0, ends)
    assemble(pj_ref, psort_ref, lambda c: below_ref[c, cells : cells + prec_cells, :],
             lambda c: above_ref[c, cells : cells + prec_cells, :], side_ref,
             flow_rows, None)
    mraw_ref[...] = mraw_in[...]
    mrank_ref[...] = mrank_in[...]

    @pl.when(end_ref[0] == 0)
    def _():
        arrivals(end_ref[4], place_ref, pay_ref, count0_ref, count_ref, mj_ref, mraw_ref, mrank_ref,
                 filled_ref)

    profile = jnp.sum(got_ref[:, 2:3, :], axis=0)[:, 0:BINS]
    push_ref[...] = jnp.zeros(push_ref.shape, jnp.float32)
    push_ref[:, 0:BINS] = jnp.broadcast_to(-coef_ref[...] * (profile * share_ref[0]), (8, BINS))
    push_row = push_ref[...]
    for j_ref, held_ref, n in ((mj_ref, mheld_ref, cells), (pj_ref, pheld_ref, prec_cells)):
        for f in range(held_ref.shape[0]):
            real = (j_ref[2, f, 0 : n + 16, :] < 500.0).astype(jnp.float32)
            held = jnp.sum(real, axis=1, keepdims=True).astype(jnp.int32)
            held_ref[f] = jnp.broadcast_to(held, (n + 16, LANES))
    for f in range(flow_rows):
        arrange(mi_ref, mj_ref, f, cells, f * cells)
    arrange(pi_ref, pj_ref, 0, prec_cells, 0)
    for f in range(flow_rows):
        search(mj_ref, f, cells, mi_ref, mbase_ref, mcount_ref, mheld_ref, mreach_ref, 0)
    search(pj_ref, 0, prec_cells, pi_ref, pbase_ref, pcount_ref, pheld_ref, preach_ref, 0)
    groups = flow_rows * cells // 8
    prec_groups = prec_cells // 8
    for g in range(groups):
        steps_ref[g] = (jnp.max(mreach_ref[8 * g : 8 * g + 8, :]) + (SHARE - 1)) // SHARE
    for g in range(prec_groups):
        steps_ref[groups + g] = (jnp.max(preach_ref[8 * g : 8 * g + 8, :]) + (SHARE - 1)) // SHARE

    def main_group(g, carry):
        f = g // (cells // 8)
        r0 = pl.multiple_of((g % (cells // 8)) * 8, 8)
        i0 = pl.multiple_of(g * 8, 8)
        sums = pair_sums(mj_ref, f, r0, mi_ref, i0, mbase_ref, mcount_ref, mheld_ref, steps_ref[g])
        force = unsorted_sums(sums, mrank_ref[pl.ds(i0, 8), :])
        occupied = mraw_ref[6, pl.ds(i0, 8), :] >= 0.0
        push = take(push_row, bin_ref[pl.ds(r0, 8), :])
        force[0] = force[0] + push * (f == flow_rows - 1).astype(jnp.float32)
        for c in range(3):
            half = mraw_ref[3 + c, pl.ds(i0, 8), :]
            mforce_out[f, c, pl.ds(r0, 8), :] = jnp.where(occupied, force[c], 0.0)
            mvel_out[f, c, pl.ds(r0, 8), :] = jnp.where(
                occupied, half + 0.5 * time_step * force[c], 0.0
            )
            mpos_out[f, c, pl.ds(r0, 8), :] = jnp.where(
                occupied, mraw_ref[c, pl.ds(i0, 8), :], 0.0
            )
        return carry

    def prec_group(g, carry):
        r0 = pl.multiple_of(g * 8, 8)
        sums = pair_sums(pj_ref, 0, r0, pi_ref, r0, pbase_ref, pcount_ref, pheld_ref,
                         steps_ref[groups + g])
        force = unsorted_sums(sums, prank_ref[pl.ds(r0, 8), :])
        for c in range(3):
            half = praw_ref[3 + c, pl.ds(r0, 8), :]
            pforce_out[0, c, pl.ds(r0, 8), :] = force[c]
            pvel_out[0, c, pl.ds(r0, 8), :] = half + 0.5 * time_step * force[c]
            ppos_out[0, c, pl.ds(r0, 8), :] = praw_ref[c, pl.ds(r0, 8), :]
        return carry

    lax.fori_loop(0, prec_groups, prec_group, 0)
    lax.fori_loop(0, groups, main_group, 0)


def whole(space, n):
    return [pl.BlockSpec(memory_space=space)] * n


def shape(dims, dtype=jnp.float32):
    return jax.ShapeDtypeStruct(dims, dtype)


def scratches(flow_rows, cells, prec_cells):
    total = flow_rows * cells
    return [
        VMEM((8, flow_rows + 2, cells + 16, LANES), jnp.float32),
        VMEM((8, 3, prec_cells + 16, LANES), jnp.float32),
        VMEM((7 * SHARE, total, LANES), jnp.float32),
        VMEM((7 * SHARE, prec_cells, LANES), jnp.float32),
        VMEM((9, total, LANES), jnp.int32),
        VMEM((9, total, LANES), jnp.int32),
        VMEM((9, prec_cells, LANES), jnp.int32),
        VMEM((9, prec_cells, LANES), jnp.int32),
        VMEM((flow_rows + 2, cells + 16, LANES), jnp.int32),
        VMEM((3, prec_cells + 16, LANES), jnp.int32),
        VMEM((total, LANES), jnp.int32),
        VMEM((prec_cells, LANES), jnp.int32),
        SMEM((total // 8 + prec_cells // 8,), jnp.int32),
        VMEM((7, total, LANES), jnp.float32),
        VMEM((total, LANES), jnp.int32),
        SMEM((cells + 16,), jnp.int32),
        VMEM((8, LANES), jnp.float32),
    ]


def shards(
    main_pos,
    main_vel,
    main_force,
    main_seed,
    main_count,
    prec_pos,
    prec_vel,
    prec_force,
    prec_seed,
    cross_row,
    cross_dest,
    cross_cell,
    outlet_bin,
    outlet_coef,
):
    flow_rows, cells = main_seed.shape[0], main_seed.shape[1]
    prec_cells = prec_seed.shape[1]
    flow_index = lax.axis_index("flow")
    trans_index = lax.axis_index("trans")
    flow_devices = lax.axis_size("flow")
    trans_devices = lax.axis_size("trans")
    total = flow_rows * cells
    big = pltpu.CompilerParams(vmem_limit_bytes=48 << 20)

    def planes(value):
        return jnp.transpose(value, (0, 2, 1, 3))

    main_state = [planes(v) for v in (main_pos, main_vel, main_force)]
    prec_state = [planes(v) for v in (prec_pos, prec_vel, prec_force)]

    share = BINS / (cells * trans_devices * LANES)
    share = jnp.where(flow_index == flow_devices - 1, jnp.float32(share), 0.0)[None]

    inputs = [outlet_bin, *prec_state, prec_seed, *main_state, main_seed]
    own, msort, psort, mraw, praw, mrank, prank, left, right = pl.pallas_call(
        prep_kernel,
        out_shape=(
            shape((8, LANES)),
            shape((8, flow_rows, cells, LANES)),
            shape((8, 1, prec_cells, LANES)),
            shape((7, total, LANES)),
            shape((7, prec_cells, LANES)),
            shape((total, LANES), jnp.int32),
            shape((prec_cells, LANES), jnp.int32),
            shape((8, 8, LANES)),
            shape((8, 8, LANES)),
        ),
        in_specs=whole(SMEM, 3) + whole(VMEM, 1) + whole(pltpu.HBM, 9),
        out_specs=tuple(whole(VMEM, 9)),
        scratch_shapes=[VMEM(v.shape, v.dtype) for v in inputs] + [pltpu.SemaphoreType.DMA((9,))],
        compiler_params=big,
        name="prep",
    )(cross_row, cross_dest, cross_cell, main_count, *inputs)

    span = cells + prec_cells
    got, below, above, side = pl.pallas_call(
        link_kernel,
        out_shape=(shape((trans_devices, 8, LANES)), shape((8, span, LANES)),
                   shape((8, span, LANES)), shape((6, 8, 8, LANES))),
        in_specs=whole(VMEM, 5),
        out_specs=tuple(whole(VMEM, 4)),
        scratch_shapes=[pltpu.SemaphoreType.DMA((trans_devices,))] * 2
        + [pltpu.SemaphoreType.DMA((10,))] * 2,
        compiler_params=pltpu.CompilerParams(vmem_limit_bytes=48 << 20, collective_id=0,
                                             has_side_effects=True),
        name="link",
    )(own, msort, psort, left, right)
    ends = jnp.stack([
        flow_index > 0,
        flow_index < flow_devices - 1,
        trans_index > 0,
        trans_index < trans_devices - 1,
        trans_index * cells - 8,
    ]).astype(jnp.int32)

    out_main = shape((flow_rows, 3, cells, LANES))
    out_prec = shape((1, 3, prec_cells, LANES))
    outs = pl.pallas_call(
        force_kernel,
        out_shape=(out_main, out_main, out_main, out_prec, out_prec, out_prec),
        in_specs=whole(SMEM, 5) + whole(VMEM, 13),
        out_specs=tuple(whole(VMEM, 6)),
        scratch_shapes=scratches(flow_rows, cells, prec_cells),
        compiler_params=big,
        name="force",
    )(ends, got[:, 1, 32:48].reshape(-1).astype(jnp.int32), got[:, 0:2].reshape(-1), main_count,
      share, main_count, outlet_coef[None], got,
      msort, psort, mraw, praw, mrank, prank, below, above, side, outlet_bin)
    return tuple(planes(v) for v in outs)


def solution(mesh):
    return jax.shard_map(
        shards,
        mesh=mesh,
        in_specs=(
            P("flow", "trans", None, None),
            P("flow", "trans", None, None),
            P("flow", "trans", None, None),
            P("flow", "trans", None),
            P("flow", "trans"),
            P("flow", "trans", None, None),
            P("flow", "trans", None, None),
            P("flow", "trans", None, None),
            P("flow", "trans", None),
            P("trans"),
            P("trans"),
            P("trans"),
            P("trans", None),
            P(),
        ),
        out_specs=(
            P("flow", "trans", None, None),
            P("flow", "trans", None, None),
            P("flow", "trans", None, None),
            P("flow", "trans", None, None),
            P("flow", "trans", None, None),
            P("flow", "trans", None, None),
        ),
        check_vma=False,
    )
```

```python
import jax
import jax.numpy as jnp
from jax import lax
from jax.experimental import pallas as pl
from jax.experimental.pallas import tpu as pltpu
from jax.sharding import PartitionSpec as P

BINS = 64
LANES = 128
SHARE = 4
CLASSES = LANES // SHARE

time_step = 0.01
repulsion = 25.0
friction = 4.5
noise_amp = 30.0
box_height = 16.0
seed_modulus = 4093
unit_spread = 3.4641016151377544

reach = 1.0005
nowhere = 1000.0
table_rate = 8.0
hash_shift = 2047.0 / 4093.0
noise_slope = noise_amp * unit_spread
drag = friction / noise_slope
noise_lift = repulsion / noise_slope - 0.5 / 4093.0 - hash_shift

VMEM = pltpu.VMEM
SMEM = pltpu.SMEM


def take(rows, lanes):
    return jnp.take_along_axis(rows, lanes, axis=1, mode="promise_in_bounds")


def lane_iota(rows):
    return lax.broadcasted_iota(jnp.int32, (rows, LANES), 1)


def column_of(row):
    n = row.shape[1]
    here = (lax.broadcasted_iota(jnp.int32, (n, n), 0) == lax.broadcasted_iota(jnp.int32, (n, n), 1))
    wide = jnp.where(here, jnp.broadcast_to(row.astype(jnp.float32), (n, n)), 0.0)
    return jnp.sum(wide, axis=1, keepdims=True).astype(jnp.int32)


def centred(seed):
    code = seed + 1
    code = jnp.where(code > 2046, code - seed_modulus, code)
    return jnp.where(code > 2046, code - seed_modulus, code)


def first_tile(row_ref, dest_ref, cell_ref, last_count, arrays, seed_ref, bin_ref, out_ref):
    rows = row_ref.shape[0]
    lane = lane_iota(1)
    lines = [jnp.zeros((1, LANES), jnp.float32) for _ in range(2)]

    def put(field, q, value):
        at = field * rows + q
        lines[at // LANES] = jnp.where(lane == at % LANES, value, lines[at // LANES])

    for q in range(rows):
        cell = row_ref[q] // LANES
        slot = row_ref[q] % LANES
        hit = lane == slot
        for a, ref in enumerate(arrays):
            for c in range(3):
                value = jnp.where(hit, ref[0, c, pl.ds(cell, 1), :], 0.0)
                put(3 * a + c, q, jnp.sum(value, axis=1, keepdims=True))
        seed = jnp.where(hit, seed_ref[0, pl.ds(cell, 1), :].astype(jnp.float32), 0.0)
        put(9, q, jnp.sum(seed, axis=1, keepdims=True))
        place = dest_ref[q] * bin_ref.shape[0] + cell_ref[q]
        put(10, q, place.astype(jnp.float32))
    cells = bin_ref.shape[0]
    bins = jnp.where(lane_iota(cells) < last_count, bin_ref[...], BINS)
    profile = jnp.zeros((1, LANES), jnp.float32)
    for b in range(BINS):
        hits = jnp.sum((bins == b).astype(jnp.float32), axis=0, keepdims=True)
        profile = jnp.where(lane == b, jnp.sum(hits, axis=1, keepdims=True), profile)
    out_ref[...] = jnp.zeros(out_ref.shape, jnp.float32)
    out_ref[0:1, :] = lines[0]
    out_ref[1:2, :] = lines[1]
    out_ref[2:3, :] = profile


def link_kernel(own_ref, msort_ref, psort_ref, left_ref, right_ref,
                got_ref, below_ref, above_ref, side_ref,
                tile_send, tile_recv, send_sem, recv_sem):
    flow, trans = lax.axis_index("flow"), lax.axis_index("trans")
    flows, count = lax.axis_size("flow"), got_ref.shape[0]
    flow_rows, cells = msort_ref.shape[1], msort_ref.shape[2]
    prec_cells = psort_ref.shape[2]

    def at(df, dt):
        return (lax.rem(flow + flows + df, flows), lax.rem(trans + count + dt, count))

    mesh_id = pl.DeviceIdType.MESH
    barrier = pltpu.get_barrier_semaphore()
    across = [(df, dt) for df in (-1, 1) for dt in (-1, 0, 1)]
    for df, dt in across:
        pl.semaphore_signal(barrier, inc=1, device_id=at(df, dt), device_id_type=mesh_id)

    def greet(s, carry):
        pl.semaphore_signal(barrier, inc=1, device_id=at(0, s), device_id_type=mesh_id)
        return carry

    meets = (flow == 0) | (flow == flows - 1)

    @pl.when(meets)
    def _():
        lax.fori_loop(1, count, greet, 0)

    @pl.when(jnp.logical_not(meets))
    def _():
        greet(1, 0)
        greet(count - 1, 0)

    pl.semaphore_wait(barrier, len(across) + jnp.where(meets, count - 1, 2))
    main_part, prec_part = pl.ds(0, cells), pl.ds(cells, prec_cells)
    plan = [
        (msort_ref.at[:, flow_rows - 1], below_ref.at[:, main_part], (1, 0)),
        (msort_ref.at[:, 0], above_ref.at[:, main_part], (-1, 0)),
        (psort_ref.at[:, 0], below_ref.at[:, prec_part], (1, 0)),
        (psort_ref.at[:, 0], above_ref.at[:, prec_part], (-1, 0)),
        (right_ref, side_ref.at[0], (0, 1)),
        (right_ref, side_ref.at[1], (1, 1)),
        (right_ref, side_ref.at[2], (-1, 1)),
        (left_ref, side_ref.at[3], (0, -1)),
        (left_ref, side_ref.at[4], (1, -1)),
        (left_ref, side_ref.at[5], (-1, -1)),
    ]
    copies = [
        pltpu.make_async_remote_copy(src_ref=src, dst_ref=dst, send_sem=send_sem.at[n],
                                     recv_sem=recv_sem.at[n], device_id=at(*step),
                                     device_id_type=mesh_id)
        for n, (src, dst, step) in enumerate(plan)
    ]
    for copy in copies:
        copy.start()

    def tile(s, slot):
        return pltpu.make_async_remote_copy(
            src_ref=own_ref, dst_ref=got_ref.at[slot], send_sem=tile_send.at[s],
            recv_sem=tile_recv.at[slot], device_id=at(0, s), device_id_type=mesh_id)

    def send(s, carry):
        tile(s, trans).start()
        return carry

    def finish(s, carry):
        tile(s, lax.rem(trans + count - s, count)).wait_recv()
        tile(s, trans).wait_send()
        return carry

    @pl.when(meets)
    def _():
        lax.fori_loop(1, count, send, 0)
        got_ref[trans] = own_ref[...]
        lax.fori_loop(1, count, finish, 0)

    @pl.when(jnp.logical_not(meets))
    def _():
        got_ref[...] = jnp.zeros(got_ref.shape, jnp.float32)

    for copy in copies:
        copy.wait()


def sorted_keys(key):
    rows = key.shape[0]
    lane = lane_iota(rows)
    size = 2
    while size <= LANES:
        dist = size // 2
        while dist >= 1:
            low = ((lane & size) == 0) == ((lane & dist) == 0)
            other = take(key, lane ^ dist)
            key = jnp.where(low, jnp.minimum(key, other), jnp.maximum(key, other))
            dist //= 2
        size *= 2
    return key


def height_keys(height):
    level = jnp.minimum(height, 16.25) * float(1 << 19)
    return level.astype(jnp.int32) * LANES + lane_iota(height.shape[0])


def first_at_least(sorted_rows, bound, rows):
    at = jnp.zeros((rows, LANES), jnp.int32)
    step = LANES // 2
    while step >= 1:
        below = take(sorted_rows, at + (step - 1)) < bound
        at = jnp.where(below, at + step, at)
        step //= 2
    return jnp.where(take(sorted_rows, at) < bound, at + 1, at)


def sort_state(pos_ref, vel_ref, force_ref, seeds, sort_ref, rank_ref, raw_out):
    flow_rows, rows = len(seeds), seeds[0].shape[0]
    fields, keys = [], []
    for f, seed in enumerate(seeds):
        at = f * rows
        occupied = seed >= 0
        half = [vel_ref[f, c] + 0.5 * time_step * force_ref[f, c] for c in range(3)]
        moved = [pos_ref[f, c] + time_step * half[c] for c in range(3)]
        for c in range(3):
            raw_out[c, at : at + rows, :] = moved[c]
            raw_out[3 + c, at : at + rows, :] = half[c]
        raw_out[6, at : at + rows, :] = seed.astype(jnp.float32)
        height = moved[2] - box_height * jnp.floor(moved[2] * (1.0 / box_height))
        height = jnp.where(occupied, height, nowhere)
        hashed = centred(seed).astype(jnp.float32) / seed_modulus
        fields.append([jnp.where(occupied, v, 0.0) if c != 2 else height for c, v in enumerate(
            moved[0:2] + [height] + [drag * v for v in half] + [hashed])])
        keys.append(height_keys(height))
    key = jnp.concatenate(keys, axis=0)
    total = flow_rows * rows
    ordered = sorted_keys(key)
    order = ordered & (LANES - 1)
    rank_ref[...] = first_at_least(ordered, key, total)
    for c in range(7):
        field = take(jnp.concatenate([v[c] for v in fields], axis=0), order)
        if c == 2:
            starts = starts_of(field)
        for f in range(flow_rows):
            sort_ref[c, f] = field[f * rows : (f + 1) * rows]
    for f in range(flow_rows):
        sort_ref[7, f] = starts[f * rows : (f + 1) * rows]


def prec_kernel(row_ref, dest_ref, cell_ref, count_ref, bin_ref, pos_ref, vel_ref, force_ref,
                seed_ref, own_ref, sort_ref, raw_ref, rank_ref):
    last = count_ref.shape[0] - 1
    first_tile(row_ref, dest_ref, cell_ref, column_of(count_ref[last : last + 1, :]),
               (pos_ref, vel_ref, force_ref), seed_ref, bin_ref, own_ref)
    sort_state(pos_ref, vel_ref, force_ref, [seed_ref[0]], sort_ref, rank_ref, raw_ref)


def main_kernel(count_ref, pos_ref, vel_ref, force_ref, seed_ref, psort_ref,
                msort_ref, raw_ref, rank_ref, left_ref, right_ref):
    flow_rows, cells = seed_ref.shape[0], seed_ref.shape[1]
    prec_cells = psort_ref.shape[2]
    seeds = [
        jnp.where(lane_iota(cells) < column_of(count_ref[f : f + 1, :]), seed_ref[f], -1)
        for f in range(flow_rows)
    ]
    sort_state(pos_ref, vel_ref, force_ref, seeds, msort_ref, rank_ref, raw_ref)
    left_ref[...] = jnp.zeros(left_ref.shape, jnp.float32)
    right_ref[...] = jnp.zeros(right_ref.shape, jnp.float32)
    for c in range(msort_ref.shape[0]):
        for f in range(flow_rows):
            left_ref[c, f : f + 1, :] = msort_ref[c, f, 0:1, :]
            right_ref[c, f : f + 1, :] = msort_ref[c, f, cells - 1 : cells, :]
        left_ref[c, flow_rows : flow_rows + 1, :] = psort_ref[c, 0, 0:1, :]
        right_ref[c, flow_rows : flow_rows + 1, :] = psort_ref[c, 0, prec_cells - 1 : prec_cells, :]


def starts_of(height):
    edges = lane_iota(height.shape[0]).astype(jnp.float32) * (1.0 / table_rate)
    return first_at_least(height, edges, height.shape[0]).astype(jnp.float32)


def arrivals(first, place_ref, got_ref, count0_ref, count_ref, j_ref, raw_ref, rank_ref,
             filled_ref, from_ref):
    cells = count0_ref.shape[1]
    per = 16
    sources = got_ref.shape[0]
    lane = lane_iota(1)
    from_ref[...] = jnp.full(from_ref.shape, -1, jnp.int32)
    for row in (7, 8 + cells):
        real = (j_ref[2, 1, row : row + 1, :] < 500.0).astype(jnp.float32)
        filled_ref[row] = jnp.sum(real).astype(jnp.int32)

    def fill(cell, carry):
        filled_ref[8 + cell] = count0_ref[0, cell]
        return carry

    lax.fori_loop(0, cells, fill, 0)

    def near(row):
        return (row >= 7) & (row <= 8 + cells)

    def look(source, carry):
        rows = [place_ref[source * per + u] - first for u in range(per)]
        found = near(rows[0])
        for u in range(1, per):
            found = found | near(rows[u])

        @pl.when(found)
        def _():
            for u in range(per):

                @pl.when(near(rows[u]))
                def _(row=rows[u], which=source * per + u):
                    slot = filled_ref[row]
                    filled_ref[row] = slot + 1
                    old = from_ref[pl.ds(row, 1), :]
                    from_ref[pl.ds(row, 1), :] = jnp.where(lane == slot, which, old)

        return carry

    lax.fori_loop(0, sources, look, 0)
    rows = from_ref.shape[0]
    came = from_ref[...]
    here = came >= 0
    block, at = came // LANES, came & (LANES - 1)
    lane8 = lane_iota(8)
    mine = lane8 // per == lax.broadcasted_iota(jnp.int32, (8, LANES), 0)
    state = []
    for c in range(10):
        value = jnp.zeros((rows, LANES), jnp.float32)
        for a in range(sources * per // LANES):
            line = got_ref[8 * a : 8 * a + 8, c // 8, :]
            line = take(line, lane8 % per + (c % 8) * per)
            line = jnp.sum(jnp.where(mine, line, 0.0), axis=0, keepdims=True)
            part = take(jnp.broadcast_to(line, (rows, LANES)), at)
            value = jnp.where(block == a, part, value)
        state.append(value)
    half = [state[3 + c] + 0.5 * time_step * state[6 + c] for c in range(3)]
    moved = [state[c] + time_step * half[c] for c in range(3)]
    height = moved[2] - box_height * jnp.floor(moved[2] * (1.0 / box_height))
    hashed = centred(state[9].astype(jnp.int32)).astype(jnp.float32) / seed_modulus
    inner = slice(8, 8 + cells)
    for c, value in enumerate(moved + half + [state[9]]):
        raw_ref[c, 0:cells, :] = jnp.where(here[inner], value[inner], raw_ref[c, 0:cells, :])
    fields = [moved[0], moved[1], height] + [drag * v for v in half] + [hashed]
    fields = [jnp.where(here, fields[c], j_ref[c, 1]) for c in range(7)]
    key = height_keys(fields[2])
    ordered = sorted_keys(key)
    order = ordered & (LANES - 1)
    for c in range(7):
        j_ref[c, 1] = take(fields[c], order)
    j_ref[7, 1] = starts_of(j_ref[2, 1])
    back = first_at_least(ordered, key, rows)[inner]
    lanes = lane_iota(cells)
    listed = jnp.where(lanes < column_of(count_ref[0:1, :]), rank_ref[0:cells, :], lanes)
    rank_ref[0:cells, :] = take(back, listed)


def assemble(j_ref, sort_ref, below, above, side_ref, shift, open_ends):
    fields, flow_rows, cells, _ = sort_ref.shape

    def keep(c, value, here):
        if open_ends is None or c != 2:
            return value
        return jnp.where(here, value, nowhere)

    for c in range(fields):
        for f in range(flow_rows):
            j_ref[c, 1 + f, 8 : 8 + cells, :] = sort_ref[c, f]
        ends = open_ends or (True,) * 4
        j_ref[c, 0, 8 : 8 + cells, :] = keep(c, below(c), ends[0])
        j_ref[c, 1 + flow_rows, 8 : 8 + cells, :] = keep(c, above(c), ends[1])
        for f in range(flow_rows + 2):
            inside_left, inside_right = ends[2], ends[3]
            if open_ends is not None and f == 0:
                inside_left, inside_right = ends[2] & ends[0], ends[3] & ends[0]
            if open_ends is not None and f == flow_rows + 1:
                inside_left, inside_right = ends[2] & ends[1], ends[3] & ends[1]
            part = 1 if f == 0 else 2 if f == flow_rows + 1 else 0
            row = shift + (flow_rows - 1 if f == 0 else 0 if f == flow_rows + 1 else f - 1)
            j_ref[c, f, 7:8, :] = keep(c, side_ref[part, c, row : row + 1, :], inside_left)
            j_ref[c, f, 8 + cells : 9 + cells, :] = keep(
                c, side_ref[3 + part, c, row : row + 1, :], inside_right
            )


def search(j_ref, f, cells, i_ref, base_ref, count_ref, held_ref, reach_ref, combo0):
    at = f * cells
    low = i_ref[2 * SHARE, at : at + cells, :]
    high = jnp.full((cells, LANES), -nowhere, jnp.float32)
    for v in range(SHARE):
        height = i_ref[2 * SHARE + v, at : at + cells, :]
        high = jnp.maximum(high, jnp.where(height < 500.0, height, -nowhere))
    used = low < 500.0
    low = jnp.where(used, low - reach, 0.0)
    high = jnp.where(used, high + reach, 0.0)
    below = low < 0.0
    above = high >= box_height
    low = jnp.where(below, low + box_height, low)
    high = jnp.where(above, high - box_height, high)
    low_bin = jnp.clip((low * table_rate).astype(jnp.int32), 0, LANES - 1)
    high_bin = jnp.floor(high * table_rate).astype(jnp.int32) + 1
    high_in = jnp.clip(high_bin, 0, LANES - 1)
    quarter = lane_iota(cells) // CLASSES
    most = jnp.zeros((cells, LANES), jnp.int32)
    for nb in range(9):
        df, dt = nb // 3, nb % 3
        heights = j_ref[2, f + df, 7 + dt : 7 + dt + cells, :]
        table = j_ref[7, f + df, 7 + dt : 7 + dt + cells, :]
        held = held_ref[f + df, 7 + dt : 7 + dt + cells, :]
        first = take(table, low_bin).astype(jnp.int32)
        step = (first < LANES - 1) & (take(heights, jnp.minimum(first + 1, LANES - 1)) < low)
        first = jnp.where(step, first + 2, first)
        step = (first < LANES) & (take(heights, jnp.minimum(first, LANES - 1)) < low)
        first = jnp.where(step, first + 1, first)
        last = jnp.where(high_bin >= LANES, held, take(table, high_in).astype(jnp.int32))
        step = (last >= 2) & (take(heights, jnp.maximum(last - 2, 0)) > high)
        last = jnp.where(step, last - 2, last)
        step = (last >= 1) & (take(heights, jnp.maximum(last - 1, 0)) > high)
        last = jnp.where(step, last - 1, last)
        first = jnp.where(below, first - held, first)
        last = jnp.where(above, last + held, last)
        count = jnp.where(used, last - first, 0)
        most = jnp.maximum(most, count)
        base_ref[combo0 + nb, at : at + cells, :] = first + quarter
        count_ref[combo0 + nb, at : at + cells, :] = count - quarter
    reach_ref[at : at + cells, :] = most


def pair_sums(j_ref, f, r0, i_ref, i0, base_ref, count_ref, held_ref, steps):
    beads = [[i_ref[c * SHARE + v, pl.ds(i0, 8), :] for c in range(7)] for v in range(SHARE)]

    def body(t, sums):
        sums = list(sums)
        k = t * SHARE
        for nb in range(9):
            df, dt = nb // 3, nb % 3
            rows = pl.ds(r0 + (7 + dt), 8)
            held = held_ref[f + df, rows, :]
            at = base_ref[nb, pl.ds(i0, 8), :] + k
            under, over = at < 0, at >= held
            lanes = (at + jnp.where(under, held, jnp.where(over, -held, 0))) & (LANES - 1)
            turn = jnp.where(under, -box_height, jnp.where(over, box_height, 0.0))
            turn = jnp.where(count_ref[nb, pl.ds(i0, 8), :] > k, turn, 10.0 * nowhere)
            other = [take(j_ref[c, f + df, rows, :], lanes) for c in range(7)]
            if df != 1:
                other[0] = other[0] + (df - 1.0)
            if dt != 1:
                other[1] = other[1] + (dt - 1.0)
            other[2] = other[2] + turn
            for v in range(SHARE):
                own = beads[v]
                dx, dy, dz = own[0] - other[0], own[1] - other[1], own[2] - other[2]
                dist_sq = dx * dx + dy * dy + dz * dz
                if nb == 4:
                    dist_sq = jnp.maximum(dist_sq, 1e-30)
                weight = jnp.maximum(lax.rsqrt(dist_sq) - 1.0, 0.0)
                along = ((own[3] - other[3]) * dx + (own[4] - other[4]) * dy
                         + (own[5] - other[5]) * dz)
                ratio = own[6] * other[6]
                noise = (ratio + noise_lift) - jnp.round(ratio - hash_shift)
                scalar = weight * (noise - weight * along)
                sums[v] = sums[v] + scalar * dx
                sums[SHARE + v] = sums[SHARE + v] + scalar * dy
                sums[2 * SHARE + v] = sums[2 * SHARE + v] + scalar * dz
        return tuple(sums)

    zero = jnp.zeros((8, LANES), jnp.float32)
    return lax.fori_loop(0, steps, body, (zero,) * (3 * SHARE))


def unsorted_sums(sums, rank):
    lanes = rank // SHARE
    which = rank % SHARE
    out = []
    for c in range(3):
        total = None
        for v in range(SHARE):
            part = sums[c * SHARE + v]
            part = part + pltpu.roll(part, LANES // 2, 1)
            part = part + pltpu.roll(part, LANES // 4, 1)
            part = take(part, lanes)
            total = part if total is None else jnp.where(which == v, part, total)
        out.append(noise_slope * total)
    return out


def arrange(i_ref, j_ref, f, cells, at):
    lane = lane_iota(cells) % CLASSES
    for v in range(SHARE):
        lanes = lane * SHARE + v
        for c in range(7):
            field = take(j_ref[c, 1 + f, 8 : 8 + cells, :], lanes)
            if c == 6:
                field = jnp.round(field * seed_modulus)
            i_ref[c * SHARE + v, at : at + cells, :] = field


def force_kernel(end_ref, place_ref, count0_ref, share_ref, count_ref, coef_ref, got_ref,
                 msort_ref, psort_ref, mraw_in, praw_ref, mrank_in, prank_ref,
                 below_ref, above_ref, side_ref, bin_ref,
                 mpos_out, mvel_out, mforce_out, ppos_out, pvel_out, pforce_out,
                 mj_ref, pj_ref, mi_ref, pi_ref, mbase_ref, mcount_ref, pbase_ref, pcount_ref,
                 mheld_ref, pheld_ref, mreach_ref, preach_ref, steps_ref,
                 mraw_ref, mrank_ref, filled_ref, push_ref,
                 from_ref):
    flow_rows, cells = msort_ref.shape[1], msort_ref.shape[2]
    prec_cells = psort_ref.shape[2]
    ends = tuple(end_ref[e] > 0 for e in range(4))
    assemble(mj_ref, msort_ref, lambda c: below_ref[c, 0:cells, :], lambda c: above_ref[c, 0:cells, :],
             side_ref, 0, ends)
    assemble(pj_ref, psort_ref, lambda c: below_ref[c, cells : cells + prec_cells, :],
             lambda c: above_ref[c, cells : cells + prec_cells, :], side_ref,
             flow_rows, None)
    mraw_ref[...] = mraw_in[...]
    mrank_ref[...] = mrank_in[...]

    @pl.when(end_ref[0] == 0)
    def _():
        arrivals(end_ref[4], place_ref, got_ref, count0_ref, count_ref, mj_ref, mraw_ref, mrank_ref,
                 filled_ref, from_ref)

    profile = jnp.sum(got_ref[:, 2:3, :], axis=0)[:, 0:BINS]
    push_ref[...] = jnp.zeros(push_ref.shape, jnp.float32)
    push_ref[:, 0:BINS] = jnp.broadcast_to(-coef_ref[...] * (profile * share_ref[0]), (8, BINS))
    push_row = push_ref[...]
    for j_ref, held_ref, n in ((mj_ref, mheld_ref, cells), (pj_ref, pheld_ref, prec_cells)):
        for f in range(held_ref.shape[0]):
            real = (j_ref[2, f, 0 : n + 16, :] < 500.0).astype(jnp.float32)
            held = jnp.sum(real, axis=1, keepdims=True).astype(jnp.int32)
            held_ref[f] = jnp.broadcast_to(held, (n + 16, LANES))
    for f in range(flow_rows):
        arrange(mi_ref, mj_ref, f, cells, f * cells)
    arrange(pi_ref, pj_ref, 0, prec_cells, 0)
    for f in range(flow_rows):
        search(mj_ref, f, cells, mi_ref, mbase_ref, mcount_ref, mheld_ref, mreach_ref, 0)
    search(pj_ref, 0, prec_cells, pi_ref, pbase_ref, pcount_ref, pheld_ref, preach_ref, 0)
    groups = flow_rows * cells // 8
    prec_groups = prec_cells // 8
    for g in range(groups):
        steps_ref[g] = (jnp.max(mreach_ref[8 * g : 8 * g + 8, :]) + (SHARE - 1)) // SHARE
    for g in range(prec_groups):
        steps_ref[groups + g] = (jnp.max(preach_ref[8 * g : 8 * g + 8, :]) + (SHARE - 1)) // SHARE

    def main_group(g, carry):
        f = g // (cells // 8)
        r0 = pl.multiple_of((g % (cells // 8)) * 8, 8)
        i0 = pl.multiple_of(g * 8, 8)
        sums = pair_sums(mj_ref, f, r0, mi_ref, i0, mbase_ref, mcount_ref, mheld_ref, steps_ref[g])
        force = unsorted_sums(sums, mrank_ref[pl.ds(i0, 8), :])
        occupied = mraw_ref[6, pl.ds(i0, 8), :] >= 0.0
        push = take(push_row, bin_ref[pl.ds(r0, 8), :])
        force[0] = force[0] + push * (f == flow_rows - 1).astype(jnp.float32)
        for c in range(3):
            half = mraw_ref[3 + c, pl.ds(i0, 8), :]
            mforce_out[f, c, pl.ds(r0, 8), :] = jnp.where(occupied, force[c], 0.0)
            mvel_out[f, c, pl.ds(r0, 8), :] = jnp.where(
                occupied, half + 0.5 * time_step * force[c], 0.0
            )
            mpos_out[f, c, pl.ds(r0, 8), :] = jnp.where(
                occupied, mraw_ref[c, pl.ds(i0, 8), :], 0.0
            )
        return carry

    def prec_group(g, carry):
        r0 = pl.multiple_of(g * 8, 8)
        sums = pair_sums(pj_ref, 0, r0, pi_ref, r0, pbase_ref, pcount_ref, pheld_ref,
                         steps_ref[groups + g])
        force = unsorted_sums(sums, prank_ref[pl.ds(r0, 8), :])
        for c in range(3):
            half = praw_ref[3 + c, pl.ds(r0, 8), :]
            pforce_out[0, c, pl.ds(r0, 8), :] = force[c]
            pvel_out[0, c, pl.ds(r0, 8), :] = half + 0.5 * time_step * force[c]
            ppos_out[0, c, pl.ds(r0, 8), :] = praw_ref[c, pl.ds(r0, 8), :]
        return carry

    lax.fori_loop(0, prec_groups, prec_group, 0)
    lax.fori_loop(0, groups, main_group, 0)


def whole(space, n):
    return [pl.BlockSpec(memory_space=space)] * n


def shape(dims, dtype=jnp.float32):
    return jax.ShapeDtypeStruct(dims, dtype)


def scratches(flow_rows, cells, prec_cells):
    total = flow_rows * cells
    return [
        VMEM((8, flow_rows + 2, cells + 16, LANES), jnp.float32),
        VMEM((8, 3, prec_cells + 16, LANES), jnp.float32),
        VMEM((7 * SHARE, total, LANES), jnp.float32),
        VMEM((7 * SHARE, prec_cells, LANES), jnp.float32),
        VMEM((9, total, LANES), jnp.int32),
        VMEM((9, total, LANES), jnp.int32),
        VMEM((9, prec_cells, LANES), jnp.int32),
        VMEM((9, prec_cells, LANES), jnp.int32),
        VMEM((flow_rows + 2, cells + 16, LANES), jnp.int32),
        VMEM((3, prec_cells + 16, LANES), jnp.int32),
        VMEM((total, LANES), jnp.int32),
        VMEM((prec_cells, LANES), jnp.int32),
        SMEM((total // 8 + prec_cells // 8,), jnp.int32),
        VMEM((7, total, LANES), jnp.float32),
        VMEM((total, LANES), jnp.int32),
        SMEM((cells + 16,), jnp.int32),
        VMEM((8, LANES), jnp.float32),
        VMEM((cells + 16, LANES), jnp.int32),
    ]


def shards(
    main_pos,
    main_vel,
    main_force,
    main_seed,
    main_count,
    prec_pos,
    prec_vel,
    prec_force,
    prec_seed,
    cross_row,
    cross_dest,
    cross_cell,
    outlet_bin,
    outlet_coef,
):
    flow_rows, cells = main_seed.shape[0], main_seed.shape[1]
    prec_cells = prec_seed.shape[1]
    flow_index = lax.axis_index("flow")
    trans_index = lax.axis_index("trans")
    flow_devices = lax.axis_size("flow")
    trans_devices = lax.axis_size("trans")
    total = flow_rows * cells
    big = pltpu.CompilerParams(vmem_limit_bytes=48 << 20)

    def planes(value):
        return jnp.transpose(value, (0, 2, 1, 3))

    main_state = [planes(v) for v in (main_pos, main_vel, main_force)]
    prec_state = [planes(v) for v in (prec_pos, prec_vel, prec_force)]

    share = BINS / (cells * trans_devices * LANES)
    share = jnp.where(flow_index == flow_devices - 1, jnp.float32(share), 0.0)[None]

    own, psort, praw, prank = pl.pallas_call(
        prec_kernel,
        out_shape=(
            shape((8, LANES)),
            shape((8, 1, prec_cells, LANES)),
            shape((7, prec_cells, LANES)),
            shape((prec_cells, LANES), jnp.int32),
        ),
        in_specs=whole(SMEM, 3) + whole(VMEM, 6),
        out_specs=tuple(whole(VMEM, 4)),
        compiler_params=big,
        name="prec",
    )(cross_row, cross_dest, cross_cell, main_count, outlet_bin, *prec_state, prec_seed)
    msort, mraw, mrank, left, right = pl.pallas_call(
        main_kernel,
        out_shape=(
            shape((8, flow_rows, cells, LANES)),
            shape((7, total, LANES)),
            shape((total, LANES), jnp.int32),
            shape((8, 8, LANES)),
            shape((8, 8, LANES)),
        ),
        in_specs=whole(VMEM, 6),
        out_specs=tuple(whole(VMEM, 5)),
        compiler_params=big,
        name="main",
    )(main_count, *main_state, main_seed, psort)

    span = cells + prec_cells
    got, below, above, side = pl.pallas_call(
        link_kernel,
        out_shape=(shape((trans_devices, 8, LANES)), shape((8, span, LANES)),
                   shape((8, span, LANES)), shape((6, 8, 8, LANES))),
        in_specs=whole(VMEM, 5),
        out_specs=tuple(whole(VMEM, 4)),
        scratch_shapes=[pltpu.SemaphoreType.DMA((trans_devices,))] * 2
        + [pltpu.SemaphoreType.DMA((10,))] * 2,
        compiler_params=pltpu.CompilerParams(vmem_limit_bytes=48 << 20, collective_id=0,
                                             has_side_effects=True),
        name="link",
    )(own, msort, psort, left, right)
    ends = jnp.stack([
        flow_index > 0,
        flow_index < flow_devices - 1,
        trans_index > 0,
        trans_index < trans_devices - 1,
        trans_index * cells - 8,
    ]).astype(jnp.int32)

    out_main = shape((flow_rows, 3, cells, LANES))
    out_prec = shape((1, 3, prec_cells, LANES))
    outs = pl.pallas_call(
        force_kernel,
        out_shape=(out_main, out_main, out_main, out_prec, out_prec, out_prec),
        in_specs=whole(SMEM, 4) + whole(VMEM, 13),
        out_specs=tuple(whole(VMEM, 6)),
        scratch_shapes=scratches(flow_rows, cells, prec_cells),
        compiler_params=big,
        name="force",
    )(ends, got[:, 1, 32:48].reshape(-1).astype(jnp.int32), main_count,
      share, main_count, outlet_coef[None], got,
      msort, psort, mraw, praw, mrank, prank, below, above, side, outlet_bin)
    return tuple(planes(v) for v in outs)


def solution(mesh):
    return jax.shard_map(
        shards,
        mesh=mesh,
        in_specs=(
            P("flow", "trans", None, None),
            P("flow", "trans", None, None),
            P("flow", "trans", None, None),
            P("flow", "trans", None),
            P("flow", "trans"),
            P("flow", "trans", None, None),
            P("flow", "trans", None, None),
            P("flow", "trans", None, None),
            P("flow", "trans", None),
            P("trans"),
            P("trans"),
            P("trans"),
            P("trans", None),
            P(),
        ),
        out_specs=(
            P("flow", "trans", None, None),
            P("flow", "trans", None, None),
            P("flow", "trans", None, None),
            P("flow", "trans", None, None),
            P("flow", "trans", None, None),
            P("flow", "trans", None, None),
        ),
        check_vma=False,
    )
```

```python
import jax
import jax.numpy as jnp
from jax import lax
from jax.experimental import pallas as pl
from jax.experimental.pallas import tpu as pltpu
from jax.sharding import PartitionSpec as P

BINS = 64
LANES = 128
SHARE = 4
CLASSES = LANES // SHARE

time_step = 0.01
repulsion = 25.0
friction = 4.5
noise_amp = 30.0
box_height = 16.0
seed_modulus = 4093
unit_spread = 3.4641016151377544

reach = 1.0005
nowhere = 1000.0
table_rate = 8.0
hash_shift = 2047.0 / 4093.0
noise_slope = noise_amp * unit_spread
drag = friction / noise_slope
noise_lift = repulsion / noise_slope - 0.5 / 4093.0 - hash_shift

VMEM = pltpu.VMEM
SMEM = pltpu.SMEM


def take(rows, lanes):
    return jnp.take_along_axis(rows, lanes, axis=1, mode="promise_in_bounds")


def lane_iota(rows):
    return lax.broadcasted_iota(jnp.int32, (rows, LANES), 1)


def column_of(row):
    n = row.shape[1]
    here = (lax.broadcasted_iota(jnp.int32, (n, n), 0) == lax.broadcasted_iota(jnp.int32, (n, n), 1))
    wide = jnp.where(here, jnp.broadcast_to(row.astype(jnp.float32), (n, n)), 0.0)
    return jnp.sum(wide, axis=1, keepdims=True).astype(jnp.int32)


def centred(seed):
    code = seed + 1
    code = jnp.where(code > 2046, code - seed_modulus, code)
    return jnp.where(code > 2046, code - seed_modulus, code)


def first_tile(row_ref, dest_ref, cell_ref, last_count, arrays, seed_ref, bin_ref, out_ref):
    rows = row_ref.shape[0]
    lane = lane_iota(1)
    lines = [jnp.zeros((1, LANES), jnp.float32) for _ in range(2)]

    def put(field, q, value):
        at = field * rows + q
        lines[at // LANES] = jnp.where(lane == at % LANES, value, lines[at // LANES])

    for q in range(rows):
        cell = row_ref[q] // LANES
        slot = row_ref[q] % LANES
        hit = lane == slot
        for a, ref in enumerate(arrays):
            for c in range(3):
                value = jnp.where(hit, ref[0, c, pl.ds(cell, 1), :], 0.0)
                put(3 * a + c, q, jnp.sum(value, axis=1, keepdims=True))
        seed = jnp.where(hit, seed_ref[0, pl.ds(cell, 1), :].astype(jnp.float32), 0.0)
        put(9, q, jnp.sum(seed, axis=1, keepdims=True))
        place = dest_ref[q] * bin_ref.shape[0] + cell_ref[q]
        put(10, q, place.astype(jnp.float32))
    cells = bin_ref.shape[0]
    bins = jnp.where(lane_iota(cells) < last_count, bin_ref[...], BINS)
    profile = jnp.zeros((1, LANES), jnp.float32)
    for b in range(BINS):
        hits = jnp.sum((bins == b).astype(jnp.float32), axis=0, keepdims=True)
        profile = jnp.where(lane == b, jnp.sum(hits, axis=1, keepdims=True), profile)
    out_ref[...] = jnp.zeros(out_ref.shape, jnp.float32)
    out_ref[0:1, :] = lines[0]
    out_ref[1:2, :] = lines[1]
    out_ref[2:3, :] = profile


def link_kernel(own_ref, msort_ref, psort_ref, left_ref, right_ref,
                got_ref, below_ref, above_ref, side_ref,
                tile_send, tile_recv, send_sem, recv_sem):
    flow, trans = lax.axis_index("flow"), lax.axis_index("trans")
    flows, count = lax.axis_size("flow"), got_ref.shape[0]
    flow_rows, cells = msort_ref.shape[1], msort_ref.shape[2]
    prec_cells = psort_ref.shape[2]

    def at(df, dt):
        return (lax.rem(flow + flows + df, flows), lax.rem(trans + count + dt, count))

    mesh_id = pl.DeviceIdType.MESH
    barrier = pltpu.get_barrier_semaphore()
    across = [(df, dt) for df in (-1, 1) for dt in (-1, 0, 1)]
    for df, dt in across:
        pl.semaphore_signal(barrier, inc=1, device_id=at(df, dt), device_id_type=mesh_id)

    def greet(s, carry):
        pl.semaphore_signal(barrier, inc=1, device_id=at(0, s), device_id_type=mesh_id)
        return carry

    meets = (flow == 0) | (flow == flows - 1)

    @pl.when(meets)
    def _():
        lax.fori_loop(1, count, greet, 0)

    @pl.when(jnp.logical_not(meets))
    def _():
        greet(1, 0)
        greet(count - 1, 0)

    pl.semaphore_wait(barrier, len(across) + jnp.where(meets, count - 1, 2))
    main_part, prec_part = pl.ds(0, cells), pl.ds(cells, prec_cells)
    plan = [
        (msort_ref.at[:, flow_rows - 1], below_ref.at[:, main_part], (1, 0)),
        (msort_ref.at[:, 0], above_ref.at[:, main_part], (-1, 0)),
        (psort_ref.at[:, 0], below_ref.at[:, prec_part], (1, 0)),
        (psort_ref.at[:, 0], above_ref.at[:, prec_part], (-1, 0)),
        (right_ref, side_ref.at[0], (0, 1)),
        (right_ref, side_ref.at[1], (1, 1)),
        (right_ref, side_ref.at[2], (-1, 1)),
        (left_ref, side_ref.at[3], (0, -1)),
        (left_ref, side_ref.at[4], (1, -1)),
        (left_ref, side_ref.at[5], (-1, -1)),
    ]
    copies = [
        pltpu.make_async_remote_copy(src_ref=src, dst_ref=dst, send_sem=send_sem.at[n],
                                     recv_sem=recv_sem.at[n], device_id=at(*step),
                                     device_id_type=mesh_id)
        for n, (src, dst, step) in enumerate(plan)
    ]
    for copy in copies:
        copy.start()

    def tile(s, slot):
        return pltpu.make_async_remote_copy(
            src_ref=own_ref, dst_ref=got_ref.at[slot], send_sem=tile_send.at[s],
            recv_sem=tile_recv.at[slot], device_id=at(0, s), device_id_type=mesh_id)

    def send(s, carry):
        tile(s, trans).start()
        return carry

    def finish(s, carry):
        tile(s, lax.rem(trans + count - s, count)).wait_recv()
        tile(s, trans).wait_send()
        return carry

    @pl.when(meets)
    def _():
        lax.fori_loop(1, count, send, 0)
        got_ref[trans] = own_ref[...]
        lax.fori_loop(1, count, finish, 0)

    @pl.when(jnp.logical_not(meets))
    def _():
        got_ref[...] = jnp.zeros(got_ref.shape, jnp.float32)

    for copy in copies:
        copy.wait()


def sorted_keys(key):
    rows = key.shape[0]
    lane = lane_iota(rows)
    size = 2
    while size <= LANES:
        dist = size // 2
        while dist >= 1:
            low = ((lane & size) == 0) == ((lane & dist) == 0)
            other = take(key, lane ^ dist)
            key = jnp.where(low, jnp.minimum(key, other), jnp.maximum(key, other))
            dist //= 2
        size *= 2
    return key


def height_keys(height):
    level = jnp.minimum(height, 16.25) * float(1 << 19)
    return level.astype(jnp.int32) * LANES + lane_iota(height.shape[0])


def first_at_least(sorted_rows, bound, rows):
    at = jnp.zeros((rows, LANES), jnp.int32)
    step = LANES // 2
    while step >= 1:
        below = take(sorted_rows, at + (step - 1)) < bound
        at = jnp.where(below, at + step, at)
        step //= 2
    return jnp.where(take(sorted_rows, at) < bound, at + 1, at)


def sort_state(pos_ref, vel_ref, force_ref, seeds, sort_ref, rank_ref, raw_out):
    flow_rows, rows = len(seeds), seeds[0].shape[0]
    fields, keys = [], []
    for f, seed in enumerate(seeds):
        at = f * rows
        occupied = seed >= 0
        half = [vel_ref[f, c] + 0.5 * time_step * force_ref[f, c] for c in range(3)]
        moved = [pos_ref[f, c] + time_step * half[c] for c in range(3)]
        for c in range(3):
            raw_out[c, at : at + rows, :] = moved[c]
            raw_out[3 + c, at : at + rows, :] = half[c]
        raw_out[6, at : at + rows, :] = seed.astype(jnp.float32)
        height = moved[2] - box_height * jnp.floor(moved[2] * (1.0 / box_height))
        height = jnp.where(occupied, height, nowhere)
        hashed = centred(seed).astype(jnp.float32) / seed_modulus
        fields.append([jnp.where(occupied, v, 0.0) if c != 2 else height for c, v in enumerate(
            moved[0:2] + [height] + [drag * v for v in half] + [hashed])])
        keys.append(height_keys(height))
    key = jnp.concatenate(keys, axis=0)
    total = flow_rows * rows
    ordered = sorted_keys(key)
    order = ordered & (LANES - 1)
    rank_ref[...] = first_at_least(ordered, key, total)
    for c in range(7):
        field = take(jnp.concatenate([v[c] for v in fields], axis=0), order)
        if c == 2:
            starts = starts_of(field)
        for f in range(flow_rows):
            sort_ref[c, f] = field[f * rows : (f + 1) * rows]
    for f in range(flow_rows):
        sort_ref[7, f] = starts[f * rows : (f + 1) * rows]


def prec_kernel(row_ref, dest_ref, cell_ref, count_ref, bin_ref, pos_ref, vel_ref, force_ref,
                seed_ref, own_ref, sort_ref, raw_ref, rank_ref):
    last = count_ref.shape[0] - 1
    first_tile(row_ref, dest_ref, cell_ref, column_of(count_ref[last : last + 1, :]),
               (pos_ref, vel_ref, force_ref), seed_ref, bin_ref, own_ref)
    sort_state(pos_ref, vel_ref, force_ref, [seed_ref[0]], sort_ref, rank_ref, raw_ref)


def main_kernel(count_ref, pos_ref, vel_ref, force_ref, seed_ref, psort_ref,
                msort_ref, raw_ref, rank_ref, left_ref, right_ref):
    flow_rows, cells = seed_ref.shape[0], seed_ref.shape[1]
    prec_cells = psort_ref.shape[2]
    seeds = [
        jnp.where(lane_iota(cells) < column_of(count_ref[f : f + 1, :]), seed_ref[f], -1)
        for f in range(flow_rows)
    ]
    sort_state(pos_ref, vel_ref, force_ref, seeds, msort_ref, rank_ref, raw_ref)
    left_ref[...] = jnp.zeros(left_ref.shape, jnp.float32)
    right_ref[...] = jnp.zeros(right_ref.shape, jnp.float32)
    for c in range(msort_ref.shape[0]):
        for f in range(flow_rows):
            left_ref[c, f : f + 1, :] = msort_ref[c, f, 0:1, :]
            right_ref[c, f : f + 1, :] = msort_ref[c, f, cells - 1 : cells, :]
        left_ref[c, flow_rows : flow_rows + 1, :] = psort_ref[c, 0, 0:1, :]
        right_ref[c, flow_rows : flow_rows + 1, :] = psort_ref[c, 0, prec_cells - 1 : prec_cells, :]


def starts_of(height):
    edges = lane_iota(height.shape[0]).astype(jnp.float32) * (1.0 / table_rate)
    return first_at_least(height, edges, height.shape[0]).astype(jnp.float32)


def arrivals(first, place_ref, got_ref, count_ref, j_ref, raw_ref, rank_ref):
    cells = count_ref.shape[1]
    per = 16
    rows = j_ref.shape[2]
    row = lax.broadcasted_iota(jnp.int32, (rows, LANES), 0)
    order_of = lax.broadcasted_iota(jnp.int32, (LANES, LANES), 0)
    upto = (order_of <= lane_iota(LANES)).astype(jnp.float32)
    held = jnp.sum((j_ref[2, 1] < 500.0).astype(jnp.float32), axis=1, keepdims=True)
    turn = lane_iota(rows).astype(jnp.float32) - held + 1.0
    before = jnp.zeros((rows, 1), jnp.float32)
    came = jnp.zeros((rows, LANES), jnp.int32)
    for a in range(place_ref.shape[0]):
        match = (place_ref[a : a + 1, :] - first == row).astype(jnp.float32)
        seen = jnp.dot(match, upto, preferred_element_type=jnp.float32) + before
        before = seen[:, LANES - 1 : LANES]
        came = came + first_at_least(seen, turn, rows)
    came = jnp.where((turn >= 1.0) & (turn <= before), came, -1)
    here = came >= 0
    block, at = came // LANES, came & (LANES - 1)
    lane8 = lane_iota(8)
    mine = lane8 // per == lax.broadcasted_iota(jnp.int32, (8, LANES), 0)
    state = []
    for c in range(10):
        value = jnp.zeros((rows, LANES), jnp.float32)
        for a in range(place_ref.shape[0]):
            line = got_ref[8 * a : 8 * a + 8, c // 8, :]
            line = take(line, lane8 % per + (c % 8) * per)
            line = jnp.sum(jnp.where(mine, line, 0.0), axis=0, keepdims=True)
            part = take(jnp.broadcast_to(line, (rows, LANES)), at)
            value = jnp.where(block == a, part, value)
        state.append(value)
    half = [state[3 + c] + 0.5 * time_step * state[6 + c] for c in range(3)]
    moved = [state[c] + time_step * half[c] for c in range(3)]
    height = moved[2] - box_height * jnp.floor(moved[2] * (1.0 / box_height))
    hashed = centred(state[9].astype(jnp.int32)).astype(jnp.float32) / seed_modulus
    inner = slice(8, 8 + cells)
    for c, value in enumerate(moved + half + [state[9]]):
        raw_ref[c, 0:cells, :] = jnp.where(here[inner], value[inner], raw_ref[c, 0:cells, :])
    fields = [moved[0], moved[1], height] + [drag * v for v in half] + [hashed]
    fields = [jnp.where(here, fields[c], j_ref[c, 1]) for c in range(7)]
    key = height_keys(fields[2])
    ordered = sorted_keys(key)
    order = ordered & (LANES - 1)
    for c in range(7):
        j_ref[c, 1] = take(fields[c], order)
    j_ref[7, 1] = starts_of(j_ref[2, 1])
    back = first_at_least(ordered, key, rows)[inner]
    lanes = lane_iota(cells)
    listed = jnp.where(lanes < column_of(count_ref[0:1, :]), rank_ref[0:cells, :], lanes)
    rank_ref[0:cells, :] = take(back, listed)


def assemble(j_ref, sort_ref, below, above, side_ref, shift, open_ends):
    fields, flow_rows, cells, _ = sort_ref.shape

    def keep(c, value, here):
        if open_ends is None or c != 2:
            return value
        return jnp.where(here, value, nowhere)

    for c in range(fields):
        for f in range(flow_rows):
            j_ref[c, 1 + f, 8 : 8 + cells, :] = sort_ref[c, f]
        ends = open_ends or (True,) * 4
        j_ref[c, 0, 8 : 8 + cells, :] = keep(c, below(c), ends[0])
        j_ref[c, 1 + flow_rows, 8 : 8 + cells, :] = keep(c, above(c), ends[1])
        for f in range(flow_rows + 2):
            inside_left, inside_right = ends[2], ends[3]
            if open_ends is not None and f == 0:
                inside_left, inside_right = ends[2] & ends[0], ends[3] & ends[0]
            if open_ends is not None and f == flow_rows + 1:
                inside_left, inside_right = ends[2] & ends[1], ends[3] & ends[1]
            part = 1 if f == 0 else 2 if f == flow_rows + 1 else 0
            row = shift + (flow_rows - 1 if f == 0 else 0 if f == flow_rows + 1 else f - 1)
            j_ref[c, f, 7:8, :] = keep(c, side_ref[part, c, row : row + 1, :], inside_left)
            j_ref[c, f, 8 + cells : 9 + cells, :] = keep(
                c, side_ref[3 + part, c, row : row + 1, :], inside_right
            )


def search(j_ref, f, cells, i_ref, base_ref, count_ref, held_ref, reach_ref, combo0):
    at = f * cells
    low = i_ref[2 * SHARE, at : at + cells, :]
    high = jnp.full((cells, LANES), -nowhere, jnp.float32)
    for v in range(SHARE):
        height = i_ref[2 * SHARE + v, at : at + cells, :]
        high = jnp.maximum(high, jnp.where(height < 500.0, height, -nowhere))
    used = low < 500.0
    low = jnp.where(used, low - reach, 0.0)
    high = jnp.where(used, high + reach, 0.0)
    below = low < 0.0
    above = high >= box_height
    low = jnp.where(below, low + box_height, low)
    high = jnp.where(above, high - box_height, high)
    low_bin = jnp.clip((low * table_rate).astype(jnp.int32), 0, LANES - 1)
    high_bin = jnp.floor(high * table_rate).astype(jnp.int32) + 1
    high_in = jnp.clip(high_bin, 0, LANES - 1)
    quarter = lane_iota(cells) // CLASSES
    most = jnp.zeros((cells, LANES), jnp.int32)
    for nb in range(9):
        df, dt = nb // 3, nb % 3
        heights = j_ref[2, f + df, 7 + dt : 7 + dt + cells, :]
        table = j_ref[7, f + df, 7 + dt : 7 + dt + cells, :]
        held = held_ref[f + df, 7 + dt : 7 + dt + cells, :]
        first = take(table, low_bin).astype(jnp.int32)
        step = (first < LANES - 1) & (take(heights, jnp.minimum(first + 1, LANES - 1)) < low)
        first = jnp.where(step, first + 2, first)
        step = (first < LANES) & (take(heights, jnp.minimum(first, LANES - 1)) < low)
        first = jnp.where(step, first + 1, first)
        last = jnp.where(high_bin >= LANES, held, take(table, high_in).astype(jnp.int32))
        step = (last >= 2) & (take(heights, jnp.maximum(last - 2, 0)) > high)
        last = jnp.where(step, last - 2, last)
        step = (last >= 1) & (take(heights, jnp.maximum(last - 1, 0)) > high)
        last = jnp.where(step, last - 1, last)
        first = jnp.where(below, first - held, first)
        last = jnp.where(above, last + held, last)
        count = jnp.where(used, last - first, 0)
        most = jnp.maximum(most, count)
        base_ref[combo0 + nb, at : at + cells, :] = first + quarter
        count_ref[combo0 + nb, at : at + cells, :] = count - quarter
    reach_ref[at : at + cells, :] = most


def pair_sums(j_ref, f, r0, i_ref, i0, base_ref, count_ref, held_ref, steps):
    beads = [[i_ref[c * SHARE + v, pl.ds(i0, 8), :] for c in range(7)] for v in range(SHARE)]

    def body(t, sums):
        sums = list(sums)
        k = t * SHARE
        for nb in range(9):
            df, dt = nb // 3, nb % 3
            rows = pl.ds(r0 + (7 + dt), 8)
            held = held_ref[f + df, rows, :]
            at = base_ref[nb, pl.ds(i0, 8), :] + k
            under, over = at < 0, at >= held
            lanes = (at + jnp.where(under, held, jnp.where(over, -held, 0))) & (LANES - 1)
            turn = jnp.where(under, -box_height, jnp.where(over, box_height, 0.0))
            turn = jnp.where(count_ref[nb, pl.ds(i0, 8), :] > k, turn, 10.0 * nowhere)
            other = [take(j_ref[c, f + df, rows, :], lanes) for c in range(7)]
            if df != 1:
                other[0] = other[0] + (df - 1.0)
            if dt != 1:
                other[1] = other[1] + (dt - 1.0)
            other[2] = other[2] + turn
            for v in range(SHARE):
                own = beads[v]
                dx, dy, dz = own[0] - other[0], own[1] - other[1], own[2] - other[2]
                dist_sq = dx * dx + dy * dy + dz * dz
                if nb == 4:
                    dist_sq = jnp.maximum(dist_sq, 1e-30)
                weight = jnp.maximum(lax.rsqrt(dist_sq) - 1.0, 0.0)
                along = ((own[3] - other[3]) * dx + (own[4] - other[4]) * dy
                         + (own[5] - other[5]) * dz)
                ratio = own[6] * other[6]
                noise = (ratio + noise_lift) - jnp.round(ratio - hash_shift)
                scalar = weight * (noise - weight * along)
                sums[v] = sums[v] + scalar * dx
                sums[SHARE + v] = sums[SHARE + v] + scalar * dy
                sums[2 * SHARE + v] = sums[2 * SHARE + v] + scalar * dz
        return tuple(sums)

    zero = jnp.zeros((8, LANES), jnp.float32)
    return lax.fori_loop(0, steps, body, (zero,) * (3 * SHARE))


def unsorted_sums(sums, rank):
    lanes = rank // SHARE
    which = rank % SHARE
    out = []
    for c in range(3):
        total = None
        for v in range(SHARE):
            part = sums[c * SHARE + v]
            part = part + pltpu.roll(part, LANES // 2, 1)
            part = part + pltpu.roll(part, LANES // 4, 1)
            part = take(part, lanes)
            total = part if total is None else jnp.where(which == v, part, total)
        out.append(noise_slope * total)
    return out


def arrange(i_ref, j_ref, f, cells, at):
    lane = lane_iota(cells) % CLASSES
    for v in range(SHARE):
        lanes = lane * SHARE + v
        for c in range(7):
            field = take(j_ref[c, 1 + f, 8 : 8 + cells, :], lanes)
            if c == 6:
                field = jnp.round(field * seed_modulus)
            i_ref[c * SHARE + v, at : at + cells, :] = field


def force_kernel(end_ref, share_ref, place_ref, count_ref, coef_ref, got_ref,
                 msort_ref, psort_ref, mraw_in, praw_ref, mrank_in, prank_ref,
                 below_ref, above_ref, side_ref, bin_ref,
                 mpos_out, mvel_out, mforce_out, ppos_out, pvel_out, pforce_out,
                 mj_ref, pj_ref, mi_ref, pi_ref, mbase_ref, mcount_ref, pbase_ref, pcount_ref,
                 mheld_ref, pheld_ref, mreach_ref, preach_ref, steps_ref,
                 mraw_ref, mrank_ref, push_ref):
    flow_rows, cells = msort_ref.shape[1], msort_ref.shape[2]
    prec_cells = psort_ref.shape[2]
    ends = tuple(end_ref[e] > 0 for e in range(4))
    assemble(mj_ref, msort_ref, lambda c: below_ref[c, 0:cells, :], lambda c: above_ref[c, 0:cells, :],
             side_ref, 0, ends)
    assemble(pj_ref, psort_ref, lambda c: below_ref[c, cells : cells + prec_cells, :],
             lambda c: above_ref[c, cells : cells + prec_cells, :], side_ref,
             flow_rows, None)
    mraw_ref[...] = mraw_in[...]
    mrank_ref[...] = mrank_in[...]

    @pl.when(end_ref[0] == 0)
    def _():
        arrivals(end_ref[4], place_ref, got_ref, count_ref, mj_ref, mraw_ref, mrank_ref)

    profile = jnp.sum(got_ref[:, 2:3, :], axis=0)[:, 0:BINS]
    push_ref[...] = jnp.zeros(push_ref.shape, jnp.float32)
    push_ref[:, 0:BINS] = jnp.broadcast_to(-coef_ref[...] * (profile * share_ref[0]), (8, BINS))
    push_row = push_ref[...]
    for j_ref, held_ref, n in ((mj_ref, mheld_ref, cells), (pj_ref, pheld_ref, prec_cells)):
        for f in range(held_ref.shape[0]):
            real = (j_ref[2, f, 0 : n + 16, :] < 500.0).astype(jnp.float32)
            held = jnp.sum(real, axis=1, keepdims=True).astype(jnp.int32)
            held_ref[f] = jnp.broadcast_to(held, (n + 16, LANES))
    for f in range(flow_rows):
        arrange(mi_ref, mj_ref, f, cells, f * cells)
    arrange(pi_ref, pj_ref, 0, prec_cells, 0)
    for f in range(flow_rows):
        search(mj_ref, f, cells, mi_ref, mbase_ref, mcount_ref, mheld_ref, mreach_ref, 0)
    search(pj_ref, 0, prec_cells, pi_ref, pbase_ref, pcount_ref, pheld_ref, preach_ref, 0)
    groups = flow_rows * cells // 8
    prec_groups = prec_cells // 8
    for g in range(groups):
        steps_ref[g] = (jnp.max(mreach_ref[8 * g : 8 * g + 8, :]) + (SHARE - 1)) // SHARE
    for g in range(prec_groups):
        steps_ref[groups + g] = (jnp.max(preach_ref[8 * g : 8 * g + 8, :]) + (SHARE - 1)) // SHARE

    def main_group(g, carry):
        f = g // (cells // 8)
        r0 = pl.multiple_of((g % (cells // 8)) * 8, 8)
        i0 = pl.multiple_of(g * 8, 8)
        sums = pair_sums(mj_ref, f, r0, mi_ref, i0, mbase_ref, mcount_ref, mheld_ref, steps_ref[g])
        force = unsorted_sums(sums, mrank_ref[pl.ds(i0, 8), :])
        occupied = mraw_ref[6, pl.ds(i0, 8), :] >= 0.0
        push = take(push_row, bin_ref[pl.ds(r0, 8), :])
        force[0] = force[0] + push * (f == flow_rows - 1).astype(jnp.float32)
        for c in range(3):
            half = mraw_ref[3 + c, pl.ds(i0, 8), :]
            mforce_out[f, c, pl.ds(r0, 8), :] = jnp.where(occupied, force[c], 0.0)
            mvel_out[f, c, pl.ds(r0, 8), :] = jnp.where(
                occupied, half + 0.5 * time_step * force[c], 0.0
            )
            mpos_out[f, c, pl.ds(r0, 8), :] = jnp.where(
                occupied, mraw_ref[c, pl.ds(i0, 8), :], 0.0
            )
        return carry

    def prec_group(g, carry):
        r0 = pl.multiple_of(g * 8, 8)
        sums = pair_sums(pj_ref, 0, r0, pi_ref, r0, pbase_ref, pcount_ref, pheld_ref,
                         steps_ref[groups + g])
        force = unsorted_sums(sums, prank_ref[pl.ds(r0, 8), :])
        for c in range(3):
            half = praw_ref[3 + c, pl.ds(r0, 8), :]
            pforce_out[0, c, pl.ds(r0, 8), :] = force[c]
            pvel_out[0, c, pl.ds(r0, 8), :] = half + 0.5 * time_step * force[c]
            ppos_out[0, c, pl.ds(r0, 8), :] = praw_ref[c, pl.ds(r0, 8), :]
        return carry

    lax.fori_loop(0, prec_groups, prec_group, 0)
    lax.fori_loop(0, groups, main_group, 0)


def whole(space, n):
    return [pl.BlockSpec(memory_space=space)] * n


def shape(dims, dtype=jnp.float32):
    return jax.ShapeDtypeStruct(dims, dtype)


def scratches(flow_rows, cells, prec_cells):
    total = flow_rows * cells
    return [
        VMEM((8, flow_rows + 2, cells + 16, LANES), jnp.float32),
        VMEM((8, 3, prec_cells + 16, LANES), jnp.float32),
        VMEM((7 * SHARE, total, LANES), jnp.float32),
        VMEM((7 * SHARE, prec_cells, LANES), jnp.float32),
        VMEM((9, total, LANES), jnp.int32),
        VMEM((9, total, LANES), jnp.int32),
        VMEM((9, prec_cells, LANES), jnp.int32),
        VMEM((9, prec_cells, LANES), jnp.int32),
        VMEM((flow_rows + 2, cells + 16, LANES), jnp.int32),
        VMEM((3, prec_cells + 16, LANES), jnp.int32),
        VMEM((total, LANES), jnp.int32),
        VMEM((prec_cells, LANES), jnp.int32),
        SMEM((total // 8 + prec_cells // 8,), jnp.int32),
        VMEM((7, total, LANES), jnp.float32),
        VMEM((total, LANES), jnp.int32),
        VMEM((8, LANES), jnp.float32),
    ]


def shards(
    main_pos,
    main_vel,
    main_force,
    main_seed,
    main_count,
    prec_pos,
    prec_vel,
    prec_force,
    prec_seed,
    cross_row,
    cross_dest,
    cross_cell,
    outlet_bin,
    outlet_coef,
):
    flow_rows, cells = main_seed.shape[0], main_seed.shape[1]
    prec_cells = prec_seed.shape[1]
    flow_index = lax.axis_index("flow")
    trans_index = lax.axis_index("trans")
    flow_devices = lax.axis_size("flow")
    trans_devices = lax.axis_size("trans")
    total = flow_rows * cells
    big = pltpu.CompilerParams(vmem_limit_bytes=63 << 20)

    def planes(value):
        return jnp.transpose(value, (0, 2, 1, 3))

    main_state = [planes(v) for v in (main_pos, main_vel, main_force)]
    prec_state = [planes(v) for v in (prec_pos, prec_vel, prec_force)]

    share = BINS / (cells * trans_devices * LANES)
    share = jnp.where(flow_index == flow_devices - 1, jnp.float32(share), 0.0)[None]

    own, psort, praw, prank = pl.pallas_call(
        prec_kernel,
        out_shape=(
            shape((8, LANES)),
            shape((8, 1, prec_cells, LANES)),
            shape((7, prec_cells, LANES)),
            shape((prec_cells, LANES), jnp.int32),
        ),
        in_specs=whole(SMEM, 3) + whole(VMEM, 6),
        out_specs=tuple(whole(VMEM, 4)),
        compiler_params=big,
        name="prec",
    )(cross_row, cross_dest, cross_cell, main_count, outlet_bin, *prec_state, prec_seed)
    msort, mraw, mrank, left, right = pl.pallas_call(
        main_kernel,
        out_shape=(
            shape((8, flow_rows, cells, LANES)),
            shape((7, total, LANES)),
            shape((total, LANES), jnp.int32),
            shape((8, 8, LANES)),
            shape((8, 8, LANES)),
        ),
        in_specs=whole(VMEM, 6),
        out_specs=tuple(whole(VMEM, 5)),
        compiler_params=big,
        name="main",
    )(main_count, *main_state, main_seed, psort)

    span = cells + prec_cells
    got, below, above, side = pl.pallas_call(
        link_kernel,
        out_shape=(shape((trans_devices, 8, LANES)), shape((8, span, LANES)),
                   shape((8, span, LANES)), shape((6, 8, 8, LANES))),
        in_specs=whole(VMEM, 1) + whole(pl.ANY, 4),
        out_specs=tuple(whole(VMEM, 1) + whole(pl.ANY, 3)),
        scratch_shapes=[pltpu.SemaphoreType.DMA((trans_devices,))] * 2
        + [pltpu.SemaphoreType.DMA((10,))] * 2,
        compiler_params=pltpu.CompilerParams(vmem_limit_bytes=63 << 20, collective_id=0,
                                             has_side_effects=True),
        name="link",
    )(own, msort, psort, left, right)
    ends = jnp.stack([
        flow_index > 0,
        flow_index < flow_devices - 1,
        trans_index > 0,
        trans_index < trans_devices - 1,
        trans_index * cells - 8,
    ]).astype(jnp.int32)

    out_main = shape((flow_rows, 3, cells, LANES))
    out_prec = shape((1, 3, prec_cells, LANES))
    outs = pl.pallas_call(
        force_kernel,
        out_shape=(out_main, out_main, out_main, out_prec, out_prec, out_prec),
        in_specs=whole(SMEM, 2) + whole(VMEM, 14),
        out_specs=tuple(whole(VMEM, 6)),
        scratch_shapes=scratches(flow_rows, cells, prec_cells),
        compiler_params=big,
        name="force",
    )(ends, share, got[:, 1, 32:48].reshape(-1, LANES).astype(jnp.int32), main_count,
      outlet_coef[None], got,
      msort, psort, mraw, praw, mrank, prank, below, above, side, outlet_bin)
    return tuple(planes(v) for v in outs)


def solution(mesh):
    return jax.shard_map(
        shards,
        mesh=mesh,
        in_specs=(
            P("flow", "trans", None, None),
            P("flow", "trans", None, None),
            P("flow", "trans", None, None),
            P("flow", "trans", None),
            P("flow", "trans"),
            P("flow", "trans", None, None),
            P("flow", "trans", None, None),
            P("flow", "trans", None, None),
            P("flow", "trans", None),
            P("trans"),
            P("trans"),
            P("trans"),
            P("trans", None),
            P(),
        ),
        out_specs=(
            P("flow", "trans", None, None),
            P("flow", "trans", None, None),
            P("flow", "trans", None, None),
            P("flow", "trans", None, None),
            P("flow", "trans", None, None),
            P("flow", "trans", None, None),
        ),
        check_vma=False,
    )
```

```python
import functools

import jax
import jax.numpy as jnp
from jax import lax
from jax.experimental import pallas as pl
from jax.experimental.pallas import tpu as pltpu
from jax.sharding import PartitionSpec as P

BINS = 64
LANES = 128
SHARE = 4
CLASSES = LANES // SHARE

time_step = 0.01
repulsion = 25.0
friction = 4.5
noise_amp = 30.0
box_height = 16.0
seed_modulus = 4093
unit_spread = 3.4641016151377544

reach = 1.0005
nowhere = 1000.0
table_rate = 8.0
hash_shift = 2047.0 / 4093.0
noise_slope = noise_amp * unit_spread
drag = friction / noise_slope
noise_lift = repulsion / noise_slope - 0.5 / 4093.0 - hash_shift

VMEM = pltpu.VMEM
SMEM = pltpu.SMEM


def take(rows, lanes):
    return jnp.take_along_axis(rows, lanes, axis=1, mode="promise_in_bounds")


def lane_iota(rows):
    return lax.broadcasted_iota(jnp.int32, (rows, LANES), 1)


def column_of(row):
    n = row.shape[1]
    here = (lax.broadcasted_iota(jnp.int32, (n, n), 0) == lax.broadcasted_iota(jnp.int32, (n, n), 1))
    wide = jnp.where(here, jnp.broadcast_to(row.astype(jnp.float32), (n, n)), 0.0)
    return jnp.sum(wide, axis=1, keepdims=True).astype(jnp.int32)


def centred(seed):
    code = seed + 1
    code = jnp.where(code > 2046, code - seed_modulus, code)
    return jnp.where(code > 2046, code - seed_modulus, code)


def first_tile(row_ref, dest_ref, cell_ref, last_count, arrays, seed_ref, bin_ref, out_ref):
    rows = row_ref.shape[0]
    lane = lane_iota(1)
    lines = [jnp.zeros((1, LANES), jnp.float32) for _ in range(2)]

    def put(field, q, value):
        at = field * rows + q
        lines[at // LANES] = jnp.where(lane == at % LANES, value, lines[at // LANES])

    for q in range(rows):
        cell = row_ref[q] // LANES
        slot = row_ref[q] % LANES
        hit = lane == slot
        for a, ref in enumerate(arrays):
            for c in range(3):
                value = jnp.where(hit, ref[0, c, pl.ds(cell, 1), :], 0.0)
                put(3 * a + c, q, jnp.sum(value, axis=1, keepdims=True))
        seed = jnp.where(hit, seed_ref[0, pl.ds(cell, 1), :].astype(jnp.float32), 0.0)
        put(9, q, jnp.sum(seed, axis=1, keepdims=True))
        place = dest_ref[q] * bin_ref.shape[0] + cell_ref[q]
        put(10, q, place.astype(jnp.float32))
    cells = bin_ref.shape[0]
    bins = jnp.where(lane_iota(cells) < last_count, bin_ref[...], BINS)
    profile = jnp.zeros((1, LANES), jnp.float32)
    for b in range(BINS):
        hits = jnp.sum((bins == b).astype(jnp.float32), axis=0, keepdims=True)
        profile = jnp.where(lane == b, jnp.sum(hits, axis=1, keepdims=True), profile)
    out_ref[...] = jnp.zeros(out_ref.shape, jnp.float32)
    out_ref[0:1, :] = lines[0]
    out_ref[1:2, :] = lines[1]
    out_ref[2:3, :] = profile


def link_kernel(own_ref, msort_ref, psort_ref, left_ref, right_ref,
                got_ref, below_ref, above_ref, side_ref,
                tile_send, tile_recv, send_sem, recv_sem):
    flow, trans = lax.axis_index("flow"), lax.axis_index("trans")
    flows, count = lax.axis_size("flow"), got_ref.shape[0]
    flow_rows, cells = msort_ref.shape[1], msort_ref.shape[2]
    prec_cells = psort_ref.shape[2]

    def at(df, dt):
        return (lax.rem(flow + flows + df, flows), lax.rem(trans + count + dt, count))

    mesh_id = pl.DeviceIdType.MESH
    barrier = pltpu.get_barrier_semaphore()
    across = [(df, dt) for df in (-1, 1) for dt in (-1, 0, 1)]
    for df, dt in across:
        pl.semaphore_signal(barrier, inc=1, device_id=at(df, dt), device_id_type=mesh_id)

    for dt in (-1, 1):
        pl.semaphore_signal(barrier, inc=1, device_id=at(0, dt), device_id_type=mesh_id)
    inner = 8
    outer = count // inner
    high, low = trans // inner, lax.rem(trans, inner)
    meets = (flow == 0) | (flow == flows - 1)

    def near(s):
        return high * inner + lax.rem(low + inner + s, inner)

    def far(s):
        return lax.rem(high + outer + s, outer)

    @pl.when(meets)
    def _():
        for s in range(1, inner):
            pl.semaphore_signal(barrier, inc=1, device_id=(flow, near(s)), device_id_type=mesh_id)
        for s in range(1, outer):
            pl.semaphore_signal(barrier, inc=1, device_id=(flow, far(s) * inner + low),
                                device_id_type=mesh_id)

    pl.semaphore_wait(barrier, len(across) + 2 + jnp.where(meets, inner + outer - 2, 0))
    main_part, prec_part = pl.ds(0, cells), pl.ds(cells, prec_cells)
    plan = [
        (msort_ref.at[:, flow_rows - 1], below_ref.at[:, main_part], (1, 0)),
        (msort_ref.at[:, 0], above_ref.at[:, main_part], (-1, 0)),
        (psort_ref.at[:, 0], below_ref.at[:, prec_part], (1, 0)),
        (psort_ref.at[:, 0], above_ref.at[:, prec_part], (-1, 0)),
        (right_ref, side_ref.at[0], (0, 1)),
        (right_ref, side_ref.at[1], (1, 1)),
        (right_ref, side_ref.at[2], (-1, 1)),
        (left_ref, side_ref.at[3], (0, -1)),
        (left_ref, side_ref.at[4], (1, -1)),
        (left_ref, side_ref.at[5], (-1, -1)),
    ]
    copies = [
        pltpu.make_async_remote_copy(src_ref=src, dst_ref=dst, send_sem=send_sem.at[n],
                                     recv_sem=recv_sem.at[n], device_id=at(*step),
                                     device_id_type=mesh_id)
        for n, (src, dst, step) in enumerate(plan)
    ]
    def tile(s, slot):
        return pltpu.make_async_remote_copy(
            src_ref=own_ref, dst_ref=got_ref.at[slot], send_sem=tile_send.at[s],
            recv_sem=tile_recv.at[lax.rem(slot, inner)], device_id=(flow, near(s)),
            device_id_type=mesh_id)

    def block(s, part):
        rows = pl.ds(part * inner, inner)
        return pltpu.make_async_remote_copy(
            src_ref=got_ref.at[rows], dst_ref=got_ref.at[rows], send_sem=tile_send.at[inner + s],
            recv_sem=tile_recv.at[inner + part], device_id=(flow, far(s) * inner + low),
            device_id_type=mesh_id)

    @pl.when(meets)
    def _():
        for s in range(1, inner):
            tile(s, trans).start()

    for copy in copies:
        copy.start()

    @pl.when(meets)
    def _():
        got_ref[trans] = own_ref[...]
        for s in range(1, inner):
            tile(s, near(-s)).wait_recv()
        for s in range(1, outer):
            block(s, high).start()
        for s in range(1, outer):
            block(s, far(-s)).wait_recv()
        for s in range(1, inner):
            tile(s, trans).wait_send()
        for s in range(1, outer):
            block(s, high).wait_send()

    @pl.when(jnp.logical_not(meets))
    def _():
        got_ref[...] = jnp.zeros(got_ref.shape, jnp.float32)

    for copy in copies:
        copy.wait()


def sorted_keys(key):
    rows = key.shape[0]
    lane = lane_iota(rows)
    size = 2
    while size <= LANES:
        dist = size // 2
        while dist >= 1:
            low = ((lane & size) == 0) == ((lane & dist) == 0)
            other = take(key, lane ^ dist)
            key = jnp.where(low, jnp.minimum(key, other), jnp.maximum(key, other))
            dist //= 2
        size *= 2
    return key


def height_keys(height):
    level = jnp.minimum(height, 16.25) * float(1 << 19)
    return level.astype(jnp.int32) * LANES + lane_iota(height.shape[0])


def first_at_least(sorted_rows, bound, rows):
    at = jnp.zeros((rows, LANES), jnp.int32)
    step = LANES // 2
    while step >= 1:
        below = take(sorted_rows, at + (step - 1)) < bound
        at = jnp.where(below, at + step, at)
        step //= 2
    return jnp.where(take(sorted_rows, at) < bound, at + 1, at)


def sort_state(pos_ref, vel_ref, force_ref, seeds, sort_ref, rank_ref, raw_out):
    flow_rows, rows = len(seeds), seeds[0].shape[0]
    fields, keys = [], []
    for f, seed in enumerate(seeds):
        at = f * rows
        occupied = seed >= 0
        half = [vel_ref[f, c] + 0.5 * time_step * force_ref[f, c] for c in range(3)]
        moved = [pos_ref[f, c] + time_step * half[c] for c in range(3)]
        for c in range(3):
            raw_out[c, at : at + rows, :] = moved[c]
            raw_out[3 + c, at : at + rows, :] = half[c]
        raw_out[6, at : at + rows, :] = seed.astype(jnp.float32)
        height = moved[2] - box_height * jnp.floor(moved[2] * (1.0 / box_height))
        height = jnp.where(occupied, height, nowhere)
        hashed = centred(seed).astype(jnp.float32) / seed_modulus
        fields.append([jnp.where(occupied, v, 0.0) if c != 2 else height for c, v in enumerate(
            moved[0:2] + [height] + [drag * v for v in half] + [hashed])])
        keys.append(height_keys(height))
    key = jnp.concatenate(keys, axis=0)
    total = flow_rows * rows
    ordered = sorted_keys(key)
    order = ordered & (LANES - 1)
    rank_ref[...] = first_at_least(ordered, key, total)
    for c in range(7):
        field = take(jnp.concatenate([v[c] for v in fields], axis=0), order)
        if c == 2:
            starts = starts_of(field)
        for f in range(flow_rows):
            sort_ref[c, f] = field[f * rows : (f + 1) * rows]
    for f in range(flow_rows):
        sort_ref[7, f] = starts[f * rows : (f + 1) * rows]


def prec_kernel(row_ref, dest_ref, cell_ref, count_ref, bin_ref, pos_ref, vel_ref, force_ref,
                seed_ref, own_ref, sort_ref, raw_ref, rank_ref):
    last = count_ref.shape[0] - 1
    first_tile(row_ref, dest_ref, cell_ref, column_of(count_ref[last : last + 1, :]),
               (pos_ref, vel_ref, force_ref), seed_ref, bin_ref, own_ref)
    sort_state(pos_ref, vel_ref, force_ref, [seed_ref[0]], sort_ref, rank_ref, raw_ref)


def main_kernel(count_ref, pos_ref, vel_ref, force_ref, seed_ref, psort_ref,
                msort_ref, raw_ref, rank_ref, left_ref, right_ref):
    flow_rows, cells = seed_ref.shape[0], seed_ref.shape[1]
    prec_cells = psort_ref.shape[2]
    seeds = [
        jnp.where(lane_iota(cells) < column_of(count_ref[f : f + 1, :]), seed_ref[f], -1)
        for f in range(flow_rows)
    ]
    sort_state(pos_ref, vel_ref, force_ref, seeds, msort_ref, rank_ref, raw_ref)
    left_ref[...] = jnp.zeros(left_ref.shape, jnp.float32)
    right_ref[...] = jnp.zeros(right_ref.shape, jnp.float32)
    for c in range(msort_ref.shape[0]):
        for f in range(flow_rows):
            left_ref[c, f : f + 1, :] = msort_ref[c, f, 0:1, :]
            right_ref[c, f : f + 1, :] = msort_ref[c, f, cells - 1 : cells, :]
        left_ref[c, flow_rows : flow_rows + 1, :] = psort_ref[c, 0, 0:1, :]
        right_ref[c, flow_rows : flow_rows + 1, :] = psort_ref[c, 0, prec_cells - 1 : prec_cells, :]


def starts_of(height):
    edges = lane_iota(height.shape[0]).astype(jnp.float32) * (1.0 / table_rate)
    return first_at_least(height, edges, height.shape[0]).astype(jnp.float32)


def arrivals(first, got_ref, count_ref, j_ref, raw_ref, rank_ref):
    cells = count_ref.shape[1]
    per = 16
    rows = j_ref.shape[2]
    row = lax.broadcasted_iota(jnp.int32, (rows, LANES), 0)
    order_of = lax.broadcasted_iota(jnp.int32, (LANES, LANES), 0)
    upto = (order_of <= lane_iota(LANES)).astype(jnp.float32)
    held = jnp.sum((j_ref[2, 1] < 500.0).astype(jnp.float32), axis=1, keepdims=True)
    turn = lane_iota(rows).astype(jnp.float32) - held + 1.0
    before = jnp.zeros((rows, 1), jnp.float32)
    came = jnp.zeros((rows, LANES), jnp.int32)
    lane8 = lane_iota(8)
    mine = lane8 // per == lax.broadcasted_iota(jnp.int32, (8, LANES), 0)
    blocks = got_ref.shape[0] * per // LANES

    def line_of(c, a):
        line = take(got_ref[8 * a : 8 * a + 8, c // 8, :], lane8 % per + (c % 8) * per)
        return jnp.sum(jnp.where(mine, line, 0.0), axis=0, keepdims=True)

    for a in range(blocks):
        match = (line_of(10, a).astype(jnp.int32) - first == row).astype(jnp.float32)
        seen = jnp.dot(match, upto, preferred_element_type=jnp.float32) + before
        before = seen[:, LANES - 1 : LANES]
        came = came + first_at_least(seen, turn, rows)
    came = jnp.where((turn >= 1.0) & (turn <= before), came, -1)
    here = came >= 0
    block, at = came // LANES, came & (LANES - 1)
    state = []
    for c in range(10):
        value = jnp.zeros((rows, LANES), jnp.float32)
        for a in range(blocks):
            line = line_of(c, a)
            part = take(jnp.broadcast_to(line, (rows, LANES)), at)
            value = jnp.where(block == a, part, value)
        state.append(value)
    half = [state[3 + c] + 0.5 * time_step * state[6 + c] for c in range(3)]
    moved = [state[c] + time_step * half[c] for c in range(3)]
    height = moved[2] - box_height * jnp.floor(moved[2] * (1.0 / box_height))
    hashed = centred(state[9].astype(jnp.int32)).astype(jnp.float32) / seed_modulus
    inner = slice(8, 8 + cells)
    for c, value in enumerate(moved + half + [state[9]]):
        raw_ref[c, 0:cells, :] = jnp.where(here[inner], value[inner], raw_ref[c, 0:cells, :])
    fields = [moved[0], moved[1], height] + [drag * v for v in half] + [hashed]
    fields = [jnp.where(here, fields[c], j_ref[c, 1]) for c in range(7)]
    key = height_keys(fields[2])
    ordered = sorted_keys(key)
    order = ordered & (LANES - 1)
    for c in range(7):
        j_ref[c, 1] = take(fields[c], order)
    j_ref[7, 1] = starts_of(j_ref[2, 1])
    back = first_at_least(ordered, key, rows)[inner]
    lanes = lane_iota(cells)
    listed = jnp.where(lanes < column_of(count_ref[0:1, :]), rank_ref[0:cells, :], lanes)
    rank_ref[0:cells, :] = take(back, listed)


def assemble(j_ref, sort_ref, below, above, side_ref, shift, open_ends):
    fields, flow_rows, cells, _ = sort_ref.shape

    def keep(c, value, here):
        if open_ends is None or c != 2:
            return value
        return jnp.where(here, value, nowhere)

    for c in range(fields):
        for f in range(flow_rows):
            j_ref[c, 1 + f, 8 : 8 + cells, :] = sort_ref[c, f]
        ends = open_ends or (True,) * 4
        j_ref[c, 0, 8 : 8 + cells, :] = keep(c, below(c), ends[0])
        j_ref[c, 1 + flow_rows, 8 : 8 + cells, :] = keep(c, above(c), ends[1])
        for f in range(flow_rows + 2):
            inside_left, inside_right = ends[2], ends[3]
            if open_ends is not None and f == 0:
                inside_left, inside_right = ends[2] & ends[0], ends[3] & ends[0]
            if open_ends is not None and f == flow_rows + 1:
                inside_left, inside_right = ends[2] & ends[1], ends[3] & ends[1]
            part = 1 if f == 0 else 2 if f == flow_rows + 1 else 0
            row = shift + (flow_rows - 1 if f == 0 else 0 if f == flow_rows + 1 else f - 1)
            j_ref[c, f, 7:8, :] = keep(c, side_ref[part, c, row : row + 1, :], inside_left)
            j_ref[c, f, 8 + cells : 9 + cells, :] = keep(
                c, side_ref[3 + part, c, row : row + 1, :], inside_right
            )


def search(j_ref, f, cells, i_ref, base_ref, count_ref, held_ref, reach_ref, combo0):
    at = f * cells
    low = i_ref[2 * SHARE, at : at + cells, :]
    high = jnp.full((cells, LANES), -nowhere, jnp.float32)
    for v in range(SHARE):
        height = i_ref[2 * SHARE + v, at : at + cells, :]
        high = jnp.maximum(high, jnp.where(height < 500.0, height, -nowhere))
    used = low < 500.0
    low = jnp.where(used, low - reach, 0.0)
    high = jnp.where(used, high + reach, 0.0)
    below = low < 0.0
    above = high >= box_height
    low = jnp.where(below, low + box_height, low)
    high = jnp.where(above, high - box_height, high)
    low_bin = jnp.clip((low * table_rate).astype(jnp.int32), 0, LANES - 1)
    high_bin = jnp.floor(high * table_rate).astype(jnp.int32) + 1
    high_in = jnp.clip(high_bin, 0, LANES - 1)
    quarter = lane_iota(cells) // CLASSES
    most = jnp.zeros((cells, LANES), jnp.int32)
    for nb in range(9):
        df, dt = nb // 3, nb % 3
        heights = j_ref[2, f + df, 7 + dt : 7 + dt + cells, :]
        table = j_ref[7, f + df, 7 + dt : 7 + dt + cells, :]
        held = held_ref[f + df, 7 + dt : 7 + dt + cells, :]
        first = take(table, low_bin).astype(jnp.int32)
        step = (first < LANES - 1) & (take(heights, jnp.minimum(first + 1, LANES - 1)) < low)
        first = jnp.where(step, first + 2, first)
        step = (first < LANES) & (take(heights, jnp.minimum(first, LANES - 1)) < low)
        first = jnp.where(step, first + 1, first)
        last = jnp.where(high_bin >= LANES, held, take(table, high_in).astype(jnp.int32))
        step = (last >= 2) & (take(heights, jnp.maximum(last - 2, 0)) > high)
        last = jnp.where(step, last - 2, last)
        step = (last >= 1) & (take(heights, jnp.maximum(last - 1, 0)) > high)
        last = jnp.where(step, last - 1, last)
        first = jnp.where(below, first - held, first)
        last = jnp.where(above, last + held, last)
        count = jnp.where(used, last - first, 0)
        most = jnp.maximum(most, count)
        base_ref[combo0 + nb, at : at + cells, :] = first + quarter
        count_ref[combo0 + nb, at : at + cells, :] = count - quarter
    reach_ref[at : at + cells, :] = most


def pair_sums(j_ref, f, r0, i_ref, i0, base_ref, count_ref, held_ref, steps):
    beads = [[i_ref[c * SHARE + v, pl.ds(i0, 8), :] for c in range(7)] for v in range(SHARE)]

    def body(t, sums):
        sums = list(sums)
        k = t * SHARE
        for nb in range(9):
            df, dt = nb // 3, nb % 3
            rows = pl.ds(r0 + (7 + dt), 8)
            held = held_ref[f + df, rows, :]
            at = base_ref[nb, pl.ds(i0, 8), :] + k
            under, over = at < 0, at >= held
            lanes = (at + jnp.where(under, held, jnp.where(over, -held, 0))) & (LANES - 1)
            turn = jnp.where(under, -box_height, jnp.where(over, box_height, 0.0))
            turn = jnp.where(count_ref[nb, pl.ds(i0, 8), :] > k, turn, 10.0 * nowhere)
            other = [take(j_ref[c, f + df, rows, :], lanes) for c in range(7)]
            if df != 1:
                other[0] = other[0] + (df - 1.0)
            if dt != 1:
                other[1] = other[1] + (dt - 1.0)
            other[2] = other[2] + turn
            for v in range(SHARE):
                own = beads[v]
                dx, dy, dz = own[0] - other[0], own[1] - other[1], own[2] - other[2]
                dist_sq = dx * dx + dy * dy + dz * dz
                if nb == 4:
                    dist_sq = jnp.maximum(dist_sq, 1e-30)
                weight = jnp.maximum(lax.rsqrt(dist_sq) - 1.0, 0.0)
                along = ((own[3] - other[3]) * dx + (own[4] - other[4]) * dy
                         + (own[5] - other[5]) * dz)
                ratio = own[6] * other[6]
                noise = (ratio + noise_lift) - jnp.round(ratio - hash_shift)
                scalar = weight * (noise - weight * along)
                sums[v] = sums[v] + scalar * dx
                sums[SHARE + v] = sums[SHARE + v] + scalar * dy
                sums[2 * SHARE + v] = sums[2 * SHARE + v] + scalar * dz
        return tuple(sums)

    zero = jnp.zeros((8, LANES), jnp.float32)
    return lax.fori_loop(0, steps, body, (zero,) * (3 * SHARE))


def unsorted_sums(sums, rank):
    lanes = rank // SHARE
    which = rank % SHARE
    out = []
    for c in range(3):
        total = None
        for v in range(SHARE):
            part = sums[c * SHARE + v]
            part = part + pltpu.roll(part, LANES // 2, 1)
            part = part + pltpu.roll(part, LANES // 4, 1)
            part = take(part, lanes)
            total = part if total is None else jnp.where(which == v, part, total)
        out.append(noise_slope * total)
    return out


def arrange(i_ref, j_ref, f, cells, at):
    lane = lane_iota(cells) % CLASSES
    for v in range(SHARE):
        lanes = lane * SHARE + v
        for c in range(7):
            field = take(j_ref[c, 1 + f, 8 : 8 + cells, :], lanes)
            if c == 6:
                field = jnp.round(field * seed_modulus)
            i_ref[c * SHARE + v, at : at + cells, :] = field


def force_kernel(share, count_ref, coef_ref, got_ref,
                 msort_ref, psort_ref, mraw_in, praw_ref, mrank_in, prank_ref,
                 below_ref, above_ref, side_ref, bin_ref,
                 mpos_out, mvel_out, mforce_out, ppos_out, pvel_out, pforce_out,
                 mj_ref, pj_ref, mi_ref, pi_ref, mbase_ref, mcount_ref, pbase_ref, pcount_ref,
                 mheld_ref, pheld_ref, mreach_ref, preach_ref, steps_ref,
                 mraw_ref, mrank_ref, push_ref):
    flow_rows, cells = msort_ref.shape[1], msort_ref.shape[2]
    prec_cells = psort_ref.shape[2]
    flow, trans = lax.axis_index("flow"), lax.axis_index("trans")
    last_flow = flow == lax.axis_size("flow") - 1
    ends = (flow > 0, jnp.logical_not(last_flow), trans > 0, trans < lax.axis_size("trans") - 1)
    assemble(mj_ref, msort_ref, lambda c: below_ref[c, 0:cells, :], lambda c: above_ref[c, 0:cells, :],
             side_ref, 0, ends)
    assemble(pj_ref, psort_ref, lambda c: below_ref[c, cells : cells + prec_cells, :],
             lambda c: above_ref[c, cells : cells + prec_cells, :], side_ref,
             flow_rows, None)
    mraw_ref[...] = mraw_in[...]
    mrank_ref[...] = mrank_in[...]

    @pl.when(flow == 0)
    def _():
        arrivals(trans * cells - 8, got_ref, count_ref, mj_ref, mraw_ref, mrank_ref)

    profile = jnp.sum(got_ref[:, 2:3, :], axis=0)[:, 0:BINS]
    push_ref[...] = jnp.zeros(push_ref.shape, jnp.float32)
    push_ref[:, 0:BINS] = jnp.broadcast_to(-coef_ref[...] * (profile * jnp.where(last_flow, share, 0.0)), (8, BINS))
    push_row = push_ref[...]
    for j_ref, held_ref, n in ((mj_ref, mheld_ref, cells), (pj_ref, pheld_ref, prec_cells)):
        for f in range(held_ref.shape[0]):
            real = (j_ref[2, f, 0 : n + 16, :] < 500.0).astype(jnp.float32)
            held = jnp.sum(real, axis=1, keepdims=True).astype(jnp.int32)
            held_ref[f] = jnp.broadcast_to(held, (n + 16, LANES))
    for f in range(flow_rows):
        arrange(mi_ref, mj_ref, f, cells, f * cells)
    arrange(pi_ref, pj_ref, 0, prec_cells, 0)
    for f in range(flow_rows):
        search(mj_ref, f, cells, mi_ref, mbase_ref, mcount_ref, mheld_ref, mreach_ref, 0)
    search(pj_ref, 0, prec_cells, pi_ref, pbase_ref, pcount_ref, pheld_ref, preach_ref, 0)
    groups = flow_rows * cells // 8
    prec_groups = prec_cells // 8
    for g in range(groups):
        steps_ref[g] = (jnp.max(mreach_ref[8 * g : 8 * g + 8, :]) + (SHARE - 1)) // SHARE
    for g in range(prec_groups):
        steps_ref[groups + g] = (jnp.max(preach_ref[8 * g : 8 * g + 8, :]) + (SHARE - 1)) // SHARE

    def main_group(g, carry):
        f = g // (cells // 8)
        r0 = pl.multiple_of((g % (cells // 8)) * 8, 8)
        i0 = pl.multiple_of(g * 8, 8)
        sums = pair_sums(mj_ref, f, r0, mi_ref, i0, mbase_ref, mcount_ref, mheld_ref, steps_ref[g])
        force = unsorted_sums(sums, mrank_ref[pl.ds(i0, 8), :])
        occupied = mraw_ref[6, pl.ds(i0, 8), :] >= 0.0
        push = take(push_row, bin_ref[pl.ds(r0, 8), :])
        force[0] = force[0] + push * (f == flow_rows - 1).astype(jnp.float32)
        for c in range(3):
            half = mraw_ref[3 + c, pl.ds(i0, 8), :]
            mforce_out[f, c, pl.ds(r0, 8), :] = jnp.where(occupied, force[c], 0.0)
            mvel_out[f, c, pl.ds(r0, 8), :] = jnp.where(
                occupied, half + 0.5 * time_step * force[c], 0.0
            )
            mpos_out[f, c, pl.ds(r0, 8), :] = jnp.where(
                occupied, mraw_ref[c, pl.ds(i0, 8), :], 0.0
            )
        return carry

    def prec_group(g, carry):
        r0 = pl.multiple_of(g * 8, 8)
        sums = pair_sums(pj_ref, 0, r0, pi_ref, r0, pbase_ref, pcount_ref, pheld_ref,
                         steps_ref[groups + g])
        force = unsorted_sums(sums, prank_ref[pl.ds(r0, 8), :])
        for c in range(3):
            half = praw_ref[3 + c, pl.ds(r0, 8), :]
            pforce_out[0, c, pl.ds(r0, 8), :] = force[c]
            pvel_out[0, c, pl.ds(r0, 8), :] = half + 0.5 * time_step * force[c]
            ppos_out[0, c, pl.ds(r0, 8), :] = praw_ref[c, pl.ds(r0, 8), :]
        return carry

    lax.fori_loop(0, prec_groups, prec_group, 0)
    lax.fori_loop(0, groups, main_group, 0)


def whole(space, n):
    return [pl.BlockSpec(memory_space=space)] * n


def shape(dims, dtype=jnp.float32):
    return jax.ShapeDtypeStruct(dims, dtype)


def scratches(flow_rows, cells, prec_cells):
    total = flow_rows * cells
    return [
        VMEM((8, flow_rows + 2, cells + 16, LANES), jnp.float32),
        VMEM((8, 3, prec_cells + 16, LANES), jnp.float32),
        VMEM((7 * SHARE, total, LANES), jnp.float32),
        VMEM((7 * SHARE, prec_cells, LANES), jnp.float32),
        VMEM((9, total, LANES), jnp.int32),
        VMEM((9, total, LANES), jnp.int32),
        VMEM((9, prec_cells, LANES), jnp.int32),
        VMEM((9, prec_cells, LANES), jnp.int32),
        VMEM((flow_rows + 2, cells + 16, LANES), jnp.int32),
        VMEM((3, prec_cells + 16, LANES), jnp.int32),
        VMEM((total, LANES), jnp.int32),
        VMEM((prec_cells, LANES), jnp.int32),
        SMEM((total // 8 + prec_cells // 8,), jnp.int32),
        VMEM((7, total, LANES), jnp.float32),
        VMEM((total, LANES), jnp.int32),
        VMEM((8, LANES), jnp.float32),
    ]


def shards(
    main_pos,
    main_vel,
    main_force,
    main_seed,
    main_count,
    prec_pos,
    prec_vel,
    prec_force,
    prec_seed,
    cross_row,
    cross_dest,
    cross_cell,
    outlet_bin,
    outlet_coef,
):
    flow_rows, cells = main_seed.shape[0], main_seed.shape[1]
    prec_cells = prec_seed.shape[1]
    trans_devices = lax.axis_size("trans")
    total = flow_rows * cells
    big = pltpu.CompilerParams(vmem_limit_bytes=63 << 20)

    def planes(value):
        return jnp.transpose(value, (0, 2, 1, 3))

    main_state = [planes(v) for v in (main_pos, main_vel, main_force)]
    prec_state = [planes(v) for v in (prec_pos, prec_vel, prec_force)]

    share = BINS / (cells * trans_devices * LANES)

    own, psort, praw, prank = pl.pallas_call(
        prec_kernel,
        out_shape=(
            shape((8, LANES)),
            shape((8, 1, prec_cells, LANES)),
            shape((7, prec_cells, LANES)),
            shape((prec_cells, LANES), jnp.int32),
        ),
        in_specs=whole(SMEM, 3) + whole(VMEM, 6),
        out_specs=tuple(whole(VMEM, 4)),
        compiler_params=big,
        name="prec",
    )(cross_row, cross_dest, cross_cell, main_count, outlet_bin, *prec_state, prec_seed)
    msort, mraw, mrank, left, right = pl.pallas_call(
        main_kernel,
        out_shape=(
            shape((8, flow_rows, cells, LANES)),
            shape((7, total, LANES)),
            shape((total, LANES), jnp.int32),
            shape((8, 8, LANES)),
            shape((8, 8, LANES)),
        ),
        in_specs=whole(VMEM, 6),
        out_specs=tuple(whole(VMEM, 5)),
        compiler_params=big,
        name="main",
    )(main_count, *main_state, main_seed, psort)

    span = cells + prec_cells
    got, below, above, side = pl.pallas_call(
        link_kernel,
        out_shape=(shape((trans_devices, 8, LANES)), shape((8, span, LANES)),
                   shape((8, span, LANES)), shape((6, 8, 8, LANES))),
        in_specs=whole(VMEM, 1) + whole(pl.ANY, 4),
        out_specs=tuple(whole(VMEM, 1) + whole(pl.ANY, 3)),
        scratch_shapes=[pltpu.SemaphoreType.DMA((8 + trans_devices // 8,))] * 2
        + [pltpu.SemaphoreType.DMA((10,))] * 2,
        compiler_params=pltpu.CompilerParams(vmem_limit_bytes=63 << 20, collective_id=0,
                                             has_side_effects=True),
        name="link",
    )(own, msort, psort, left, right)
    out_main = shape((flow_rows, 3, cells, LANES))
    out_prec = shape((1, 3, prec_cells, LANES))
    outs = pl.pallas_call(
        functools.partial(force_kernel, share),
        out_shape=(out_main, out_main, out_main, out_prec, out_prec, out_prec),
        in_specs=whole(VMEM, 13),
        out_specs=tuple(whole(VMEM, 6)),
        scratch_shapes=scratches(flow_rows, cells, prec_cells),
        compiler_params=big,
        name="force",
    )(main_count, outlet_coef[None], got,
      msort, psort, mraw, praw, mrank, prank, below, above, side, outlet_bin)
    return tuple(planes(v) for v in outs)


def solution(mesh):
    return jax.shard_map(
        shards,
        mesh=mesh,
        in_specs=(
            P("flow", "trans", None, None),
            P("flow", "trans", None, None),
            P("flow", "trans", None, None),
            P("flow", "trans", None),
            P("flow", "trans"),
            P("flow", "trans", None, None),
            P("flow", "trans", None, None),
            P("flow", "trans", None, None),
            P("flow", "trans", None),
            P("trans"),
            P("trans"),
            P("trans"),
            P("trans", None),
            P(),
        ),
        out_specs=(
            P("flow", "trans", None, None),
            P("flow", "trans", None, None),
            P("flow", "trans", None, None),
            P("flow", "trans", None, None),
            P("flow", "trans", None, None),
            P("flow", "trans", None, None),
        ),
        check_vma=False,
    )
```

```python
import functools

import jax
import jax.numpy as jnp
from jax import lax
from jax.experimental import pallas as pl
from jax.experimental.pallas import tpu as pltpu
from jax.sharding import PartitionSpec as P

BINS = 64
LANES = 128
SHARE = 4
CLASSES = LANES // SHARE

time_step = 0.01
repulsion = 25.0
friction = 4.5
noise_amp = 30.0
box_height = 16.0
seed_modulus = 4093
unit_spread = 3.4641016151377544

reach = 1.0005
nowhere = 1000.0
table_rate = 8.0
hash_shift = 2047.0 / 4093.0
noise_slope = noise_amp * unit_spread
drag = friction / noise_slope
noise_lift = repulsion / noise_slope - 0.5 / 4093.0 - hash_shift

VMEM = pltpu.VMEM
SMEM = pltpu.SMEM


def take(rows, lanes):
    return jnp.take_along_axis(rows, lanes, axis=1, mode="promise_in_bounds")


def lane_iota(rows):
    return lax.broadcasted_iota(jnp.int32, (rows, LANES), 1)


def column_of(row):
    n = row.shape[1]
    here = (lax.broadcasted_iota(jnp.int32, (n, n), 0) == lax.broadcasted_iota(jnp.int32, (n, n), 1))
    wide = jnp.where(here, jnp.broadcast_to(row.astype(jnp.float32), (n, n)), 0.0)
    return jnp.sum(wide, axis=1, keepdims=True).astype(jnp.int32)


def centred(seed):
    code = seed + 1
    code = jnp.where(code > 2046, code - seed_modulus, code)
    return jnp.where(code > 2046, code - seed_modulus, code)


def first_tile(row_ref, dest_ref, cell_ref, last_count, arrays, seed_ref, bin_ref, out_ref):
    rows = row_ref.shape[0]
    lane = lane_iota(1)
    lines = [jnp.zeros((1, LANES), jnp.float32) for _ in range(2)]

    def put(field, q, value):
        at = field * rows + q
        lines[at // LANES] = jnp.where(lane == at % LANES, value, lines[at // LANES])

    for q in range(rows):
        cell = row_ref[q] // LANES
        slot = row_ref[q] % LANES
        hit = lane == slot
        for a, ref in enumerate(arrays):
            for c in range(3):
                value = jnp.where(hit, ref[0, c, pl.ds(cell, 1), :], 0.0)
                put(3 * a + c, q, jnp.sum(value, axis=1, keepdims=True))
        seed = jnp.where(hit, seed_ref[0, pl.ds(cell, 1), :].astype(jnp.float32), 0.0)
        put(9, q, jnp.sum(seed, axis=1, keepdims=True))
        place = dest_ref[q] * bin_ref.shape[0] + cell_ref[q]
        put(10, q, place.astype(jnp.float32))
    cells = bin_ref.shape[0]
    bins = jnp.where(lane_iota(cells) < last_count, bin_ref[...], BINS)
    profile = jnp.zeros((1, LANES), jnp.float32)
    for b in range(BINS):
        hits = jnp.sum((bins == b).astype(jnp.float32), axis=0, keepdims=True)
        profile = jnp.where(lane == b, jnp.sum(hits, axis=1, keepdims=True), profile)
    out_ref[...] = jnp.zeros(out_ref.shape, jnp.float32)
    out_ref[0:1, :] = lines[0]
    out_ref[1:2, :] = lines[1]
    out_ref[2:3, :] = profile


def link_kernel(own_ref, msort_ref, psort_ref, left_ref, right_ref,
                got_ref, below_ref, above_ref, side_ref,
                tile_send, tile_recv, send_sem, recv_sem):
    flow, trans = lax.axis_index("flow"), lax.axis_index("trans")
    flows, count = lax.axis_size("flow"), got_ref.shape[0]
    flow_rows, cells = msort_ref.shape[1], msort_ref.shape[2]
    prec_cells = psort_ref.shape[2]

    def at(df, dt):
        return (lax.rem(flow + flows + df, flows), lax.rem(trans + count + dt, count))

    mesh_id = pl.DeviceIdType.MESH
    barrier = pltpu.get_barrier_semaphore()
    across = [(df, dt) for df in (-1, 1) for dt in (-1, 0, 1)]
    for df, dt in across:
        pl.semaphore_signal(barrier, inc=1, device_id=at(df, dt), device_id_type=mesh_id)

    for dt in (-1, 1):
        pl.semaphore_signal(barrier, inc=1, device_id=at(0, dt), device_id_type=mesh_id)
    inner = 8
    outer = count // inner
    high, low = trans // inner, lax.rem(trans, inner)
    meets = (flow == 0) | (flow == flows - 1)

    def near(s):
        return high * inner + lax.rem(low + inner + s, inner)

    def far(s):
        return lax.rem(high + outer + s, outer)

    @pl.when(meets)
    def _():
        for s in range(1, inner):
            pl.semaphore_signal(barrier, inc=1, device_id=(flow, near(s)), device_id_type=mesh_id)
        for s in range(1, outer):
            pl.semaphore_signal(barrier, inc=1, device_id=(flow, far(s) * inner + low),
                                device_id_type=mesh_id)

    pl.semaphore_wait(barrier, len(across) + 2 + jnp.where(meets, inner + outer - 2, 0))
    main_part, prec_part = pl.ds(0, cells), pl.ds(cells, prec_cells)
    plan = [
        (msort_ref.at[:, flow_rows - 1], below_ref.at[:, main_part], (1, 0)),
        (msort_ref.at[:, 0], above_ref.at[:, main_part], (-1, 0)),
        (psort_ref.at[:, 0], below_ref.at[:, prec_part], (1, 0)),
        (psort_ref.at[:, 0], above_ref.at[:, prec_part], (-1, 0)),
        (right_ref, side_ref.at[0], (0, 1)),
        (right_ref, side_ref.at[1], (1, 1)),
        (right_ref, side_ref.at[2], (-1, 1)),
        (left_ref, side_ref.at[3], (0, -1)),
        (left_ref, side_ref.at[4], (1, -1)),
        (left_ref, side_ref.at[5], (-1, -1)),
    ]
    copies = [
        pltpu.make_async_remote_copy(src_ref=src, dst_ref=dst, send_sem=send_sem.at[n],
                                     recv_sem=recv_sem.at[n], device_id=at(*step),
                                     device_id_type=mesh_id)
        for n, (src, dst, step) in enumerate(plan)
    ]
    def tile(s, slot):
        return pltpu.make_async_remote_copy(
            src_ref=own_ref, dst_ref=got_ref.at[slot], send_sem=tile_send.at[s],
            recv_sem=tile_recv.at[lax.rem(slot, inner)], device_id=(flow, near(s)),
            device_id_type=mesh_id)

    def block(s, part):
        rows = pl.ds(part * inner, inner)
        return pltpu.make_async_remote_copy(
            src_ref=got_ref.at[rows], dst_ref=got_ref.at[rows], send_sem=tile_send.at[inner + s],
            recv_sem=tile_recv.at[inner + part], device_id=(flow, far(s) * inner + low),
            device_id_type=mesh_id)

    @pl.when(meets)
    def _():
        for s in range(1, inner):
            tile(s, trans).start()

    for copy in copies:
        copy.start()

    @pl.when(meets)
    def _():
        got_ref[trans] = own_ref[...]
        for s in range(1, inner):
            tile(s, near(-s)).wait_recv()
        for s in range(1, outer):
            block(s, high).start()
        for s in range(1, outer):
            block(s, far(-s)).wait_recv()
        for s in range(1, inner):
            tile(s, trans).wait_send()
        for s in range(1, outer):
            block(s, high).wait_send()

    @pl.when(jnp.logical_not(meets))
    def _():
        got_ref[...] = jnp.zeros(got_ref.shape, jnp.float32)

    for copy in copies:
        copy.wait()


def sorted_keys(key):
    rows = key.shape[0]
    lane = lane_iota(rows)
    size = 2
    while size <= LANES:
        dist = size // 2
        while dist >= 1:
            low = ((lane & size) == 0) == ((lane & dist) == 0)
            other = take(key, lane ^ dist)
            key = jnp.where(low, jnp.minimum(key, other), jnp.maximum(key, other))
            dist //= 2
        size *= 2
    return key


def height_keys(height):
    level = jnp.minimum(height, 16.25) * float(1 << 19)
    return level.astype(jnp.int32) * LANES + lane_iota(height.shape[0])


def first_at_least(sorted_rows, bound, rows):
    at = jnp.zeros((rows, LANES), jnp.int32)
    step = LANES // 2
    while step >= 1:
        below = take(sorted_rows, at + (step - 1)) < bound
        at = jnp.where(below, at + step, at)
        step //= 2
    return jnp.where(take(sorted_rows, at) < bound, at + 1, at)


def sort_state(pos_ref, vel_ref, force_ref, seeds, sort_ref, rank_ref, raw_out):
    flow_rows, rows = len(seeds), seeds[0].shape[0]
    fields, keys = [], []
    for f, seed in enumerate(seeds):
        at = f * rows
        occupied = seed >= 0
        half = [vel_ref[f, c] + 0.5 * time_step * force_ref[f, c] for c in range(3)]
        moved = [pos_ref[f, c] + time_step * half[c] for c in range(3)]
        for c in range(3):
            raw_out[c, at : at + rows, :] = moved[c]
            raw_out[3 + c, at : at + rows, :] = half[c]
        raw_out[6, at : at + rows, :] = seed.astype(jnp.float32)
        height = moved[2] - box_height * jnp.floor(moved[2] * (1.0 / box_height))
        height = jnp.where(occupied, height, nowhere)
        hashed = centred(seed).astype(jnp.float32) / seed_modulus
        fields.append([jnp.where(occupied, v, 0.0) if c != 2 else height for c, v in enumerate(
            moved[0:2] + [height] + [drag * v for v in half] + [hashed])])
        keys.append(height_keys(height))
    key = jnp.concatenate(keys, axis=0)
    total = flow_rows * rows
    ordered = sorted_keys(key)
    order = ordered & (LANES - 1)
    rank_ref[...] = first_at_least(ordered, key, total)
    for c in range(7):
        field = take(jnp.concatenate([v[c] for v in fields], axis=0), order)
        if c == 2:
            starts = starts_of(field)
        for f in range(flow_rows):
            sort_ref[c, f] = field[f * rows : (f + 1) * rows]
    for f in range(flow_rows):
        sort_ref[7, f] = starts[f * rows : (f + 1) * rows]


def prec_kernel(row_ref, dest_ref, cell_ref, count_ref, bin_ref, pos_ref, vel_ref, force_ref,
                seed_ref, own_ref, sort_ref, raw_ref, rank_ref):
    last = count_ref.shape[0] - 1
    first_tile(row_ref, dest_ref, cell_ref, column_of(count_ref[last : last + 1, :]),
               (pos_ref, vel_ref, force_ref), seed_ref, bin_ref, own_ref)
    sort_state(pos_ref, vel_ref, force_ref, [seed_ref[0]], sort_ref, rank_ref, raw_ref)


def main_kernel(count_ref, pos_ref, vel_ref, force_ref, seed_ref, psort_ref,
                msort_ref, raw_ref, rank_ref, left_ref, right_ref):
    flow_rows, cells = seed_ref.shape[0], seed_ref.shape[1]
    prec_cells = psort_ref.shape[2]
    seeds = [
        jnp.where(lane_iota(cells) < column_of(count_ref[f : f + 1, :]), seed_ref[f], -1)
        for f in range(flow_rows)
    ]
    sort_state(pos_ref, vel_ref, force_ref, seeds, msort_ref, rank_ref, raw_ref)
    left_ref[...] = jnp.zeros(left_ref.shape, jnp.float32)
    right_ref[...] = jnp.zeros(right_ref.shape, jnp.float32)
    for c in range(msort_ref.shape[0]):
        for f in range(flow_rows):
            left_ref[c, f : f + 1, :] = msort_ref[c, f, 0:1, :]
            right_ref[c, f : f + 1, :] = msort_ref[c, f, cells - 1 : cells, :]
        left_ref[c, flow_rows : flow_rows + 1, :] = psort_ref[c, 0, 0:1, :]
        right_ref[c, flow_rows : flow_rows + 1, :] = psort_ref[c, 0, prec_cells - 1 : prec_cells, :]


def starts_of(height):
    edges = lane_iota(height.shape[0]).astype(jnp.float32) * (1.0 / table_rate)
    return first_at_least(height, edges, height.shape[0]).astype(jnp.float32)


def arrivals(first, got_ref, count_ref, j_ref, raw_ref, rank_ref):
    cells = count_ref.shape[1]
    per = 16
    rows = j_ref.shape[2]
    row = lax.broadcasted_iota(jnp.int32, (rows, LANES), 0)
    order_of = lax.broadcasted_iota(jnp.int32, (LANES, LANES), 0)
    upto = (order_of <= lane_iota(LANES)).astype(jnp.float32)
    held = jnp.sum((j_ref[2, 1] < 500.0).astype(jnp.float32), axis=1, keepdims=True)
    turn = lane_iota(rows).astype(jnp.float32) - held + 1.0
    before = jnp.zeros((rows, 1), jnp.float32)
    came = jnp.zeros((rows, LANES), jnp.int32)
    lane8 = lane_iota(8)
    mine = lane8 // per == lax.broadcasted_iota(jnp.int32, (8, LANES), 0)
    blocks = got_ref.shape[0] * per // LANES

    def line_of(c, a):
        line = take(got_ref[8 * a : 8 * a + 8, c // 8, :], lane8 % per + (c % 8) * per)
        return jnp.sum(jnp.where(mine, line, 0.0), axis=0, keepdims=True)

    for a in range(blocks):
        match = (line_of(10, a).astype(jnp.int32) - first == row).astype(jnp.float32)
        seen = jnp.dot(match, upto, preferred_element_type=jnp.float32) + before
        before = seen[:, LANES - 1 : LANES]
        came = came + first_at_least(seen, turn, rows)
    came = jnp.where((turn >= 1.0) & (turn <= before), came, -1)
    here = came >= 0
    block, at = came // LANES, came & (LANES - 1)
    state = []
    for c in range(10):
        value = jnp.zeros((rows, LANES), jnp.float32)
        for a in range(blocks):
            line = line_of(c, a)
            part = take(jnp.broadcast_to(line, (rows, LANES)), at)
            value = jnp.where(block == a, part, value)
        state.append(value)
    half = [state[3 + c] + 0.5 * time_step * state[6 + c] for c in range(3)]
    moved = [state[c] + time_step * half[c] for c in range(3)]
    height = moved[2] - box_height * jnp.floor(moved[2] * (1.0 / box_height))
    hashed = centred(state[9].astype(jnp.int32)).astype(jnp.float32) / seed_modulus
    inner = slice(8, 8 + cells)
    for c, value in enumerate(moved + half + [state[9]]):
        raw_ref[c, 0:cells, :] = jnp.where(here[inner], value[inner], raw_ref[c, 0:cells, :])
    fields = [moved[0], moved[1], height] + [drag * v for v in half] + [hashed]
    fields = [jnp.where(here, fields[c], j_ref[c, 1]) for c in range(7)]
    key = height_keys(fields[2])
    ordered = sorted_keys(key)
    order = ordered & (LANES - 1)
    for c in range(7):
        j_ref[c, 1] = take(fields[c], order)
    j_ref[7, 1] = starts_of(j_ref[2, 1])
    back = first_at_least(ordered, key, rows)[inner]
    lanes = lane_iota(cells)
    listed = jnp.where(lanes < column_of(count_ref[0:1, :]), rank_ref[0:cells, :], lanes)
    rank_ref[0:cells, :] = take(back, listed)


def assemble(j_ref, sort_ref, below, above, side_ref, shift, open_ends):
    fields, flow_rows, cells, _ = sort_ref.shape

    def keep(c, value, here):
        if open_ends is None or c != 2:
            return value
        return jnp.where(here, value, nowhere)

    for c in range(fields):
        for f in range(flow_rows):
            j_ref[c, 1 + f, 8 : 8 + cells, :] = sort_ref[c, f]
        ends = open_ends or (True,) * 4
        j_ref[c, 0, 8 : 8 + cells, :] = keep(c, below(c), ends[0])
        j_ref[c, 1 + flow_rows, 8 : 8 + cells, :] = keep(c, above(c), ends[1])
        for f in range(flow_rows + 2):
            inside_left, inside_right = ends[2], ends[3]
            if open_ends is not None and f == 0:
                inside_left, inside_right = ends[2] & ends[0], ends[3] & ends[0]
            if open_ends is not None and f == flow_rows + 1:
                inside_left, inside_right = ends[2] & ends[1], ends[3] & ends[1]
            part = 1 if f == 0 else 2 if f == flow_rows + 1 else 0
            row = shift + (flow_rows - 1 if f == 0 else 0 if f == flow_rows + 1 else f - 1)
            j_ref[c, f, 7:8, :] = keep(c, side_ref[part, c, row : row + 1, :], inside_left)
            j_ref[c, f, 8 + cells : 9 + cells, :] = keep(
                c, side_ref[3 + part, c, row : row + 1, :], inside_right
            )


def search(j_ref, f, cells, i_ref, base_ref, count_ref, held_ref, reach_ref, combo0):
    at = f * cells
    low = i_ref[2 * SHARE, at : at + cells, :]
    high = jnp.full((cells, LANES), -nowhere, jnp.float32)
    for v in range(SHARE):
        height = i_ref[2 * SHARE + v, at : at + cells, :]
        high = jnp.maximum(high, jnp.where(height < 500.0, height, -nowhere))
    used = low < 500.0
    low = jnp.where(used, low - reach, 0.0)
    high = jnp.where(used, high + reach, 0.0)
    below = low < 0.0
    above = high >= box_height
    low = jnp.where(below, low + box_height, low)
    high = jnp.where(above, high - box_height, high)
    low_bin = jnp.clip((low * table_rate).astype(jnp.int32), 0, LANES - 1)
    high_bin = jnp.floor(high * table_rate).astype(jnp.int32) + 1
    high_in = jnp.clip(high_bin, 0, LANES - 1)
    quarter = lane_iota(cells) // CLASSES
    most = jnp.zeros((cells, LANES), jnp.int32)
    for nb in range(9):
        df, dt = nb // 3, nb % 3
        heights = j_ref[2, f + df, 7 + dt : 7 + dt + cells, :]
        table = j_ref[7, f + df, 7 + dt : 7 + dt + cells, :]
        held = held_ref[f + df, 7 + dt : 7 + dt + cells, :]
        first = take(table, low_bin).astype(jnp.int32)
        step = (first < LANES - 1) & (take(heights, jnp.minimum(first + 1, LANES - 1)) < low)
        first = jnp.where(step, first + 2, first)
        step = (first < LANES) & (take(heights, jnp.minimum(first, LANES - 1)) < low)
        first = jnp.where(step, first + 1, first)
        last = jnp.where(high_bin >= LANES, held, take(table, high_in).astype(jnp.int32))
        step = (last >= 2) & (take(heights, jnp.maximum(last - 2, 0)) > high)
        last = jnp.where(step, last - 2, last)
        step = (last >= 1) & (take(heights, jnp.maximum(last - 1, 0)) > high)
        last = jnp.where(step, last - 1, last)
        first = jnp.where(below, first - held, first)
        last = jnp.where(above, last + held, last)
        count = jnp.where(used, last - first, 0)
        most = jnp.maximum(most, count)
        base_ref[combo0 + nb, at : at + cells, :] = first + quarter
        count_ref[combo0 + nb, at : at + cells, :] = count - quarter
    reach_ref[at : at + cells, :] = most


def pair_sums(j_ref, f, r0, i_ref, i0, base_ref, count_ref, held_ref, steps):
    beads = [[i_ref[c * SHARE + v, pl.ds(i0, 8), :] for c in range(7)] for v in range(SHARE)]

    def body(t, sums):
        sums = list(sums)
        k = t * SHARE
        for nb in range(9):
            df, dt = nb // 3, nb % 3
            rows = pl.ds(r0 + (7 + dt), 8)
            held = held_ref[f + df, rows, :]
            at = base_ref[nb, pl.ds(i0, 8), :] + k
            under, over = at < 0, at >= held
            lanes = (at + jnp.where(under, held, jnp.where(over, -held, 0))) & (LANES - 1)
            turn = jnp.where(under, -box_height, jnp.where(over, box_height, 0.0))
            turn = jnp.where(count_ref[nb, pl.ds(i0, 8), :] > k, turn, 10.0 * nowhere)
            other = [take(j_ref[c, f + df, rows, :], lanes) for c in range(7)]
            if df != 1:
                other[0] = other[0] + (df - 1.0)
            if dt != 1:
                other[1] = other[1] + (dt - 1.0)
            other[2] = other[2] + turn
            for v in range(SHARE):
                own = beads[v]
                dx, dy, dz = own[0] - other[0], own[1] - other[1], own[2] - other[2]
                dist_sq = dx * dx + dy * dy + dz * dz
                if nb == 4:
                    dist_sq = jnp.maximum(dist_sq, 1e-30)
                weight = jnp.maximum(lax.rsqrt(dist_sq) - 1.0, 0.0)
                along = ((own[3] - other[3]) * dx + (own[4] - other[4]) * dy
                         + (own[5] - other[5]) * dz)
                ratio = own[6] * other[6]
                noise = (ratio + noise_lift) - jnp.round(ratio - hash_shift)
                scalar = weight * (noise - weight * along)
                sums[v] = sums[v] + scalar * dx
                sums[SHARE + v] = sums[SHARE + v] + scalar * dy
                sums[2 * SHARE + v] = sums[2 * SHARE + v] + scalar * dz
        return tuple(sums)

    zero = jnp.zeros((8, LANES), jnp.float32)
    return lax.fori_loop(0, steps, body, (zero,) * (3 * SHARE))


def unsorted_sums(sums, rank):
    lanes = rank // SHARE
    which = rank % SHARE
    out = []
    for c in range(3):
        total = None
        for v in range(SHARE):
            part = sums[c * SHARE + v]
            part = part + pltpu.roll(part, LANES // 2, 1)
            part = part + pltpu.roll(part, LANES // 4, 1)
            part = take(part, lanes)
            total = part if total is None else jnp.where(which == v, part, total)
        out.append(noise_slope * total)
    return out


def arrange(i_ref, j_ref, f, cells, at):
    lane = lane_iota(cells) % CLASSES
    for v in range(SHARE):
        lanes = lane * SHARE + v
        for c in range(7):
            field = take(j_ref[c, 1 + f, 8 : 8 + cells, :], lanes)
            if c == 6:
                field = jnp.round(field * seed_modulus)
            i_ref[c * SHARE + v, at : at + cells, :] = field


def force_kernel(share, count_ref, coef_ref, got_ref,
                 msort_ref, psort_ref, mraw_in, praw_ref, mrank_in, prank_ref,
                 below_ref, above_ref, side_ref, bin_ref,
                 mpos_out, mvel_out, mforce_out, ppos_out, pvel_out, pforce_out,
                 mj_ref, pj_ref, mi_ref, pi_ref, mbase_ref, mcount_ref, pbase_ref, pcount_ref,
                 mheld_ref, pheld_ref, mreach_ref, preach_ref, steps_ref,
                 mraw_ref, mrank_ref, push_ref, table_ref, sem_ref):
    flow_rows, cells = msort_ref.shape[1], msort_ref.shape[2]
    prec_cells = psort_ref.shape[2]
    flow, trans = lax.axis_index("flow"), lax.axis_index("trans")
    last_flow = flow == lax.axis_size("flow") - 1
    ends = (flow > 0, jnp.logical_not(last_flow), trans > 0, trans < lax.axis_size("trans") - 1)
    assemble(mj_ref, msort_ref, lambda c: below_ref[c, 0:cells, :], lambda c: above_ref[c, 0:cells, :],
             side_ref, 0, ends)
    assemble(pj_ref, psort_ref, lambda c: below_ref[c, cells : cells + prec_cells, :],
             lambda c: above_ref[c, cells : cells + prec_cells, :], side_ref,
             flow_rows, None)
    mraw_ref[...] = mraw_in[...]
    mrank_ref[...] = mrank_in[...]

    @pl.when(flow == 0)
    def _():
        arrivals(trans * cells - 8, got_ref, count_ref, mj_ref, mraw_ref, mrank_ref)

    profile = jnp.sum(got_ref[:, 2:3, :], axis=0)[:, 0:BINS]
    push_ref[...] = jnp.zeros(push_ref.shape, jnp.float32)
    push_ref[:, 0:BINS] = jnp.broadcast_to(-coef_ref[...] * (profile * jnp.where(last_flow, share, 0.0)), (8, BINS))
    push_row = push_ref[...]
    for j_ref, held_ref, n in ((mj_ref, mheld_ref, cells), (pj_ref, pheld_ref, prec_cells)):
        for f in range(held_ref.shape[0]):
            real = (j_ref[2, f, 0 : n + 16, :] < 500.0).astype(jnp.float32)
            held = jnp.sum(real, axis=1, keepdims=True).astype(jnp.int32)
            held_ref[f] = jnp.broadcast_to(held, (n + 16, LANES))
    for f in range(flow_rows):
        arrange(mi_ref, mj_ref, f, cells, f * cells)
    arrange(pi_ref, pj_ref, 0, prec_cells, 0)
    for f in range(flow_rows):
        search(mj_ref, f, cells, mi_ref, mbase_ref, mcount_ref, mheld_ref, mreach_ref, 0)
    search(pj_ref, 0, prec_cells, pi_ref, pbase_ref, pcount_ref, pheld_ref, preach_ref, 0)
    groups = flow_rows * cells // 8
    prec_groups = prec_cells // 8
    for ref, start, n in ((mreach_ref, 0, groups), (preach_ref, groups, prec_groups)):
        most = jnp.max(ref[...].reshape(n, 8, LANES), axis=1)
        most = (jnp.max(most, axis=1, keepdims=True) + (SHARE - 1)) // SHARE
        table_ref[start : start + n, :] = jnp.broadcast_to(most, (n, LANES))
    to_scalars = pltpu.make_async_copy(table_ref, steps_ref, sem_ref.at[0])
    to_scalars.start()
    to_scalars.wait()

    def main_group(g, carry):
        f = g // (cells // 8)
        r0 = pl.multiple_of((g % (cells // 8)) * 8, 8)
        i0 = pl.multiple_of(g * 8, 8)
        sums = pair_sums(mj_ref, f, r0, mi_ref, i0, mbase_ref, mcount_ref, mheld_ref, steps_ref[g, 0])
        force = unsorted_sums(sums, mrank_ref[pl.ds(i0, 8), :])
        occupied = mraw_ref[6, pl.ds(i0, 8), :] >= 0.0
        push = take(push_row, bin_ref[pl.ds(r0, 8), :])
        force[0] = force[0] + push * (f == flow_rows - 1).astype(jnp.float32)
        for c in range(3):
            half = mraw_ref[3 + c, pl.ds(i0, 8), :]
            mforce_out[f, c, pl.ds(r0, 8), :] = jnp.where(occupied, force[c], 0.0)
            mvel_out[f, c, pl.ds(r0, 8), :] = jnp.where(
                occupied, half + 0.5 * time_step * force[c], 0.0
            )
            mpos_out[f, c, pl.ds(r0, 8), :] = jnp.where(
                occupied, mraw_ref[c, pl.ds(i0, 8), :], 0.0
            )
        return carry

    def prec_group(g, carry):
        r0 = pl.multiple_of(g * 8, 8)
        sums = pair_sums(pj_ref, 0, r0, pi_ref, r0, pbase_ref, pcount_ref, pheld_ref,
                         steps_ref[groups + g, 0])
        force = unsorted_sums(sums, prank_ref[pl.ds(r0, 8), :])
        for c in range(3):
            half = praw_ref[3 + c, pl.ds(r0, 8), :]
            pforce_out[0, c, pl.ds(r0, 8), :] = force[c]
            pvel_out[0, c, pl.ds(r0, 8), :] = half + 0.5 * time_step * force[c]
            ppos_out[0, c, pl.ds(r0, 8), :] = praw_ref[c, pl.ds(r0, 8), :]
        return carry

    lax.fori_loop(0, prec_groups, prec_group, 0)
    lax.fori_loop(0, groups, main_group, 0)


def whole(space, n):
    return [pl.BlockSpec(memory_space=space)] * n


def shape(dims, dtype=jnp.float32):
    return jax.ShapeDtypeStruct(dims, dtype)


def scratches(flow_rows, cells, prec_cells):
    total = flow_rows * cells
    return [
        VMEM((8, flow_rows + 2, cells + 16, LANES), jnp.float32),
        VMEM((8, 3, prec_cells + 16, LANES), jnp.float32),
        VMEM((7 * SHARE, total, LANES), jnp.float32),
        VMEM((7 * SHARE, prec_cells, LANES), jnp.float32),
        VMEM((9, total, LANES), jnp.int32),
        VMEM((9, total, LANES), jnp.int32),
        VMEM((9, prec_cells, LANES), jnp.int32),
        VMEM((9, prec_cells, LANES), jnp.int32),
        VMEM((flow_rows + 2, cells + 16, LANES), jnp.int32),
        VMEM((3, prec_cells + 16, LANES), jnp.int32),
        VMEM((total, LANES), jnp.int32),
        VMEM((prec_cells, LANES), jnp.int32),
        SMEM((total // 8 + prec_cells // 8, LANES), jnp.int32),
        VMEM((7, total, LANES), jnp.float32),
        VMEM((total, LANES), jnp.int32),
        VMEM((8, LANES), jnp.float32),
        VMEM((total // 8 + prec_cells // 8, LANES), jnp.int32),
        pltpu.SemaphoreType.DMA((1,)),
    ]


def shards(
    main_pos,
    main_vel,
    main_force,
    main_seed,
    main_count,
    prec_pos,
    prec_vel,
    prec_force,
    prec_seed,
    cross_row,
    cross_dest,
    cross_cell,
    outlet_bin,
    outlet_coef,
):
    flow_rows, cells = main_seed.shape[0], main_seed.shape[1]
    prec_cells = prec_seed.shape[1]
    trans_devices = lax.axis_size("trans")
    total = flow_rows * cells
    big = pltpu.CompilerParams(vmem_limit_bytes=63 << 20)

    def planes(value):
        return jnp.transpose(value, (0, 2, 1, 3))

    main_state = [planes(v) for v in (main_pos, main_vel, main_force)]
    prec_state = [planes(v) for v in (prec_pos, prec_vel, prec_force)]

    share = BINS / (cells * trans_devices * LANES)

    own, psort, praw, prank = pl.pallas_call(
        prec_kernel,
        out_shape=(
            shape((8, LANES)),
            shape((8, 1, prec_cells, LANES)),
            shape((7, prec_cells, LANES)),
            shape((prec_cells, LANES), jnp.int32),
        ),
        in_specs=whole(SMEM, 3) + whole(VMEM, 6),
        out_specs=tuple(whole(VMEM, 4)),
        compiler_params=big,
        name="prec",
    )(cross_row, cross_dest, cross_cell, main_count, outlet_bin, *prec_state, prec_seed)
    msort, mraw, mrank, left, right = pl.pallas_call(
        main_kernel,
        out_shape=(
            shape((8, flow_rows, cells, LANES)),
            shape((7, total, LANES)),
            shape((total, LANES), jnp.int32),
            shape((8, 8, LANES)),
            shape((8, 8, LANES)),
        ),
        in_specs=whole(VMEM, 6),
        out_specs=tuple(whole(VMEM, 5)),
        compiler_params=big,
        name="main",
    )(main_count, *main_state, main_seed, psort)

    span = cells + prec_cells
    got, below, above, side = pl.pallas_call(
        link_kernel,
        out_shape=(shape((trans_devices, 8, LANES)), shape((8, span, LANES)),
                   shape((8, span, LANES)), shape((6, 8, 8, LANES))),
        in_specs=whole(VMEM, 1) + whole(pl.ANY, 4),
        out_specs=tuple(whole(VMEM, 1) + whole(pl.ANY, 3)),
        scratch_shapes=[pltpu.SemaphoreType.DMA((8 + trans_devices // 8,))] * 2
        + [pltpu.SemaphoreType.DMA((10,))] * 2,
        compiler_params=pltpu.CompilerParams(vmem_limit_bytes=63 << 20, collective_id=0,
                                             has_side_effects=True),
        name="link",
    )(own, msort, psort, left, right)
    out_main = shape((flow_rows, 3, cells, LANES))
    out_prec = shape((1, 3, prec_cells, LANES))
    outs = pl.pallas_call(
        functools.partial(force_kernel, share),
        out_shape=(out_main, out_main, out_main, out_prec, out_prec, out_prec),
        in_specs=whole(VMEM, 13),
        out_specs=tuple(whole(VMEM, 6)),
        scratch_shapes=scratches(flow_rows, cells, prec_cells),
        compiler_params=big,
        name="force",
    )(main_count, outlet_coef[None], got,
      msort, psort, mraw, praw, mrank, prank, below, above, side, outlet_bin)
    return tuple(planes(v) for v in outs)


def solution(mesh):
    return jax.shard_map(
        shards,
        mesh=mesh,
        in_specs=(
            P("flow", "trans", None, None),
            P("flow", "trans", None, None),
            P("flow", "trans", None, None),
            P("flow", "trans", None),
            P("flow", "trans"),
            P("flow", "trans", None, None),
            P("flow", "trans", None, None),
            P("flow", "trans", None, None),
            P("flow", "trans", None),
            P("trans"),
            P("trans"),
            P("trans"),
            P("trans", None),
            P(),
        ),
        out_specs=(
            P("flow", "trans", None, None),
            P("flow", "trans", None, None),
            P("flow", "trans", None, None),
            P("flow", "trans", None, None),
            P("flow", "trans", None, None),
            P("flow", "trans", None, None),
        ),
        check_vma=False,
    )
```
